32 devices in a mesh: shard: 4 (over y, x), ctx: 4 (over z), tp: 2 (over core).
Axes of the slice: x: 2, y: 2, z: 4, core: 2. Of those that a mesh axis runs over, the one named last changes fastest.
Arguments:
- block_entries: bfloat16 [2, 4, 1024, 1024], P(None, 'shard', 'ctx', 'tp'), may hold values from -6 to 6
- row_extents: int32 [2, 4], P(None, 'shard'), may hold values from 256 to 1024, as said below
- upstream_loss_deriv: bfloat16 [2, 4, 1024, 1024], P(None, 'shard', 'ctx', 'tp'), may hold values from -6 to 6
- earlier_layernorm_scaling: float32 [1024], P('tp'), may hold values from 0.25 to 1.75
- earlier_layernorm_offset: float32 [1024], P('tp'), may hold values from -1.2 to 1.2
- temporal_mix_lookup_fraction: float32 [1024], P('tp'), may hold values from 0.05 to 0.95
- temporal_mix_payload_fraction: float32 [1024], P('tp'), may hold values from 0.05 to 0.95
- temporal_mix_filter_fraction: float32 [1024], P('tp'), may hold values from 0.05 to 0.95
- logarithmic_fading_per_feature: float32 [1024], P('tp'), may hold values from -11 to -2.5
- present_entry_reward: float32 [1024], P('tp'), may hold values from -1 to 1
- filter_projection: bfloat16 [1024, 1024], P('shard', 'tp'), may hold values from -0.1875 to 0.1875
- lookup_projection: bfloat16 [1024, 1024], P('shard', 'tp'), may hold values from -0.1875 to 0.1875
- payload_projection: bfloat16 [1024, 1024], P('shard', 'tp'), may hold values from -0.1875 to 0.1875
- temporal_mix_emit_projection: bfloat16 [1024, 1024], P('tp', 'shard'), may hold values from -0.75 to 0.75
- later_layernorm_scaling: float32 [1024], P('tp'), may hold values from 0.25 to 1.75
- later_layernorm_offset: float32 [1024], P('tp'), may hold values from -1.2 to 1.2
- feature_mix_lookup_fraction: float32 [1024], P('tp'), may hold values from 0.05 to 0.95
- feature_mix_filter_fraction: float32 [1024], P('tp'), may hold values from 0.05 to 0.95
- feature_mix_lookup_proj: bfloat16 [1024, 4096], P('shard', 'tp'), may hold values from -0.1875 to 0.1875
- feature_mix_filter_proj: bfloat16 [1024, 1024], P('shard', 'tp'), may hold values from -0.1875 to 0.1875
- feature_mix_payload_proj: bfloat16 [4096, 1024], P('tp', 'shard'), may hold values from -0.09375 to 0.09375
Outputs:
- block_out: bfloat16 [2, 4, 1024, 1024], P(None, 'shard', 'ctx', 'tp')
- input_grad: float32 [2, 4, 1024, 1024], P(None, 'shard', 'ctx', 'tp')
- first_gain_grad: float32 [1024], P('tp')
- first_bias_grad: float32 [1024], P('tp')
- shift_key_grad: float32 [1024], P('tp')
- shift_value_grad: float32 [1024], P('tp')
- shift_gate_grad: float32 [1024], P('tp')
- decay_log_grad: float32 [1024], P('tp')
- time_bonus_grad: float32 [1024], P('tp')
- gate_weight_grad: float32 [1024, 1024], P(('shard', 'ctx'), 'tp')
- key_weight_grad: float32 [1024, 1024], P(('shard', 'ctx'), 'tp')
- value_weight_grad: float32 [1024, 1024], P(('shard', 'ctx'), 'tp')
- output_weight_grad: float32 [1024, 1024], P('tp', ('shard', 'ctx'))
- second_gain_grad: float32 [1024], P('tp')
- second_bias_grad: float32 [1024], P('tp')
- channel_shift_key_grad: float32 [1024], P('tp')
- channel_shift_gate_grad: float32 [1024], P('tp')
- hidden_weight_grad: float32 [1024, 4096], P(('shard', 'ctx'), 'tp')
- filter_weight_grad: float32 [1024, 1024], P(('shard', 'ctx'), 'tp')
- return_weight_grad: float32 [4096, 1024], P('tp', ('shard', 'ctx'))
The draws below stay inside these ranges and needn't reach their ends.
Inputs may be any that keep to these rules, and one draw needn't show every extreme that they name: `row_extents`: each row's valid tokens come first; in every draw some row has exactly 1024 valid tokens and some row exactly 256.
All inputs are finite; a program needn't handle non-finite values.
Results may differ from the reference program's by a relative error of at most 0.011.
Values may be sent and summed in bfloat16 or wider, within the bound.
No kernel may reach another device: no remote copies, remote signals or barrier semaphores. Data moves between devices by JAX's collectives and lax.ppermute only.
A program may use at most 192 MiB of HBM per device.

```python
import jax
import jax.numpy as jnp
from jax import lax

EMBED_SIZE = 1024
FF = 4096
MB = 2
ROWS_MB = 1
ROWS = 4
LEN = 1024
N_SHARD = 4


def draw_row_extents(key, part):
    count_rows = MB * ROWS
    lengths_drawn = jax.random.randint(jax.random.fold_in(key, 11), (count_rows,), LEN // 4, LEN + 1, dtype=jnp.int32)
    chosen = jax.random.randint(jax.random.fold_in(key, 12), (), 0, count_rows, dtype=jnp.int32)
    lengths_drawn = lengths_drawn.at[chosen].set(LEN)
    lengths_drawn = lengths_drawn.at[(chosen + 1) % count_rows].set(LEN // 4)
    return lengths_drawn.reshape(MB, ROWS)


def level_of(rng, extent, split, smallest, top_value):
    def one(position, shards_of):
        heights = jax.random.uniform(jax.random.fold_in(jax.random.fold_in(rng, 6), position), (shards_of,), jnp.float32, smallest / len(split), top_value / len(split))
        return jnp.repeat(jnp.exp(heights), extent[position] // shards_of).reshape((-1,) + (1,) * (len(extent) - position - 1))

    gain = one(*split[0])
    for cut in split[1:]:
        gain = gain * one(*cut)
    return gain


def noise(stream_key, dims, width, limit, pieces=(), kind=jnp.bfloat16):
    entries = width * jax.random.normal(stream_key, dims, jnp.float32)
    if pieces:
        entries = entries * level_of(stream_key, dims, pieces, -0.22, 0.18)
    return jnp.clip(entries, -limit, limit).astype(kind)


def setup_inputs(seed: int = 0) -> dict:
    arg_keys = jax.random.split(jax.random.key(seed), 22)
    block_entries = noise(arg_keys[0], (MB, ROWS, LEN, EMBED_SIZE), 1.0, 6.0, ((1, 4), (2, 4), (3, 2)))
    row_extents = draw_row_extents(jax.random.fold_in(arg_keys[21], 71), 0)
    upstream_loss_deriv = noise(arg_keys[2], (MB, ROWS, LEN, EMBED_SIZE), 1.0, 6.0, ((1, 4), (2, 4), (3, 2)))
    earlier_layernorm_scaling = jnp.clip(1.0 + 0.15 * jax.random.normal(arg_keys[3], (EMBED_SIZE,), jnp.float32), 0.25, 1.75)
    earlier_layernorm_offset = noise(arg_keys[4], (EMBED_SIZE,), 0.3, 1.2, ((0, 2),), jnp.float32)
    temporal_mix_lookup_fraction = jnp.clip(0.05 + 0.9 * jax.random.uniform(arg_keys[5], (EMBED_SIZE,), jnp.float32) ** level_of(arg_keys[5], (EMBED_SIZE,), ((0, 2),), -0.2, 0.2), 0.05, 0.95)
    temporal_mix_payload_fraction = jnp.clip(0.05 + 0.9 * jax.random.uniform(arg_keys[6], (EMBED_SIZE,), jnp.float32) ** level_of(arg_keys[6], (EMBED_SIZE,), ((0, 2),), -0.2, 0.2), 0.05, 0.95)
    temporal_mix_filter_fraction = jnp.clip(0.05 + 0.9 * jax.random.uniform(arg_keys[7], (EMBED_SIZE,), jnp.float32) ** level_of(arg_keys[7], (EMBED_SIZE,), ((0, 2),), -0.2, 0.2), 0.05, 0.95)
    logarithmic_fading_per_feature = jnp.clip(-11.0 + 8.5 * jax.random.uniform(arg_keys[8], (EMBED_SIZE,), jnp.float32) ** level_of(arg_keys[8], (EMBED_SIZE,), ((0, 2),), -0.2, 0.2), -11.0, -2.5)
    present_entry_reward = jnp.clip(jax.random.uniform(arg_keys[9], (EMBED_SIZE,), jnp.float32, -1.0, 1.0) * level_of(arg_keys[9], (EMBED_SIZE,), ((0, 2),), -0.4, 0.0), -1.0, 1.0)
    filter_projection = noise(arg_keys[10], (EMBED_SIZE, EMBED_SIZE), EMBED_SIZE ** -0.5, 0.1875, ((0, 4), (1, 2)))
    lookup_projection = noise(arg_keys[11], (EMBED_SIZE, EMBED_SIZE), EMBED_SIZE ** -0.5, 0.1875, ((0, 4), (1, 2)))
    payload_projection = noise(arg_keys[12], (EMBED_SIZE, EMBED_SIZE), EMBED_SIZE ** -0.5, 0.1875, ((0, 4), (1, 2)))
    temporal_mix_emit_projection = noise(arg_keys[13], (EMBED_SIZE, EMBED_SIZE), (EMBED_SIZE // 16) ** -0.5, 0.75, ((0, 2), (1, 4)))
    later_layernorm_scaling = jnp.clip(1.0 + 0.15 * jax.random.normal(arg_keys[14], (EMBED_SIZE,), jnp.float32), 0.25, 1.75)
    later_layernorm_offset = noise(arg_keys[15], (EMBED_SIZE,), 0.3, 1.2, ((0, 2),), jnp.float32)
    feature_mix_lookup_fraction = jnp.clip(0.05 + 0.9 * jax.random.uniform(arg_keys[16], (EMBED_SIZE,), jnp.float32) ** level_of(arg_keys[16], (EMBED_SIZE,), ((0, 2),), -0.2, 0.2), 0.05, 0.95)
    feature_mix_filter_fraction = jnp.clip(0.05 + 0.9 * jax.random.uniform(arg_keys[17], (EMBED_SIZE,), jnp.float32) ** level_of(arg_keys[17], (EMBED_SIZE,), ((0, 2),), -0.2, 0.2), 0.05, 0.95)
    feature_mix_lookup_proj = noise(arg_keys[18], (EMBED_SIZE, FF), EMBED_SIZE ** -0.5, 0.1875, ((0, 4), (1, 2)))
    feature_mix_filter_proj = noise(arg_keys[19], (EMBED_SIZE, EMBED_SIZE), EMBED_SIZE ** -0.5, 0.1875, ((0, 4), (1, 2)))
    feature_mix_payload_proj = noise(arg_keys[20], (FF, EMBED_SIZE), FF ** -0.5, 0.09375, ((0, 2), (1, 4)))
    return dict(block_entries=block_entries, row_extents=row_extents, upstream_loss_deriv=upstream_loss_deriv, earlier_layernorm_scaling=earlier_layernorm_scaling, earlier_layernorm_offset=earlier_layernorm_offset, temporal_mix_lookup_fraction=temporal_mix_lookup_fraction, temporal_mix_payload_fraction=temporal_mix_payload_fraction, temporal_mix_filter_fraction=temporal_mix_filter_fraction, logarithmic_fading_per_feature=logarithmic_fading_per_feature, present_entry_reward=present_entry_reward, filter_projection=filter_projection, lookup_projection=lookup_projection, payload_projection=payload_projection, temporal_mix_emit_projection=temporal_mix_emit_projection, later_layernorm_scaling=later_layernorm_scaling, later_layernorm_offset=later_layernorm_offset, feature_mix_lookup_fraction=feature_mix_lookup_fraction, feature_mix_filter_fraction=feature_mix_filter_fraction, feature_mix_lookup_proj=feature_mix_lookup_proj, feature_mix_filter_proj=feature_mix_filter_proj, feature_mix_payload_proj=feature_mix_payload_proj)


epsilon = 1e-05
lowest = -1e+30
highest_precision = lax.Precision.HIGHEST

@jax.custom_vjp
def low(v):
    return lax.optimization_barrier(v.astype(jnp.bfloat16)).astype(jnp.float32)

@jax.custom_vjp
def low_back(v):
    return v

def low_keep(v):
    return (low(v), None)

def low_pass(kept, grad):
    return (grad,)

def back_keep(v):
    return (v, None)

def back_low(kept, grad):
    return (low(grad),)
low.defvjp(low_keep, low_pass)
low_back.defvjp(back_keep, back_low)

def layer_norm(values, norm_gain, norm_bias):
    center = lax.optimization_barrier(jnp.mean(values, axis=-1, keepdims=True))
    spread = lax.optimization_barrier(jnp.mean(values * values, axis=-1, keepdims=True)) - center * center
    return (values - center) * lax.rsqrt(spread + epsilon) * norm_gain + norm_bias

def token_shift(normed):
    return jnp.pad(normed[:, :-1, :], ((0, 0), (1, 0), (0, 0)))

def project(lhs_values, matrix):
    return jnp.einsum('btd,de->bte', lhs_values, matrix, precision=highest_precision)

def cumulative_lookup_payload_sweep(lookup_mapped, payload_mapped, feature_fading_factor, present_entry_reward):

    def advance(running, current):
        running_num, running_den, cumulative_largest = running
        present_lookup, value_now = current
        with_present_reward = present_entry_reward + present_lookup
        largest_power_level = jnp.maximum(cumulative_largest, with_present_reward)
        old_part = jnp.exp(cumulative_largest - largest_power_level)
        newly_added_part = jnp.exp(with_present_reward - largest_power_level)
        final_output = (old_part * running_num + newly_added_part * value_now) / (old_part * running_den + newly_added_part)
        decayed = cumulative_largest - feature_fading_factor
        newest = jnp.maximum(decayed, present_lookup)
        old_next = jnp.exp(decayed - newest)
        new_next = jnp.exp(present_lookup - newest)
        return ((old_next * running_num + new_next * value_now, old_next * running_den + new_next, newest), final_output)
    lookup_series = jnp.transpose(lookup_mapped, (1, 0, 2))
    payload_series = jnp.transpose(payload_mapped, (1, 0, 2))
    empty_state = jnp.zeros(lookup_series.shape[1:], jnp.float32)
    initial = (empty_state, empty_state, jnp.full(lookup_series.shape[1:], lowest, jnp.float32))
    closing, results = lax.scan(advance, initial, (lookup_series, payload_series))
    return jnp.transpose(results, (1, 0, 2))

def block_forward(values, live_mask, learnable_bundle):
    earlier_layernorm_scaling, earlier_layernorm_offset, temporal_mix_lookup_fraction, temporal_mix_payload_fraction, temporal_mix_filter_fraction, logarithmic_fading_per_feature, present_entry_reward, filter_projection, lookup_projection, payload_projection, temporal_mix_emit_projection, later_layernorm_scaling, later_layernorm_offset, feature_mix_lookup_fraction, feature_mix_filter_fraction, feature_mix_lookup_proj, feature_mix_filter_proj, feature_mix_payload_proj = learnable_bundle
    normed_one = layer_norm(values, earlier_layernorm_scaling, earlier_layernorm_offset)
    prev_one = token_shift(normed_one)
    mixed_key = low(normed_one * temporal_mix_lookup_fraction + prev_one * (1.0 - temporal_mix_lookup_fraction))
    mixed_value = low(normed_one * temporal_mix_payload_fraction + prev_one * (1.0 - temporal_mix_payload_fraction))
    mixed_gate = low(normed_one * temporal_mix_filter_fraction + prev_one * (1.0 - temporal_mix_filter_fraction))
    lookup_mapped = low_back(project(mixed_key, lookup_projection))
    payload_mapped = low_back(project(mixed_value, payload_projection))
    gate_logit = low_back(project(mixed_gate, filter_projection))
    proportional_blend = cumulative_lookup_payload_sweep(lookup_mapped, payload_mapped, jnp.exp(logarithmic_fading_per_feature), present_entry_reward)
    gated = low(jax.nn.sigmoid(gate_logit) * proportional_blend)
    middle = values + low_back(project(gated, temporal_mix_emit_projection))
    normed_two = layer_norm(middle, later_layernorm_scaling, later_layernorm_offset)
    prev_two = token_shift(normed_two)
    channel_key = low(normed_two * feature_mix_lookup_fraction + prev_two * (1.0 - feature_mix_lookup_fraction))
    channel_gate = low(normed_two * feature_mix_filter_fraction + prev_two * (1.0 - feature_mix_filter_fraction))
    hidden_pre = low_back(project(channel_key, feature_mix_lookup_proj))
    squared = low(jnp.square(jax.nn.relu(hidden_pre)))
    returned = low_back(project(squared, feature_mix_payload_proj))
    filter_logit = low_back(project(channel_gate, feature_mix_filter_proj))
    return live_mask * (middle + jax.nn.sigmoid(filter_logit) * returned)

def reference(block_entries, row_extents, upstream_loss_deriv, earlier_layernorm_scaling, earlier_layernorm_offset, temporal_mix_lookup_fraction, temporal_mix_payload_fraction, temporal_mix_filter_fraction, logarithmic_fading_per_feature, present_entry_reward, filter_projection, lookup_projection, payload_projection, temporal_mix_emit_projection, later_layernorm_scaling, later_layernorm_offset, feature_mix_lookup_fraction, feature_mix_filter_fraction, feature_mix_lookup_proj, feature_mix_filter_proj, feature_mix_payload_proj):
    learnable_nested = tuple((supplied_operand.astype(jnp.float32) for supplied_operand in (earlier_layernorm_scaling, earlier_layernorm_offset, temporal_mix_lookup_fraction, temporal_mix_payload_fraction, temporal_mix_filter_fraction, logarithmic_fading_per_feature, present_entry_reward, filter_projection, lookup_projection, payload_projection, temporal_mix_emit_projection, later_layernorm_scaling, later_layernorm_offset, feature_mix_lookup_fraction, feature_mix_filter_fraction, feature_mix_lookup_proj, feature_mix_filter_proj, feature_mix_payload_proj)))
    groups = MB * N_SHARD
    shaped_inputs = block_entries.astype(jnp.float32).reshape(groups, ROWS_MB, LEN, EMBED_SIZE)
    shaped_grads = upstream_loss_deriv.astype(jnp.float32).reshape(groups, ROWS_MB, LEN, EMBED_SIZE)
    shaped_lengths = row_extents.reshape(groups, ROWS_MB)
    positions = jnp.arange(LEN, dtype=jnp.int32)

    def group_step(totals, packed):
        group_inputs, group_cot, group_len = packed
        live_mask = (positions[None, :] < group_len[:, None]).astype(jnp.float32)[:, :, None]

        def forward(values, *learnable_bundle):
            return block_forward(values, live_mask, learnable_bundle)
        output, pullback = jax.vjp(forward, group_inputs, *learnable_nested)
        gradients = pullback(group_cot)
        totals = tuple((total + gradient for total, gradient in zip(totals, gradients[1:])))
        return (totals, (output.astype(jnp.bfloat16), gradients[0]))
    zero_totals = tuple((jnp.zeros_like(supplied_operand) for supplied_operand in learnable_nested))
    totals, outs = lax.scan(group_step, zero_totals, (shaped_inputs, shaped_grads, shaped_lengths))
    block_out = outs[0].reshape(MB, ROWS, LEN, EMBED_SIZE)
    input_grad = outs[1].reshape(MB, ROWS, LEN, EMBED_SIZE)
    return (block_out, input_grad, totals[0], totals[1], totals[2], totals[3], totals[4], totals[5], totals[6], totals[7], totals[8], totals[9], totals[10], totals[11], totals[12], totals[13], totals[14], totals[15], totals[16], totals[17])
```

```python
import jax
import jax.numpy as jnp
from jax import lax
from jax.experimental import pallas as pl
from jax.experimental.pallas import tpu as pltpu
from jax.sharding import PartitionSpec as P

F32, BF16 = jnp.float32, jnp.bfloat16
WIDTH = 1024
epsilon = 1e-05
lowest = -1e30
CHUNKS = 8

VMEM = pl.BlockSpec(memory_space=pltpu.VMEM)
SMEM = pl.BlockSpec(memory_space=pltpu.SMEM)
HBM = pl.BlockSpec(memory_space=pl.ANY)
KINDS = {"v": VMEM, "s": SMEM, "h": HBM}


def launch(body, kinds, inputs, outs, scratch=()):
    return pl.pallas_call(
        body,
        out_shape=[jax.ShapeDtypeStruct(shape, dtype) for shape, dtype in outs],
        in_specs=[KINDS[kind] for kind in kinds],
        out_specs=[VMEM] * len(outs),
        scratch_shapes=list(scratch),
        name=body.__name__,
    )(*inputs)


def bits_of(count):
    return count.bit_length() - 1


def swap(value, axis, step):
    size = lax.axis_size(axis)
    return lax.ppermute(value, axis, [(i, i ^ step) for i in range(size)])


def along_ctx(value, step, cross):
    count = lax.axis_size("ctx")
    if not cross:
        pairs = [(i, i + step) for i in range(count) if 0 <= i + step < count]
        return lax.ppermute(value, "ctx", pairs)
    pairs = []
    for i in range(count):
        if 0 <= i + step < count:
            for core in range(2):
                pairs.append((2 * i + core, 2 * (i + step) + 1 - core))
    return lax.ppermute(value, ("ctx", "tp"), pairs)


def gather_pieces(matrix, cut):
    half = matrix.shape[cut] // 2
    across_x = swap(matrix, "shard", 1)
    across_y = swap(matrix, "shard", 2)
    first = swap(lax.slice_in_dim(across_x, 0, half, axis=cut), "shard", 2)
    second = swap(lax.slice_in_dim(across_y, half, 2 * half, axis=cut), "shard", 1)
    return [matrix, across_x, across_y, first, second]


def place_rows(idx, pieces, whole, sems):
    base = idx[0]
    rows, cols = pieces[0].shape
    half = cols // 2

    def spot(step):
        return pl.ds(pl.multiple_of((base ^ step) * rows, rows), rows)

    targets = [
        whole.at[spot(0), :],
        whole.at[spot(1), :],
        whole.at[spot(2), :],
        whole.at[spot(3), pl.ds(0, half)],
        whole.at[spot(3), pl.ds(half, half)],
    ]
    return [
        pltpu.make_async_copy(piece, target, sems.at[i])
        for i, (piece, target) in enumerate(zip(pieces, targets))
    ]


def place_blocks(idx, pieces, whole, sems):
    base = idx[0]
    half = pieces[0].shape[0] // 2
    targets = [
        whole.at[base],
        whole.at[base ^ 1],
        whole.at[base ^ 2],
        whole.at[base ^ 3, pl.ds(0, half), :],
        whole.at[base ^ 3, pl.ds(half, half), :],
    ]
    return [
        pltpu.make_async_copy(piece, target, sems.at[i])
        for i, (piece, target) in enumerate(zip(pieces, targets))
    ]


def begin(copies):
    for copy in copies:
        copy.start()


def finish(copies):
    for copy in copies:
        copy.wait()


def dot(left, right):
    return jnp.dot(left, right, preferred_element_type=F32)


def dot_t(left, right):
    return lax.dot_general(left, right, (((1,), (1,)), ((), ())), preferred_element_type=F32)


def norm(values):
    center = jnp.sum(values, axis=-1, keepdims=True) * (1.0 / WIDTH)
    squares = jnp.sum(values * values, axis=-1, keepdims=True) * (1.0 / WIDTH)
    root = lax.rsqrt(squares - center * center + epsilon)
    return (values - center) * root, root


def both(own, other, i):
    return jnp.concatenate([own[i : i + 1, :], other[i : i + 1, :]], axis=1)


def shift_down(values, first):
    row = lax.broadcasted_iota(jnp.int32, values.shape, 0)
    return jnp.where(row == 0, first, pltpu.roll(values, 1, 0))


def shift_up(values, last):
    count = values.shape[0]
    row = lax.broadcasted_iota(jnp.int32, values.shape, 0)
    return jnp.where(row == count - 1, last, pltpu.roll(values, count - 1, 0))


def combine(earlier, later, later_span):
    shifted = earlier[2] - later_span
    high = jnp.maximum(shifted, later[2])
    early = jnp.exp(shifted - high)
    late = jnp.exp(later[2] - high)
    return (earlier[0] * early + later[0] * late, earlier[1] * early + later[1] * late, high)


def get(ref, rows):
    return jnp.concatenate([ref[g, rows, :] for g in range(ref.shape[0])], axis=1)


def put(ref, rows, values):
    for g in range(ref.shape[0]):
        ref[g, rows, :] = values[:, g * 128 : (g + 1) * 128]


def swapped(values):
    half = values.shape[1] // 2
    return jnp.concatenate([values[:, half:], values[:, :half]], axis=1)


def per_device(
    block_entries,
    row_extents,
    upstream_loss_deriv,
    earlier_layernorm_scaling,
    earlier_layernorm_offset,
    temporal_mix_lookup_fraction,
    temporal_mix_payload_fraction,
    temporal_mix_filter_fraction,
    logarithmic_fading_per_feature,
    present_entry_reward,
    filter_projection,
    lookup_projection,
    payload_projection,
    temporal_mix_emit_projection,
    later_layernorm_scaling,
    later_layernorm_offset,
    feature_mix_lookup_fraction,
    feature_mix_filter_fraction,
    feature_mix_lookup_proj,
    feature_mix_filter_proj,
    feature_mix_payload_proj,
):
    batches, rows_local, L, H = block_entries.shape
    R = batches * rows_local
    T = R * L
    S, C = lax.axis_size("shard"), lax.axis_size("ctx")
    FH = feature_mix_lookup_proj.shape[1]
    ST = L // CHUNKS
    TB = min(32, L)
    NT = L // TB
    G = H // 128
    EVERY = slice(None)
    BLOCKS = S * C
    BR = WIDTH // BLOCKS
    SR = WIDTH // S
    assert S == 4 and WIDTH == 2 * H
    s_at, c_at, t_at = lax.axis_index("shard"), lax.axis_index("ctx"), lax.axis_index("tp")
    idx = jnp.concatenate(
        [
            jnp.stack(
                [s_at ^ (2 * t_at), c_at, (s_at * C + c_at) ^ (t_at * (BLOCKS // 2))]
            ).astype(jnp.int32),
            row_extents.reshape(R).astype(jnp.int32),
        ]
    )

    def rows_at(r, i):
        return pl.ds(pl.multiple_of(r * L + i * TB, TB), TB)

    def scan_rows(r, t):
        return pl.ds(pl.multiple_of((r * ST + t) * CHUNKS, CHUNKS), CHUNKS)

    def step_rows(r, t):
        return pl.ds(r * L + t, CHUNKS, stride=ST)

    def chunk_rows(part, i):
        return pl.ds(part * R * CHUNKS + i, R, stride=CHUNKS)

    x_own = block_entries.reshape(T, H)
    up_own = upstream_loss_deriv.reshape(T, H)
    params = jnp.stack(
        [
            earlier_layernorm_scaling,
            earlier_layernorm_offset,
            temporal_mix_lookup_fraction,
            temporal_mix_payload_fraction,
            temporal_mix_filter_fraction,
            later_layernorm_scaling,
            later_layernorm_offset,
            feature_mix_lookup_fraction,
            feature_mix_filter_fraction,
        ]
    )
    fading = logarithmic_fading_per_feature.reshape(1, H)
    bonus = present_entry_reward.reshape(1, H)
    time_pieces = gather_pieces(
        jnp.concatenate([lookup_projection, payload_projection, filter_projection], axis=1), 1
    )
    x_other = swap(x_own, "tp", 1)
    params_other = swap(params, "tp", 1)
    edge_out = block_entries[:, :, L - 1, :].reshape(R, H)
    edge_own = along_ctx(edge_out, 1, False)
    edge_other = along_ctx(edge_out, 1, True)
    emit_pieces = gather_pieces(temporal_mix_emit_projection, 0)
    hidden_pieces = gather_pieces(
        jnp.concatenate([feature_mix_lookup_proj, feature_mix_filter_proj], axis=1), 1
    )
    return_pieces = gather_pieces(feature_mix_payload_proj, 0)
    up_other = swap(up_own, "tp", 1)

    def mix_time(
        idx, xo, xp, eo, ep, po, pp, mixed_key, mixed_value, mixed_gate, hat, diff, root, hat_edge
    ):
        gain, bias = both(po, pp, 0), both(po, pp, 1)
        shares = [both(po, pp, i) for i in (2, 3, 4)]
        flag = jnp.where(idx[1] > 0, 1.0, 0.0).astype(F32)
        edge_hat, _ = norm(jnp.concatenate([eo[...], ep[...]], axis=1).astype(F32))
        hat_edge[...] = edge_hat * flag
        first = (edge_hat * gain + bias) * flag
        for r in range(R):

            def tile(i, last):
                at = rows_at(r, i)
                values = jnp.concatenate([xo[at, :], xp[at, :]], axis=1).astype(F32)
                n, q = norm(values)
                normed = n * gain + bias
                prev = shift_down(normed, last)
                hat[at, :] = n
                root[at, :] = q
                diff[at, :] = normed - prev
                for share, target in zip(shares, (mixed_key, mixed_value, mixed_gate)):
                    target[at, :] = (normed * share + prev * (1.0 - share)).astype(BF16)
                return normed[TB - 1 : TB, :]

            lax.fori_loop(0, NT, tile, first[r : r + 1, :])

    mixed_key, mixed_value, mixed_gate, hat_one, diff_one, root_one, hat_edge_one = launch(
        mix_time,
        "svvvvvv",
        (idx, x_own, x_other, edge_own, edge_other, params, params_other),
        [((T, WIDTH), BF16)] * 3
        + [((T, WIDTH), F32), ((T, WIDTH), F32), ((T, 1), F32), ((R, WIDTH), F32)],
    )

    def project_time(
        idx, mk, mv, mg, ld, p0, p1, p2, p3, p4, key, value, opened, states, closing, w, sems
    ):
        copies = place_rows(idx, [p0, p1, p2, p3, p4], w, sems)
        begin(copies)
        finish(copies)
        put(key, EVERY, dot(mk[...], w[:, :H]))
        put(value, EVERY, dot(mv[...], w[:, H : 2 * H]))
        rate = jnp.exp(ld[...])

        def step(t, carry):
            new = []
            for r in range(R):
                num, den, high = carry[r]
                k_now, v_now = get(key, step_rows(r, t)), get(value, step_rows(r, t))
                faded = high - rate
                top = jnp.maximum(faded, k_now)
                old, fresh = jnp.exp(faded - top), jnp.exp(k_now - top)
                new.append((old * num + fresh * v_now, old * den + fresh, top))
            return tuple(new)

        zero = jnp.zeros((CHUNKS, H), F32)
        ends = lax.fori_loop(0, ST, step, ((zero, zero, zero + lowest),) * R)
        for r in range(R):
            for part in range(3):
                put(states, pl.ds((part * R + r) * CHUNKS, CHUNKS), ends[r][part])
        total = tuple(get(states, chunk_rows(part, 0)) for part in range(3))
        for i in range(1, CHUNKS):
            total = combine(
                total, tuple(get(states, chunk_rows(part, i)) for part in range(3)), ST * rate
            )
        for part in range(3):
            closing[pl.ds(part * R, R), :] = total[part]
        opened[...] = jax.nn.sigmoid(dot(mg[...], w[:, 2 * H : 3 * H]))

    key, value, opened, states, closing = launch(
        project_time,
        "svvvv" + "h" * 5,
        (idx, mixed_key, mixed_value, mixed_gate, fading, *time_pieces),
        [((G, T, 128), F32)] * 2
        + [((T, H), F32), ((G, 3 * R * CHUNKS, 128), F32), ((3 * R, H), F32)],
        [pltpu.VMEM((WIDTH, 3 * H), BF16), pltpu.SemaphoreType.DMA((5,))],
    )

    rate = jnp.exp(fading)
    total = tuple(closing.reshape(3, R, H))
    prefix = (jnp.zeros((R, H), F32), jnp.zeros((R, H), F32), jnp.full((R, H), lowest, F32))
    for bit in range(bits_of(C)):
        other = tuple(swap(jnp.stack(total), "ctx", 1 << bit))
        up = (c_at >> bit) & 1 == 1
        span = rate * (L << bit)
        so_far = rate * (L * (c_at & ((1 << bit) - 1))).astype(F32)
        with_other = combine(other, prefix, so_far)
        prefix = tuple(jnp.where(up, a, b) for a, b in zip(with_other, prefix))
        if bit + 1 < bits_of(C):
            as_later, as_earlier = combine(other, total, span), combine(total, other, span)
            total = tuple(jnp.where(up, a, b) for a, b in zip(as_later, as_earlier))
    entering = jnp.concatenate(prefix, axis=0)

    def sweep_time(
        key, value, opened, ld, un, states, enter,
        gated, out, part_old, part_new, keep, fresh, nums, dens, fade, starts,
    ):
        rate = jnp.exp(ld[...])
        reward = un[...]
        state = tuple(enter[pl.ds(part * R, R), :] for part in range(3))
        for i in range(CHUNKS):
            for part in range(3):
                put(starts, chunk_rows(part, i), state[part])
            state = combine(
                state, tuple(get(states, chunk_rows(part, i)) for part in range(3)), ST * rate
            )

        def step(t, carry):
            new = []
            for r in range(R):
                num, den, high = carry[r]
                k_now, v_now = get(key, step_rows(r, t)), get(value, step_rows(r, t))
                at = scan_rows(r, t)
                now = reward + k_now
                top = jnp.maximum(high, now)
                e_old, e_new = jnp.exp(high - top), jnp.exp(now - top)
                inverse = 1.0 / (e_old * den + e_new)
                e_old, e_new = e_old * inverse, e_new * inverse
                put(out, step_rows(r, t), e_old * num + e_new * v_now)
                part_old[at, :] = e_old
                part_new[at, :] = e_new
                nums[at, :] = num
                dens[at, :] = den
                faded = high - rate
                peak = jnp.maximum(faded, k_now)
                a, b = jnp.exp(faded - peak), jnp.exp(k_now - peak)
                keep[at, :] = a
                fresh[at, :] = b
                new.append((a * num + b * v_now, a * den + b, peak))
            return tuple(new)

        begin_at = tuple(
            tuple(get(starts, pl.ds((part * R + r) * CHUNKS, CHUNKS)) for part in range(3))
            for r in range(R)
        )
        ends = lax.fori_loop(0, ST, step, begin_at)
        for r in range(R):
            put(
                fade,
                pl.ds(r * CHUNKS, CHUNKS),
                jnp.exp(begin_at[r][2] - ST * rate - ends[r][2]),
            )
        gated[...] = (opened[...] * get(out, EVERY)).astype(BF16)

    gated, mixed_out, part_old, part_new, keep, fresh, nums, dens, fade = launch(
        sweep_time,
        "v" * 7,
        (key, value, opened, fading, bonus, states, entering),
        [((T, H), BF16), ((G, T, 128), F32)]
        + [((T, H), F32)] * 6
        + [((G, R * CHUNKS, 128), F32)],
        [pltpu.VMEM((G, 3 * R * CHUNKS, 128), F32)],
    )

    def emit(idx, gated, p0, p1, p2, p3, p4, part, w, sems):
        copies = place_blocks(idx, [p0, p1, p2, p3, p4], w, sems)
        begin(copies)
        finish(copies)
        for p in range(S):
            part[:, p * SR : (p + 1) * SR] = dot(gated[...], w[p])

    (emitted,) = launch(
        emit,
        "sv" + "h" * 5,
        (idx, gated, *emit_pieces),
        [((T, WIDTH), F32)],
        [pltpu.VMEM((S, H, SR), BF16), pltpu.SemaphoreType.DMA((5,))],
    )
    emitted_other = swap(emitted, "tp", 1)

    def middle_norm(xo, xp, mine, theirs, middle, hat, root, last):
        for r in range(R):

            def tile(i, carry):
                at = rows_at(r, i)
                values = jnp.concatenate([xo[at, :], xp[at, :]], axis=1).astype(F32)
                values = values + (mine[at, :] + swapped(theirs[at, :]))
                n, q = norm(values)
                middle[at, :] = values[:, :H]
                hat[at, :] = n
                root[at, :] = q
                return n[TB - 1 : TB, :]

            last[r : r + 1, :] = lax.fori_loop(0, NT, tile, jnp.zeros((1, WIDTH), F32))

    middle, hat_two, root_two, hat_last = launch(
        middle_norm,
        "vvvv",
        (x_own, x_other, emitted, emitted_other),
        [((T, H), F32), ((T, WIDTH), F32), ((T, 1), F32), ((R, WIDTH), F32)],
    )
    hat_edge_two = along_ctx(hat_last, 1, False)

    NF = FH + H
    NB = min(512, FH)

    def channel_forward(
        idx, hat, edge, po, pp, h0, h1, h2, h3, h4, r0, r1, r2, r3, r4,
        ckey, cgate, diff, active, squared, keep_own, send_other, opened, wh, wr, sems_h, sems_r,
    ):
        copies_h = place_rows(idx, [h0, h1, h2, h3, h4], wh, sems_h)
        copies_r = place_blocks(idx, [r0, r1, r2, r3, r4], wr, sems_r)
        begin(copies_h)
        begin(copies_r)
        gain, bias = both(po, pp, 5), both(po, pp, 6)
        shares = [both(po, pp, i) for i in (7, 8)]
        flag = jnp.where(idx[1] > 0, 1.0, 0.0).astype(F32)
        first = (edge[...] * gain + bias) * flag
        for r in range(R):

            def tile(i, last):
                at = rows_at(r, i)
                normed = hat[at, :] * gain + bias
                prev = shift_down(normed, last)
                diff[at, :] = normed - prev
                for share, target in zip(shares, (ckey, cgate)):
                    target[at, :] = (normed * share + prev * (1.0 - share)).astype(BF16)
                return normed[TB - 1 : TB, :]

            lax.fori_loop(0, NT, tile, first[r : r + 1, :])
        finish(copies_h)
        for n in range(0, FH, NB):
            pre = jnp.maximum(dot(ckey[...], wh[:, n : n + NB]), 0.0)
            active[:, n : n + NB] = pre.astype(BF16)
            squared[:, n : n + NB] = (pre * pre).astype(BF16)
        opened[...] = jax.nn.sigmoid(dot(cgate[...], wh[:, FH:NF]))
        finish(copies_r)
        for p in range(S):
            target = keep_own if p < S // 2 else send_other
            at = (p % (S // 2)) * SR
            target[:, at : at + SR] = dot(squared[...], wr[p])

    channel_key, channel_gate, diff_two, active, squared, ret_keep, ret_send, filter_open = launch(
        channel_forward,
        "svvvv" + "h" * 10,
        (idx, hat_two, hat_edge_two, params, params_other, *hidden_pieces, *return_pieces),
        [
            ((T, WIDTH), BF16),
            ((T, WIDTH), BF16),
            ((T, WIDTH), F32),
            ((T, FH), BF16),
            ((T, FH), BF16),
            ((T, H), F32),
            ((T, H), F32),
            ((T, H), F32),
        ],
        [
            pltpu.VMEM((WIDTH, NF), BF16),
            pltpu.VMEM((S, FH, SR), BF16),
            pltpu.SemaphoreType.DMA((5,)),
            pltpu.SemaphoreType.DMA((5,)),
        ],
    )
    ret_other = swap(ret_send, "tp", 1)

    def live_rows(idx, r, i):
        at = lax.broadcasted_iota(jnp.int32, (TB, 1), 0) + (idx[1] * L + i * TB)
        return jnp.where(at < idx[3 + r], 1.0, 0.0).astype(F32)

    def close_block(idx, mine, theirs, opened, middle, up, out, grad_ret, grad_fil):
        for r in range(R):

            def tile(i, carry):
                at = rows_at(r, i)
                live = live_rows(idx, r, i)
                returned = mine[at, :] + theirs[at, :]
                s = opened[at, :]
                out[at, :] = (live * (middle[at, :] + s * returned)).astype(BF16)
                grad = live * up[at, :].astype(F32)
                grad_ret[at, :] = (grad * s).astype(BF16)
                grad_fil[at, :] = (grad * returned * s * (1.0 - s)).astype(BF16)
                return carry

            lax.fori_loop(0, NT, tile, 0)

    block_out, grad_returned, grad_filter = launch(
        close_block,
        "svvvvv",
        (idx, ret_keep, ret_other, filter_open, middle, up_own),
        [((T, H), BF16)] * 3,
    )
    grad_returned_other = swap(grad_returned, "tp", 1)

    def channel_backward(
        idx, gro, grp, gf, active, diff, hat, edge, po, pp,
        h0, h1, h2, h3, h4, r0, r1, r2, r3, r4,
        grad_hidden, grad_normed, first_out, sums, wh, wr, ckey, cgate, sems_h, sems_r,
    ):
        copies_h = place_rows(idx, [h0, h1, h2, h3, h4], wh, sems_h)
        copies_r = place_blocks(idx, [r0, r1, r2, r3, r4], wr, sems_r)
        begin(copies_r)
        begin(copies_h)
        finish(copies_r)
        half = S // 2
        for n in range(0, FH, NB):
            acc = None
            for p in range(S):
                source = gro if p < half else grp
                at = (p % half) * SR
                term = dot_t(source[:, at : at + SR], wr[p, n : n + NB, :])
                acc = term if acc is None else acc + term
            grad_hidden[:, n : n + NB] = (
                acc * 2.0 * active[:, n : n + NB].astype(F32)
            ).astype(BF16)
        finish(copies_h)
        for p in range(S):
            at = slice(p * SR, (p + 1) * SR)
            ckey[:, at] = dot_t(grad_hidden[...], wh[at, :FH])
            cgate[:, at] = dot_t(gf[...], wh[at, FH:NF])
        share_k, share_g = both(po, pp, 7), both(po, pp, 8)
        flag = jnp.where(idx[1] > 0, 1.0, 0.0).astype(F32)
        zero = jnp.zeros((1, WIDTH), F32)
        totals = (zero, zero, zero, zero)
        for r in range(R):

            def tile(j, carry):
                after, gain_sum, bias_sum, key_sum, gate_sum = carry
                at = rows_at(r, NT - 1 - j)
                gk, gg, d = ckey[at, :], cgate[at, :], diff[at, :]
                now = gk * share_k + gg * share_g
                back = gk * (1.0 - share_k) + gg * (1.0 - share_g)
                grad = now + shift_up(back, after)
                grad_normed[at, :] = grad
                return (
                    back[0:1, :],
                    gain_sum + jnp.sum(grad * hat[at, :], axis=0, keepdims=True),
                    bias_sum + jnp.sum(grad, axis=0, keepdims=True),
                    key_sum + jnp.sum(gk * d, axis=0, keepdims=True),
                    gate_sum + jnp.sum(gg * d, axis=0, keepdims=True),
                )

            front, *totals = lax.fori_loop(0, NT, tile, (zero, *totals))
            first_out[r : r + 1, :] = front
            totals[0] = totals[0] + front * (edge[r : r + 1, :] * flag)
            totals[1] = totals[1] + front * flag
        for i in range(4):
            sums[i : i + 1, :] = totals[i]

    grad_hidden, grad_two, first_two, sums_two = launch(
        channel_backward,
        "s" + "v" * 9 + "h" * 10,
        (
            idx,
            grad_returned,
            grad_returned_other,
            grad_filter,
            active,
            diff_two,
            hat_two,
            hat_edge_two,
            params,
            params_other,
            *hidden_pieces,
            *return_pieces,
        ),
        [((T, FH), BF16), ((T, WIDTH), F32), ((R, WIDTH), F32), ((4, WIDTH), F32)],
        [
            pltpu.VMEM((WIDTH, NF), BF16),
            pltpu.VMEM((S, FH, SR), BF16),
            pltpu.VMEM((T, WIDTH), F32),
            pltpu.VMEM((T, WIDTH), F32),
            pltpu.SemaphoreType.DMA((5,)),
            pltpu.SemaphoreType.DMA((5,)),
        ],
    )
    grad_two_other = swap(grad_two, "tp", 1)
    first_two_own = along_ctx(first_two, -1, False)
    first_two_other = along_ctx(first_two, -1, True)

    order = []
    for spot in range(BLOCKS):
        high, low = spot // C, spot % C
        turned = 0
        for bit in range(bits_of(C)):
            turned = turned * 2 + ((low >> bit) & 1)
        order.append(high * C + turned)

    def weight_grads(lefts, rights, jobs):
        count_left = [len(group) for group in lefts]
        flat = [ref for group in lefts for ref in group]
        width = sum(job[3] for job in jobs if job[4] == 0)

        def weight_products(idx, *refs):
            left_refs = list(refs[: len(flat)])
            right_refs = refs[len(flat) : len(flat) + len(rights)]
            send_a, keep_a, send_b, keep_b, tall, turned = refs[len(flat) + len(rights) :]
            groups = []
            for count in count_left:
                groups.append(left_refs[:count])
                left_refs = left_refs[count:]
            half, quarter = WIDTH // 2, WIDTH // 4
            for g, group in enumerate(groups):
                row = 0
                for ref in group:
                    for lane in range(0, ref.shape[1], 128):
                        tall[row : row + 128, :] = ref[:, lane : lane + 128].astype(F32).T
                        row += 128
                for spot in range(BLOCKS):
                    block = order[spot] ^ idx[2]
                    turned[spot * BR : (spot + 1) * BR, :] = tall[
                        pl.ds(pl.multiple_of(block * BR, BR), BR), :
                    ].astype(BF16)
                for left, right, start, size, part, at in jobs:
                    if left != g:
                        continue
                    for n in range(0, size, 256):
                        to = slice(at + n, at + n + 256)
                        acc = dot(
                            turned[...], right_refs[right][:, start + n : start + n + 256]
                        ).astype(BF16)
                        if part == 0:
                            keep_a[:quarter, to] = acc[:quarter]
                            send_a[:quarter, to] = acc[quarter:half]
                            keep_a[quarter:, to] = acc[half : half + quarter]
                            send_a[quarter:, to] = acc[half + quarter :]
                        else:
                            keep_b[:, to] = acc[:half]
                            send_b[:, to] = acc[half:]

        return launch(
            weight_products,
            "s" + "v" * (len(flat) + len(rights)),
            (idx, *flat, *rights),
            [((WIDTH // 2, width), BF16)] * 4,
            [pltpu.VMEM((WIDTH, T), F32), pltpu.VMEM((WIDTH, T), BF16)],
        )

    def add(mine, theirs):
        return mine.astype(F32) + theirs.astype(F32)

    def halves(values):
        half = values.shape[0] // 2
        return values[:half], values[half:]

    def scatter(send_a, keep_a, send_b, keep_b):
        got_a, got_b = swap(send_a, "shard", 1), swap(send_b, "shard", 2)
        keep_a, send_a = halves(add(keep_a, got_a).astype(BF16))
        keep_b, send_b = halves(add(keep_b, got_b).astype(BF16))
        got_a, got_b = swap(send_a, "shard", 2), swap(send_b, "shard", 1)
        joined = jnp.concatenate([add(keep_a, got_a), add(keep_b, got_b)], axis=1)
        for bit in range(bits_of(C)):
            mine, theirs = halves(joined.astype(BF16))
            joined = add(mine, swap(theirs, "ctx", 1 << bit))
        return joined

    return_w = scatter(
        *weight_grads(
            [[grad_returned, grad_returned_other]],
            [squared],
            [(0, 0, 0, FH // 2, 0, 0), (0, 0, FH // 2, FH // 2, 1, 0)],
        )
    )
    part = NF // 2
    hidden_w = scatter(
        *weight_grads(
            [[channel_key], [channel_gate]],
            [grad_hidden, grad_filter],
            [
                (0, 0, 0, part, 0, 0),
                (0, 0, part, FH - part, 1, 0),
                (1, 1, 0, H, 1, FH - part),
            ],
        )
    )

    def middle_backward(
        idx, mine, theirs, e_own, e_other, hat, root, po, pp, uo, upp, opened, out,
        part_old, keep, fade, p0, p1, p2, p3, p4,
        grad_mid, grad_own, grad_res, grad_gate, adjoint, entry, w, gates, sems,
    ):
        copies = place_blocks(idx, [p0, p1, p2, p3, p4], w, sems)
        begin(copies)
        gain = both(po, pp, 5)
        tail = e_own[...] + swapped(e_other[...])
        row = lax.broadcasted_iota(jnp.int32, (TB, 1), 0)
        for r in range(R):

            def tile(i, carry):
                at = rows_at(r, i)
                is_last = jnp.where((row == TB - 1) & (i == NT - 1), 1.0, 0.0).astype(F32)
                grad = mine[at, :] + swapped(theirs[at, :]) + is_last * tail[r : r + 1, :]
                n = hat[at, :]
                scaled = grad * gain
                mean_one = jnp.sum(scaled, axis=-1, keepdims=True) * (1.0 / WIDTH)
                mean_two = jnp.sum(scaled * n, axis=-1, keepdims=True) * (1.0 / WIDTH)
                up = jnp.concatenate([uo[at, :], upp[at, :]], axis=1).astype(F32)
                full = live_rows(idx, r, i) * up + root[at, :] * (scaled - mean_one - n * mean_two)
                grad_mid[at, :] = full.astype(BF16)
                grad_own[at, :] = full[:, :H]
                return carry

            lax.fori_loop(0, NT, tile, 0)
        finish(copies)
        acc = None
        for p in range(S):
            term = dot_t(grad_mid[:, p * SR : (p + 1) * SR], w[p])
            acc = term if acc is None else acc + term
        gates[...] = acc
        for r in range(R):

            def gate_tile(i, carry):
                at = rows_at(r, i)
                g, s = gates[at, :], opened[at, :]
                put(grad_res, at, g * s)
                grad_gate[at, :] = (g * get(out, at) * s * (1.0 - s)).astype(BF16)
                return carry

            lax.fori_loop(0, NT, gate_tile, 0)

        def step(j, carry):
            t = ST - 1 - j
            new = []
            for r in range(R):
                alpha, beta = carry[r]
                at = scan_rows(r, t)
                direct = part_old[at, :] * get(grad_res, step_rows(r, t))
                a = keep[at, :]
                new.append(
                    (direct + a * alpha, a * beta - direct * get(out, step_rows(r, t)))
                )
            return tuple(new)

        zero = jnp.zeros((CHUNKS, H), F32)
        ends = lax.fori_loop(0, ST, step, ((zero, zero),) * R)
        for r in range(R):
            for k in range(2):
                put(adjoint, pl.ds((k * R + r) * CHUNKS, CHUNKS), ends[r][k])
        alpha = beta = jnp.zeros((R, H), F32)
        span = jnp.ones((R, H), F32)
        for i in range(CHUNKS - 1, -1, -1):
            f = get(fade, chunk_rows(0, i))
            alpha = get(adjoint, chunk_rows(0, i)) + f * alpha
            beta = get(adjoint, chunk_rows(1, i)) + f * beta
            span = span * f
        entry[pl.ds(0, R), :] = alpha
        entry[pl.ds(R, R), :] = beta
        entry[pl.ds(2 * R, R), :] = span

    grad_mid, grad_mid_own, grad_res, grad_gate, adjoint, entry = launch(
        middle_backward,
        "s" + "v" * 15 + "h" * 5,
        (
            idx,
            grad_two,
            grad_two_other,
            first_two_own,
            first_two_other,
            hat_two,
            root_two,
            params,
            params_other,
            up_own,
            up_other,
            opened,
            mixed_out,
            part_old,
            keep,
            fade,
            *emit_pieces,
        ),
        [
            ((T, WIDTH), BF16),
            ((T, H), F32),
            ((G, T, 128), F32),
            ((T, H), BF16),
            ((G, 2 * R * CHUNKS, 128), F32),
            ((3 * R, H), F32),
        ],
        [
            pltpu.VMEM((S, H, SR), BF16),
            pltpu.VMEM((T, H), F32),
            pltpu.SemaphoreType.DMA((5,)),
        ],
    )

    alpha, beta, span = entry.reshape(3, R, H)
    late_alpha = late_beta = jnp.zeros((R, H), F32)
    late_span = jnp.ones((R, H), F32)
    for bit in range(bits_of(C)):
        alpha_o, beta_o, span_o = swap(jnp.stack([alpha, beta, span]), "ctx", 1 << bit)
        low = (c_at >> bit) & 1 == 0
        late_alpha, late_beta, late_span = (
            jnp.where(low, late_alpha + late_span * alpha_o, late_alpha),
            jnp.where(low, late_beta + late_span * beta_o, late_beta),
            jnp.where(low, late_span * span_o, late_span),
        )
        if bit + 1 < bits_of(C):
            alpha, beta, span = (
                jnp.where(low, alpha + span * alpha_o, alpha_o + span_o * alpha),
                jnp.where(low, beta + span * beta_o, beta_o + span_o * beta),
                span * span_o,
            )
    late = jnp.concatenate([late_alpha, late_beta], axis=0)

    early_w = scatter(
        *weight_grads(
            [[grad_mid], [mixed_gate]],
            [gated, grad_gate],
            [(0, 0, 0, H, 0, 0), (1, 1, 0, H, 1, 0)],
        )
    )

    def time_backward(
        idx, res, out, value, part_old, part_new, keep, fresh, nums, dens, fade, adjoint, late,
        ld, gate, diff, hat, edge, po, pp, p0, p1, p2, p3, p4,
        grad_key, grad_value, mine_own, send, first_out, sums, sums_own,
        w, dk, dv, gk, gv, gg, starts, sems,
    ):
        copies = place_rows(idx, [p0, p1, p2, p3, p4], w, sems)
        begin(copies)
        late_now = (late[pl.ds(0, R), :], late[pl.ds(R, R), :])
        for i in range(CHUNKS - 1, -1, -1):
            for k in range(2):
                put(starts, chunk_rows(k, i), late_now[k])
            f = get(fade, chunk_rows(0, i))
            late_now = tuple(get(adjoint, chunk_rows(k, i)) + f * late_now[k] for k in range(2))

        def step(j, carry):
            t = ST - 1 - j
            adj, fade_sum, bonus_sum = carry
            new = []
            for r in range(R):
                alpha, beta = adj[r]
                at, spread = scan_rows(r, t), step_rows(r, t)
                g, y, v = get(res, spread), get(out, spread), get(value, spread)
                b, a = fresh[at, :], keep[at, :]
                near = part_new[at, :] * g
                lift = near * (v - y)
                put(dv, spread, b * alpha + near)
                put(dk, spread, b * (v * alpha + beta) + lift)
                bonus_sum = bonus_sum + lift
                fade_sum = fade_sum - a * (nums[at, :] * alpha + dens[at, :] * beta)
                direct = part_old[at, :] * g
                new.append((direct + a * alpha, a * beta - direct * y))
            return (tuple(new), fade_sum, bonus_sum)

        first_adj = tuple(
            tuple(get(starts, pl.ds((k * R + r) * CHUNKS, CHUNKS)) for k in range(2))
            for r in range(R)
        )
        zero = jnp.zeros((CHUNKS, H), F32)
        _, fade_sum, bonus_sum = lax.fori_loop(0, ST, step, (first_adj, zero, zero))
        sums_own[0:1, :] = jnp.sum(fade_sum, axis=0, keepdims=True) * jnp.exp(ld[...])
        sums_own[1:2, :] = jnp.sum(bonus_sum, axis=0, keepdims=True)
        grad_key[...] = get(dk, EVERY).astype(BF16)
        grad_value[...] = get(dv, EVERY).astype(BF16)
        finish(copies)
        gk[...] = dot_t(grad_key[...], w[:, :H])
        gv[...] = dot_t(grad_value[...], w[:, H : 2 * H])
        gg[...] = dot_t(gate[...], w[:, 2 * H : 3 * H])
        gain = both(po, pp, 0)
        shares = [both(po, pp, i) for i in (2, 3, 4)]
        flag = jnp.where(idx[1] > 0, 1.0, 0.0).astype(F32)
        zero = jnp.zeros((1, WIDTH), F32)
        totals = (zero,) * 5
        lane = lax.broadcasted_iota(jnp.int32, (TB, 128), 1)
        for r in range(R):

            def tile(j, carry):
                after, gain_sum, bias_sum, *mix_sums = carry
                at = rows_at(r, NT - 1 - j)
                grads = (gk[at, :], gv[at, :], gg[at, :])
                d, n = diff[at, :], hat[at, :]
                now = back = None
                for share, grad in zip(shares, grads):
                    a, b = grad * share, grad * (1.0 - share)
                    now = a if now is None else now + a
                    back = b if back is None else back + b
                grad = now + shift_up(back, after)
                mine_own[at, :] = grad[:, :H]
                send[at, :H] = grad[:, H:]
                scaled = grad * gain
                one = jnp.sum(scaled, axis=-1, keepdims=True)
                two = jnp.sum(scaled * n, axis=-1, keepdims=True)
                send[at, H:] = jnp.where(lane == 0, one, jnp.where(lane == 1, two, 0.0))
                return (
                    back[0:1, :],
                    gain_sum + jnp.sum(grad * n, axis=0, keepdims=True),
                    bias_sum + jnp.sum(grad, axis=0, keepdims=True),
                    *(
                        total + jnp.sum(one_grad * d, axis=0, keepdims=True)
                        for total, one_grad in zip(mix_sums, grads)
                    ),
                )

            front, *totals = lax.fori_loop(0, NT, tile, (zero, *totals))
            first_out[r : r + 1, :] = front
            totals[0] = totals[0] + front * edge[r : r + 1, :]
            totals[1] = totals[1] + front * flag
        for i in range(5):
            sums[i : i + 1, :] = totals[i]

    grad_key, grad_value, one_own, one_send, first_one, sums_one, sums_own = launch(
        time_backward,
        "s" + "v" * 19 + "h" * 5,
        (
            idx,
            grad_res,
            mixed_out,
            value,
            part_old,
            part_new,
            keep,
            fresh,
            nums,
            dens,
            fade,
            adjoint,
            late,
            fading,
            grad_gate,
            diff_one,
            hat_one,
            hat_edge_one,
            params,
            params_other,
            *time_pieces,
        ),
        [
            ((T, H), BF16),
            ((T, H), BF16),
            ((T, H), F32),
            ((T, H + 128), F32),
            ((R, WIDTH), F32),
            ((5, WIDTH), F32),
            ((2, H), F32),
        ],
        [pltpu.VMEM((WIDTH, 3 * H), BF16)]
        + [pltpu.VMEM((G, T, 128), F32)] * 2
        + [pltpu.VMEM((T, WIDTH), F32)] * 3
        + [pltpu.VMEM((G, 2 * R * CHUNKS, 128), F32), pltpu.SemaphoreType.DMA((5,))],
    )
    one_other = swap(one_send, "tp", 1)
    first_one_own = along_ctx(first_one, -1, False)
    first_one_other = along_ctx(first_one, -1, True)

    late_w = scatter(
        *weight_grads(
            [[mixed_key], [mixed_value]],
            [grad_key, grad_value],
            [(0, 0, 0, H, 0, 0), (1, 1, 0, H, 1, 0)],
        )
    )

    wide = jnp.concatenate([sums_one, sums_two], axis=0)
    own = wide[:, :H] + swap(wide[:, H:], "tp", 1)
    vectors = jnp.concatenate([own, sums_own], axis=0)
    for bit in range(bits_of(S)):
        vectors = vectors + swap(vectors, "shard", 1 << bit)
    for bit in range(bits_of(C)):
        vectors = vectors + swap(vectors, "ctx", 1 << bit)

    def input_backward(mine, sent, theirs, e_own, e_other, hat, root, po, pp, gm, out):
        gain_full = both(po, pp, 0)
        tail = e_own[...] + swapped(e_other[...])
        row = lax.broadcasted_iota(jnp.int32, (TB, 1), 0)
        for r in range(R):
            weighted = tail[r : r + 1, :] * gain_full
            tail_one = jnp.sum(weighted, axis=-1, keepdims=True)
            tail_two = jnp.sum(
                weighted * hat[(r + 1) * L - 1 : (r + 1) * L, :], axis=-1, keepdims=True
            )

            def tile(i, carry):
                at = rows_at(r, i)
                is_last = jnp.where((row == TB - 1) & (i == NT - 1), 1.0, 0.0).astype(F32)
                grad = mine[at, :] + theirs[at, :H] + is_last * tail[r : r + 1, :H]
                stats = sent[at, H:] + theirs[at, H:]
                mean_one = (stats[:, 0:1] + is_last * tail_one) * (1.0 / WIDTH)
                mean_two = (stats[:, 1:2] + is_last * tail_two) * (1.0 / WIDTH)
                scaled = grad * gain_full[:, :H]
                out[at, :] = gm[at, :] + root[at, :] * (
                    scaled - mean_one - hat[at, :H] * mean_two
                )
                return carry

            lax.fori_loop(0, NT, tile, 0)

    (input_grad,) = launch(
        input_backward,
        "v" * 10,
        (
            one_own,
            one_send,
            one_other,
            first_one_own,
            first_one_other,
            hat_one,
            root_one,
            params,
            params_other,
            grad_mid_own,
        ),
        [((T, H), F32)],
    )

    shape = block_entries.shape
    return (
        block_out.reshape(shape),
        input_grad.reshape(shape),
        vectors[0],
        vectors[1],
        vectors[2],
        vectors[3],
        vectors[4],
        vectors[9],
        vectors[10],
        early_w[:, H:],
        late_w[:, :H],
        late_w[:, H:],
        early_w[:, :H].T,
        vectors[5],
        vectors[6],
        vectors[7],
        vectors[8],
        hidden_w[:, :FH],
        hidden_w[:, FH:],
        return_w.T,
    )


def solution(mesh):
    token = P(None, "shard", "ctx", "tp")
    feature = P("tp")
    rows = P("shard", "tp")
    cols = P("tp", "shard")
    rows_out = P(("shard", "ctx"), "tp")
    cols_out = P("tp", ("shard", "ctx"))
    return jax.shard_map(
        per_device,
        mesh=mesh,
        in_specs=(
            (token, P(None, "shard"), token)
            + (feature,) * 7
            + (rows, rows, rows, cols)
            + (feature,) * 4
            + (rows, rows, cols)
        ),
        out_specs=(
            (token, token)
            + (feature,) * 7
            + (rows_out, rows_out, rows_out, cols_out)
            + (feature,) * 4
            + (rows_out, rows_out, cols_out)
        ),
        check_vma=False,
    )
```

```python
import jax
import jax.numpy as jnp
from jax import lax
from jax.experimental import pallas as pl
from jax.experimental.pallas import tpu as pltpu
from jax.sharding import PartitionSpec as P

F32, BF16 = jnp.float32, jnp.bfloat16
WIDTH = 1024
epsilon = 1e-05
lowest = -1e30
CHUNKS = 8
SPARE = 6 * 2**20

VMEM = pl.BlockSpec(memory_space=pltpu.VMEM)
SMEM = pl.BlockSpec(memory_space=pltpu.SMEM)
HBM = pl.BlockSpec(memory_space=pl.ANY)
KINDS = {"v": VMEM, "s": SMEM, "h": HBM}


def padded_bytes(shape, dtype):
    rows = -(-shape[-2] // 8) * 8
    lanes = -(-shape[-1] // 128) * 128
    size = rows * lanes * jnp.dtype(dtype).itemsize
    for dim in shape[:-2]:
        size *= dim
    return size


def launch(body, kinds, inputs, outs, scratch=(), after=()):
    count = len(kinds)
    room = sum(padded_bytes(x.shape, x.dtype) for x in scratch if len(x.shape) > 1) + SPARE

    def run(*refs):
        body(*refs[:count], *refs[count + len(after) :])

    return pl.pallas_call(
        run,
        out_shape=[
            jax.ShapeDtypeStruct(shape, dtype) for shape, dtype in outs
        ],
        in_specs=[KINDS[kind] for kind in kinds] + [HBM] * len(after),
        out_specs=[VMEM] * len(outs),
        scratch_shapes=list(scratch),
        name=body.__name__,
        compiler_params=pltpu.CompilerParams(vmem_limit_bytes=room),
    )(*inputs, *after)


def side_by_side(*parts):
    widths = [part.shape[1] for part in parts]

    def pack(*refs):
        sources, whole, sems = refs[: len(parts)], refs[-2], refs[-1]
        copies, at = [], 0
        for i, source in enumerate(sources):
            target = whole.at[:, pl.ds(at, widths[i])]
            copies.append(pltpu.make_async_copy(source, target, sems.at[i]))
            at += widths[i]
        begin(copies)
        finish(copies)

    (whole,) = launch(
        pack,
        "h" * len(parts),
        [pltpu.with_memory_space_constraint(part, pltpu.HBM) for part in parts],
        [((parts[0].shape[0], sum(widths)), parts[0].dtype)],
        [pltpu.SemaphoreType.DMA((len(parts),))],
    )
    return whole


def hold(values, *others):
    return lax.optimization_barrier((values, others))[0]


def bits_of(count):
    return count.bit_length() - 1


def swap(value, axis, step):
    size = lax.axis_size(axis)
    return lax.ppermute(value, axis, [(i, i ^ step) for i in range(size)])


def along_ctx(value, step, cross):
    count = lax.axis_size("ctx")
    if not cross:
        pairs = [(i, i + step) for i in range(count) if 0 <= i + step < count]
        return lax.ppermute(value, "ctx", pairs)
    pairs = []
    for i in range(count):
        if 0 <= i + step < count:
            for core in range(2):
                pairs.append((2 * i + core, 2 * (i + step) + 1 - core))
    return lax.ppermute(value, ("ctx", "tp"), pairs)


def gather_first(matrix):
    return swap(matrix, "shard", 1), swap(matrix, "shard", 2)


def gather_turn(across, cut):
    half = across[0].shape[cut] // 2
    return (
        lax.slice_in_dim(across[0], 0, half, axis=cut),
        lax.slice_in_dim(across[1], half, 2 * half, axis=cut),
    )


def gather_cross(turn):
    return swap(turn[0], "shard", 2), swap(turn[1], "shard", 1)


def place_rows(idx, pieces, whole, sems, start=0, stop=None):
    base = idx[0]
    rows, cols = pieces[0].shape
    half = cols // 2
    stop = cols if stop is None else stop

    def spot(step):
        return pl.ds(pl.multiple_of((base ^ step) * rows, rows), rows)

    copies = []
    for step in range(3):
        copies.append((pieces[step].at[:, pl.ds(start, stop - start)], whole.at[spot(step), :]))
    for i in range(2):
        low, high = max(start, i * half), min(stop, (i + 1) * half)
        if low < high:
            source = pieces[3 + i].at[:, pl.ds(low - i * half, high - low)]
            copies.append((source, whole.at[spot(3), pl.ds(low - start, high - low)]))
    return [
        pltpu.make_async_copy(source, target, sems.at[i])
        for i, (source, target) in enumerate(copies)
    ]


def place_blocks(idx, pieces, whole, sems):
    base = idx[0]
    half = pieces[0].shape[0] // 2
    targets = [
        whole.at[base],
        whole.at[base ^ 1],
        whole.at[base ^ 2],
        whole.at[base ^ 3, pl.ds(0, half), :],
        whole.at[base ^ 3, pl.ds(half, half), :],
    ]
    return [
        pltpu.make_async_copy(piece, target, sems.at[i])
        for i, (piece, target) in enumerate(zip(pieces, targets))
    ]


def begin(copies):
    for copy in copies:
        copy.start()


def finish(copies):
    for copy in copies:
        copy.wait()


def dot(left, right):
    return jnp.dot(left, right, preferred_element_type=F32)


def dot_t(left, right):
    return lax.dot_general(left, right, (((1,), (1,)), ((), ())), preferred_element_type=F32)


def norm(values):
    center = jnp.sum(values, axis=-1, keepdims=True) * (1.0 / WIDTH)
    squares = jnp.sum(values * values, axis=-1, keepdims=True) * (1.0 / WIDTH)
    root = lax.rsqrt(squares - center * center + epsilon)
    return (values - center) * root, root


def both(own, other, i):
    return jnp.concatenate([own[i : i + 1, :], other[i : i + 1, :]], axis=1)


def shift_down(values, first):
    row = lax.broadcasted_iota(jnp.int32, values.shape, 0)
    return jnp.where(row == 0, first, pltpu.roll(values, 1, 0))


def shift_up(values, last):
    count = values.shape[0]
    row = lax.broadcasted_iota(jnp.int32, values.shape, 0)
    return jnp.where(row == count - 1, last, pltpu.roll(values, count - 1, 0))


def combine(earlier, later, later_span):
    shifted = earlier[2] - later_span
    high = jnp.maximum(shifted, later[2])
    early = jnp.exp(shifted - high)
    late = jnp.exp(later[2] - high)
    return (earlier[0] * early + later[0] * late, earlier[1] * early + later[1] * late, high)


def get(ref, rows):
    return jnp.concatenate([ref[g, rows, :] for g in range(ref.shape[0])], axis=1)


def put(ref, rows, values):
    for g in range(ref.shape[0]):
        ref[g, rows, :] = values[:, g * 128 : (g + 1) * 128]


def columns(refs, rows):
    return jnp.concatenate([ref[rows, :] for ref in refs], axis=1)


def swap_parts(parts):
    half = len(parts) // 2
    got = [swap(part, "tp", 1) for part in parts]
    return got[half:] + got[:half]


def swapped(values):
    half = values.shape[1] // 2
    return jnp.concatenate([values[:, half:], values[:, :half]], axis=1)


def per_device(
    block_entries,
    row_extents,
    upstream_loss_deriv,
    earlier_layernorm_scaling,
    earlier_layernorm_offset,
    temporal_mix_lookup_fraction,
    temporal_mix_payload_fraction,
    temporal_mix_filter_fraction,
    logarithmic_fading_per_feature,
    present_entry_reward,
    filter_projection,
    lookup_projection,
    payload_projection,
    temporal_mix_emit_projection,
    later_layernorm_scaling,
    later_layernorm_offset,
    feature_mix_lookup_fraction,
    feature_mix_filter_fraction,
    feature_mix_lookup_proj,
    feature_mix_filter_proj,
    feature_mix_payload_proj,
):
    batches, rows_local, L, H = block_entries.shape
    R = batches * rows_local
    T = R * L
    S, C = lax.axis_size("shard"), lax.axis_size("ctx")
    FH = feature_mix_lookup_proj.shape[1]
    ST = L // CHUNKS
    TB = min(32, L)
    NT = L // TB
    G = H // 128
    EVERY = slice(None)
    BLOCKS = S * C
    BR = WIDTH // BLOCKS
    SR = WIDTH // S
    assert S == 4 and WIDTH == 2 * H
    s_at, c_at, t_at = lax.axis_index("shard"), lax.axis_index("ctx"), lax.axis_index("tp")
    idx = jnp.concatenate(
        [
            jnp.stack(
                [s_at ^ (2 * t_at), c_at, (s_at * C + c_at) ^ (t_at * (BLOCKS // 2))]
            ).astype(jnp.int32),
            row_extents.reshape(R).astype(jnp.int32),
        ]
    )

    def rows_at(r, i):
        return pl.ds(pl.multiple_of(r * L + i * TB, TB), TB)

    def scan_rows(r, t):
        return pl.ds(pl.multiple_of((r * ST + t) * CHUNKS, CHUNKS), CHUNKS)

    def step_rows(r, t):
        return pl.ds(r * L + t, CHUNKS, stride=ST)

    def chunk_rows(part, i):
        return pl.ds(part * R * CHUNKS + i, R, stride=CHUNKS)

    x_own = block_entries.reshape(T, H)
    up_own = upstream_loss_deriv.reshape(T, H)
    params = jnp.stack(
        [
            earlier_layernorm_scaling,
            earlier_layernorm_offset,
            temporal_mix_lookup_fraction,
            temporal_mix_payload_fraction,
            temporal_mix_filter_fraction,
            later_layernorm_scaling,
            later_layernorm_offset,
            feature_mix_lookup_fraction,
            feature_mix_filter_fraction,
        ]
    )
    fading = logarithmic_fading_per_feature.reshape(1, H)
    bonus = present_entry_reward.reshape(1, H)
    time_matrix = side_by_side(
        lookup_projection,
        payload_projection,
        filter_projection,
        temporal_mix_emit_projection.T,
    )
    time_first = gather_first(time_matrix)
    x_other = swap(x_own, "tp", 1)
    params_other = swap(params, "tp", 1)
    last_rows = [
        part.reshape(batches, rows_local, L, H)[:, :, L - 1, :].reshape(R, H)
        for part in (x_own, x_other)
    ]
    edge = along_ctx(jnp.concatenate(last_rows, axis=1), 1, False)
    up_other = swap(up_own, "tp", 1)

    def mix_time(
        idx, xo, xp, ed, po, pp, mixed_key, mixed_value, mixed_gate, hat, diff, root, hat_edge
    ):
        gain, bias = both(po, pp, 0), both(po, pp, 1)
        shares = [both(po, pp, i) for i in (2, 3, 4)]
        flag = jnp.where(idx[1] > 0, 1.0, 0.0).astype(F32)
        edge_hat, _ = norm(ed[...].astype(F32))
        hat_edge[...] = edge_hat * flag
        first = (edge_hat * gain + bias) * flag
        for r in range(R):

            def tile(i, last):
                at = rows_at(r, i)
                values = jnp.concatenate([xo[at, :], xp[at, :]], axis=1).astype(F32)
                n, q = norm(values)
                normed = n * gain + bias
                prev = shift_down(normed, last)
                hat[at, :] = n.astype(BF16)
                root[at, :] = q
                diff[at, :] = (normed - prev).astype(BF16)
                for share, target in zip(shares, (mixed_key, mixed_value, mixed_gate)):
                    target[at, :] = (normed * share + prev * (1.0 - share)).astype(BF16)
                return normed[TB - 1 : TB, :]

            lax.fori_loop(0, NT, tile, first[r : r + 1, :])

    def mixes(*tokens):
        return launch(
            mix_time,
            "svvvvv",
            (idx, *tokens, edge, params, params_other),
            [((T, WIDTH), BF16)] * 5 + [((T, 1), F32), ((R, WIDTH), F32)],
        )

    mixed_key, mixed_value, mixed_gate, *_, hat_edge_one = mixes(x_own, x_other)
    time_turn = gather_turn(hold(time_first, hat_edge_one), 1)
    time_across = gather_cross(time_turn)
    time_pieces = [time_matrix, *time_first, *time_across]
    hidden_matrix = side_by_side(feature_mix_lookup_proj, feature_mix_filter_proj)
    hidden_first = gather_first(hold(hidden_matrix, time_across))
    return_matrix = hold(feature_mix_payload_proj, time_across)
    return_first = gather_first(return_matrix)
    return_turn_in = gather_turn(return_first, 0)
    return_across = gather_cross(return_turn_in)
    return_pieces = [return_matrix, *return_first, *return_across]

    def project_time(
        idx, mk, mv, mg, ld, p0, p1, p2, p3, p4, key, value, opened, states, closing, w, sems
    ):
        copies = place_rows(idx, [p0, p1, p2, p3, p4], w, sems, 0, 3 * H)
        begin(copies)
        finish(copies)
        put(key, EVERY, dot(mk[...], w[:, :H]))
        put(value, EVERY, dot(mv[...], w[:, H : 2 * H]))
        rate = jnp.exp(ld[...])

        def step(t, carry):
            new = []
            for r in range(R):
                num, den, high = carry[r]
                k_now, v_now = get(key, step_rows(r, t)), get(value, step_rows(r, t))
                faded = high - rate
                top = jnp.maximum(faded, k_now)
                old, fresh = jnp.exp(faded - top), jnp.exp(k_now - top)
                new.append((old * num + fresh * v_now, old * den + fresh, top))
            return tuple(new)

        zero = jnp.zeros((CHUNKS, H), F32)
        ends = lax.fori_loop(0, ST, step, ((zero, zero, zero + lowest),) * R)
        for r in range(R):
            for part in range(3):
                put(states, pl.ds((part * R + r) * CHUNKS, CHUNKS), ends[r][part])
        total = tuple(get(states, chunk_rows(part, 0)) for part in range(3))
        for i in range(1, CHUNKS):
            total = combine(
                total, tuple(get(states, chunk_rows(part, i)) for part in range(3)), ST * rate
            )
        for part in range(3):
            closing[pl.ds(part * R, R), :] = total[part]
        opened[...] = jax.nn.sigmoid(dot(mg[...], w[:, 2 * H : 3 * H]))

    key, value, opened, states, closing = launch(
        project_time,
        "svvvv" + "h" * 5,
        (idx, mixed_key, mixed_value, mixed_gate, fading, *time_pieces),
        [((G, T, 128), F32)] * 2
        + [((T, H), F32), ((G, 3 * R * CHUNKS, 128), F32), ((3 * R, H), F32)],
        [pltpu.VMEM((WIDTH, 3 * H), BF16), pltpu.SemaphoreType.DMA((5,))],
        after=(up_other,),
    )

    def parts_of(ref):
        return tuple(ref[pl.ds(part * R, R), :] for part in range(3))

    def put_parts(ref, values):
        for part in range(3):
            ref[pl.ds(part * R, R), :] = values[part]

    def scan_rounds(first_total, empty, join):
        total, so_far = first_total, None
        for bit in range(bits_of(C)):
            other = swap(total, "ctx", 1 << bit)
            last = bit + 1 == bits_of(C)

            def join_round(idx, ld, total, other, *refs):
                if so_far is None:
                    before = empty()
                else:
                    before, refs = parts_of(refs[0]), refs[1:]
                new_total, new_before = join(
                    idx, ld, bit, parts_of(total), parts_of(other), before
                )
                put_parts(refs[0], new_before)
                if not last:
                    put_parts(refs[1], new_total)

            inputs = [idx, fading, total, other] + ([] if so_far is None else [so_far])
            so_far, *rest = launch(
                join_round, "s" + "v" * (len(inputs) - 1), inputs, [((3 * R, H), F32)] * (2 - last)
            )
            total = None if last else rest[0]
        return so_far

    def no_state():
        zero = jnp.zeros((R, H), F32)
        return (zero, zero, zero + lowest)

    def join_states(idx, ld, bit, total, other, before):
        up = (idx[1] >> bit) & 1 == 1
        rate = jnp.exp(ld[...])
        span = rate * float(L << bit)
        passed = (L * (idx[1] & ((1 << bit) - 1))).astype(F32)
        with_other = combine(other, before, rate * passed)
        as_later, as_earlier = combine(other, total, span), combine(total, other, span)
        return (
            tuple(jnp.where(up, a, b) for a, b in zip(as_later, as_earlier)),
            tuple(jnp.where(up, a, b) for a, b in zip(with_other, before)),
        )

    entering = scan_rounds(closing, no_state, join_states)

    hidden_turn = gather_turn(hold(hidden_first, entering), 1)
    hidden_across = gather_cross(hidden_turn)
    hidden_pieces = [hidden_matrix, *hidden_first, *hidden_across]

    def sweep(key, value, opened, ld, un, states, enter, gated, out, starts, saved=None):
        rate = jnp.exp(ld[...])
        reward = un[...]
        state = tuple(enter[pl.ds(part * R, R), :] for part in range(3))
        for i in range(CHUNKS):
            for part in range(3):
                put(starts, chunk_rows(part, i), state[part])
            state = combine(
                state, tuple(get(states, chunk_rows(part, i)) for part in range(3)), ST * rate
            )

        def step(t, carry):
            new = []
            for r in range(R):
                num, den, high = carry[r]
                k_now, v_now = get(key, step_rows(r, t)), get(value, step_rows(r, t))
                at = scan_rows(r, t)
                now = reward + k_now
                top = jnp.maximum(high, now)
                e_old, e_new = jnp.exp(high - top), jnp.exp(now - top)
                inverse = 1.0 / (e_old * den + e_new)
                e_old, e_new = e_old * inverse, e_new * inverse
                put(out, step_rows(r, t), e_old * num + e_new * v_now)
                if saved:
                    part_old, part_new, keep, fresh, nums, dens, fade = saved
                    part_old[at, :] = e_old
                    part_new[at, :] = e_new
                    nums[at, :] = num
                    dens[at, :] = den
                faded = high - rate
                peak = jnp.maximum(faded, k_now)
                a, b = jnp.exp(faded - peak), jnp.exp(k_now - peak)
                if saved:
                    keep[at, :] = a
                    fresh[at, :] = b
                new.append((a * num + b * v_now, a * den + b, peak))
            return tuple(new)

        begin_at = tuple(
            tuple(get(starts, pl.ds((part * R + r) * CHUNKS, CHUNKS)) for part in range(3))
            for r in range(R)
        )
        ends = lax.fori_loop(0, ST, step, begin_at)
        if saved:
            for r in range(R):
                put(
                    saved[-1],
                    pl.ds(r * CHUNKS, CHUNKS),
                    jnp.exp(begin_at[r][2] - ST * rate - ends[r][2]),
                )
        gated[...] = (opened[...] * get(out, EVERY)).astype(BF16)

    def sweep_time(
        idx, key, value, opened, ld, un, states, enter, p0, p1, p2, p3, p4,
        e0, e1, e2, e3, gated, out, starts, w, sems,
    ):
        copies = place_rows(idx, [p0, p1, p2, p3, p4], w, sems, 3 * H, 4 * H)
        begin(copies)
        sweep(key, value, opened, ld, un, states, enter, gated, out, starts)
        finish(copies)
        for p, part in enumerate((e0, e1, e2, e3)):
            part[...] = dot_t(gated[...], w[p * SR : (p + 1) * SR, :])

    emitted = launch(
        sweep_time,
        "s" + "v" * 7 + "h" * 5,
        (idx, key, value, opened, fading, bonus, states, entering, *time_pieces),
        [((T, SR), F32)] * S,
        [
            pltpu.VMEM((T, H), BF16),
            pltpu.VMEM((G, T, 128), F32),
            pltpu.VMEM((G, 3 * R * CHUNKS, 128), F32),
            pltpu.VMEM((WIDTH, H), BF16),
            pltpu.SemaphoreType.DMA((5,)),
        ],
        after=hidden_turn,
    )
    emitted_other = swap_parts(emitted)

    def middle_norm(xo, xp, *refs):
        mine, theirs, (middle, hat, root, last) = refs[:S], refs[S : 2 * S], refs[2 * S :]
        for r in range(R):

            def tile(i, carry):
                at = rows_at(r, i)
                values = jnp.concatenate([xo[at, :], xp[at, :]], axis=1).astype(F32)
                values = values + (columns(mine, at) + columns(theirs, at))
                n, q = norm(values)
                middle[at, :] = values[:, :H]
                hat[at, :] = n
                root[at, :] = q
                return n[TB - 1 : TB, :]

            last[r : r + 1, :] = lax.fori_loop(0, NT, tile, jnp.zeros((1, WIDTH), F32))

    middle, hat_two, root_two, hat_last = launch(
        middle_norm,
        "vv" + "v" * (2 * S),
        (x_own, x_other, *emitted, *emitted_other),
        [((T, H), F32), ((T, WIDTH), F32), ((T, 1), F32), ((R, WIDTH), F32)],
        after=return_turn_in,
    )
    hat_edge_two = along_ctx(hat_last, 1, False)
    NF = FH + H
    NB = min(512, FH)

    def channel_forward(
        idx, hat, edge, po, pp, h0, h1, h2, h3, h4,
        ckey, cgate, diff, hat_low, active, squared, opened, wh, sems_h,
    ):
        copies_h = place_rows(idx, [h0, h1, h2, h3, h4], wh, sems_h)
        begin(copies_h)
        gain, bias = both(po, pp, 5), both(po, pp, 6)
        shares = [both(po, pp, i) for i in (7, 8)]
        flag = jnp.where(idx[1] > 0, 1.0, 0.0).astype(F32)
        first = (edge[...] * gain + bias) * flag
        for r in range(R):

            def tile(i, last):
                at = rows_at(r, i)
                n = hat[at, :]
                hat_low[at, :] = n.astype(BF16)
                normed = n * gain + bias
                prev = shift_down(normed, last)
                diff[at, :] = (normed - prev).astype(BF16)
                for share, target in zip(shares, (ckey, cgate)):
                    target[at, :] = (normed * share + prev * (1.0 - share)).astype(BF16)
                return normed[TB - 1 : TB, :]

            lax.fori_loop(0, NT, tile, first[r : r + 1, :])
        finish(copies_h)
        for n in range(0, FH, NB):
            pre = jnp.maximum(dot(ckey[...], wh[:, n : n + NB]), 0.0)
            active[:, n : n + NB] = pre.astype(BF16)
            squared[:, n : n + NB] = (pre * pre).astype(BF16)
        opened[...] = jax.nn.sigmoid(dot(cgate[...], wh[:, FH:NF]))

    channel_key, channel_gate, diff_two, hat_two, active, squared, filter_open = launch(
        channel_forward,
        "svvvv" + "h" * 5,
        (idx, hat_two, hat_edge_two, params, params_other, *hidden_pieces),
        [((T, WIDTH), BF16)] * 4 + [((T, FH), BF16)] * 2 + [((T, H), F32)],
        [pltpu.VMEM((WIDTH, NF), BF16), pltpu.SemaphoreType.DMA((5,))],
    )

    def channel_return(idx, squared, r0, r1, r2, r3, r4, *rest):
        parts, (wr, sems_r) = rest[:S], rest[S:]
        copies_r = place_blocks(idx, [r0, r1, r2, r3, r4], wr, sems_r)
        begin(copies_r)
        finish(copies_r)
        for p in range(S):
            parts[p][...] = dot(squared[...], wr[p])

    returned = launch(
        channel_return,
        "sv" + "h" * 5,
        (idx, squared, *return_pieces),
        [((T, SR), F32)] * S,
        [pltpu.VMEM((S, FH, SR), BF16), pltpu.SemaphoreType.DMA((5,))],
    )
    ret_keep = returned[: S // 2]
    ret_other = [swap(part, "tp", 1) for part in returned[S // 2 :]]

    def live_rows(idx, r, i):
        at = lax.broadcasted_iota(jnp.int32, (TB, 1), 0) + (idx[1] * L + i * TB)
        return jnp.where(at < idx[3 + r], 1.0, 0.0).astype(F32)

    def close_block(idx, m0, m1, t0, t1, opened, middle, up, out, grad_ret, grad_fil):
        for r in range(R):

            def tile(i, carry):
                at = rows_at(r, i)
                live = live_rows(idx, r, i)
                returned = columns((m0, m1), at) + columns((t0, t1), at)
                s = opened[at, :]
                out[at, :] = (live * (middle[at, :] + s * returned)).astype(BF16)
                grad = live * up[at, :].astype(F32)
                grad_ret[at, :] = (grad * s).astype(BF16)
                grad_fil[at, :] = (grad * returned * s * (1.0 - s)).astype(BF16)
                return carry

            lax.fori_loop(0, NT, tile, 0)

    block_out, grad_returned, grad_filter = launch(
        close_block,
        "svvvvvvv",
        (idx, *ret_keep, *ret_other, filter_open, middle, up_own),
        [((T, H), BF16), ((T, H), BF16), ((T, H), BF16)],
    )
    grad_returned_other = swap(grad_returned, "tp", 1)

    order = []
    for spot in range(BLOCKS):
        high, low = spot // C, spot % C
        turned = 0
        for bit in range(bits_of(C)):
            turned = turned * 2 + ((low >> bit) & 1)
        order.append(high * C + turned)

    VR = 16

    def weight_grads(lefts, rights, jobs, after=(), riders=()):
        count_left = [len(group) for group in lefts]
        flat = [ref for group in lefts for ref in group]
        width = sum(job[3] for job in jobs if job[4] == 0)
        half, quarter = WIDTH // 2, WIDTH // 4

        def weight_products(idx, *refs):
            left_refs, refs = list(refs[: len(flat)]), refs[len(flat) :]
            right_refs, refs = refs[: len(rights)], refs[len(rights) :]
            rider_refs, refs = refs[: len(riders)], refs[len(riders) :]
            send_a, keep_a, send_b, keep_b, *mine, tall, turned = refs
            if riders:
                one, two, other, own = rider_refs
                total = mine[0]
                total[...] = jnp.zeros((VR, H), F32)
                total[0:5, :] = one[:, :H] + other[0:5, :]
                total[5:9, :] = two[:, :H] + other[5:9, :]
                total[9:11, :] = own[...]
                total[...] = write_pair(send_a, half, total[...])
            for g, count in enumerate(count_left):
                group, left_refs = left_refs[:count], left_refs[count:]
                row = 0
                for ref in group:
                    for lane in range(0, ref.shape[1], 128):
                        tall[row : row + 128, :] = ref[:, lane : lane + 128].astype(F32).T
                        row += 128
                for spot in range(BLOCKS):
                    block = order[spot] ^ idx[2]
                    turned[spot * BR : (spot + 1) * BR, :] = tall[
                        pl.ds(pl.multiple_of(block * BR, BR), BR), :
                    ].astype(BF16)
                for left, right, start, size, part, at in jobs:
                    if left != g:
                        continue
                    for n in range(0, size, 256):
                        to = slice(at + n, at + n + 256)
                        acc = dot(
                            turned[...], right_refs[right][:, start + n : start + n + 256]
                        ).astype(BF16)
                        if part == 0:
                            keep_a[:quarter, to] = acc[:quarter]
                            send_a[:quarter, to] = acc[quarter:half]
                            keep_a[quarter:, to] = acc[half : half + quarter]
                            send_a[quarter:half, to] = acc[half + quarter :]
                        else:
                            keep_b[:, to] = acc[:half]
                            send_b[:, to] = acc[half:]

        extra = VR if riders else 0
        return launch(
            weight_products,
            "s" + "v" * (len(flat) + len(rights) + len(riders)),
            (idx, *flat, *rights, *riders),
            [((half + extra, width), BF16)]
            + [((half, width), BF16)] * 3
            + ([((VR, H), F32)] if riders else []),
            [pltpu.VMEM((WIDTH, T), F32), pltpu.VMEM((WIDTH, T), BF16)],
            after=after,
        )

    def write_pair(ref, row, values):
        high = values.astype(BF16)
        low = (values - high.astype(F32)).astype(BF16)
        ref[row:, :H] = high
        ref[row:, H : 2 * H] = low
        if ref.shape[1] > 2 * H:
            ref[row:, 2 * H :] = jnp.zeros((VR, ref.shape[1] - 2 * H), BF16)
        return high.astype(F32) + low.astype(F32)

    def read_pair(ref, row):
        return ref[row:, :H].astype(F32) + ref[row:, H : 2 * H].astype(F32)

    def add(mine, theirs):
        return mine.astype(F32) + theirs.astype(F32)

    def square_start(send_a, keep_a, send_b, keep_b, *mine):
        return [keep_a, swap(send_a, "shard", 1), keep_b, swap(send_b, "shard", 2), *mine]

    def square_turn(state):
        rows, width = state[0].shape
        half = rows // 2
        extra = VR if len(state) > 4 else 0

        def turn_square(keep_a, got_a, keep_b, got_b, *refs):
            if extra:
                mine, refs = refs[0], refs[1:]
            send_a, new_a, send_b, new_b, *total = refs
            low, high = slice(0, half), slice(half, rows)
            new_a[...] = add(keep_a[low, :], got_a[low, :]).astype(BF16)
            send_a[:half, :] = add(keep_a[high, :], got_a[high, :]).astype(BF16)
            new_b[...] = add(keep_b[low, :], got_b[low, :]).astype(BF16)
            send_b[...] = add(keep_b[high, :], got_b[high, :]).astype(BF16)
            if extra:
                total[0][...] = write_pair(send_a, half, mine[...] + read_pair(got_a, rows))

        return launch(
            turn_square,
            "v" * len(state),
            state,
            [((half + extra, width), BF16)]
            + [((half, width), BF16)] * 3
            + ([((VR, H), F32)] if extra else []),
        )

    def square_cross(send_a, keep_a, send_b, keep_b, *mine):
        return [keep_a, swap(send_a, "shard", 2), keep_b, swap(send_b, "shard", 1), *mine]

    def square_end(state):
        rows, width = state[0].shape
        half = rows // 2
        extra = VR if len(state) > 4 else 0

        def end_square(keep_a, got_a, keep_b, got_b, *refs):
            if extra:
                mine, refs = refs[0], refs[1:]
            send, new, *total = refs
            for part, (keep, got) in enumerate(((keep_a, got_a), (keep_b, got_b))):
                at = slice(part * width, (part + 1) * width)
                new[:, at] = add(keep[:half, :], got[:half, :]).astype(BF16)
                send[:half, at] = add(keep[half:, :], got[half:rows, :]).astype(BF16)
            if extra:
                total[0][...] = write_pair(send, half, mine[...] + read_pair(got_a, rows))

        return launch(
            end_square,
            "v" * len(state),
            state,
            [((half + extra, 2 * width), BF16), ((half, 2 * width), BF16)]
            + ([((VR, H), F32)] if extra else []),
        )

    def scatter_line(send, keep, *mine, seen=None):
        extra = VR if mine else 0
        for bit in range(bits_of(C)):
            got = swap(send, "ctx", 1 << bit)
            if seen is not None:
                seen.append(got)
            rows, width = keep.shape
            last = bit + 1 == bits_of(C)
            half = rows if last else rows // 2

            def turn_line(keep, got, *refs):
                if extra:
                    own, refs = refs[0], refs[1:]
                new, *refs = refs
                if last:
                    new[...] = add(keep[...], got[:rows, :])
                else:
                    send = refs.pop(0)
                    new[...] = add(keep[:half, :], got[:half, :]).astype(BF16)
                    send[:half, :] = add(keep[half:, :], got[half:rows, :]).astype(BF16)
                if extra:
                    total = own[...] + read_pair(got, rows)
                    refs[0][...] = total if last else write_pair(send, half, total)

            outs = [((half, width), F32 if last else BF16)]
            if not last:
                outs.append(((half + extra, width), BF16))
            if extra:
                outs.append(((VR, H), F32))
            result = launch(turn_line, "v" * (2 + len(mine)), (keep, got, *mine), outs)
            keep, result = result[0], result[1:]
            if not last:
                send, result = result[0], result[1:]
            mine = tuple(result)
        return (keep, *mine)

    return_parts = weight_grads(
        [[grad_returned, grad_returned_other]],
        [squared],
        [(0, 0, 0, FH // 2, 0, 0), (0, 0, FH // 2, FH // 2, 1, 0)],
    )
    return_state = square_start(*return_parts)

    def channel_backward(
        idx, gro, grp, gf, active, diff, hat, edge, po, pp,
        h0, h1, h2, h3, h4, r0, r1, r2, r3, r4,
        grad_hidden, n0, n1, n2, n3, first_out, sums, wh, wr, ckey, cgate, sems_h, sems_r,
    ):
        copies_h = place_rows(idx, [h0, h1, h2, h3, h4], wh, sems_h)
        copies_r = place_blocks(idx, [r0, r1, r2, r3, r4], wr, sems_r)
        begin(copies_r)
        begin(copies_h)
        finish(copies_r)
        half = S // 2
        for n in range(0, FH, NB):
            acc = None
            for p in range(S):
                source = gro if p < half else grp
                at = (p % half) * SR
                term = dot_t(source[:, at : at + SR], wr[p, n : n + NB, :])
                acc = term if acc is None else acc + term
            grad_hidden[:, n : n + NB] = (
                acc * 2.0 * active[:, n : n + NB].astype(F32)
            ).astype(BF16)
        finish(copies_h)
        for p in range(S):
            at = slice(p * SR, (p + 1) * SR)
            ckey[:, at] = dot_t(grad_hidden[...], wh[at, :FH])
            cgate[:, at] = dot_t(gf[...], wh[at, FH:NF])
        share_k, share_g = both(po, pp, 7), both(po, pp, 8)
        flag = jnp.where(idx[1] > 0, 1.0, 0.0).astype(F32)
        zero = jnp.zeros((1, WIDTH), F32)
        totals = (zero, zero, zero, zero)
        for r in range(R):

            def tile(j, carry):
                after, gain_sum, bias_sum, key_sum, gate_sum = carry
                at = rows_at(r, NT - 1 - j)
                gk, gg, d = ckey[at, :], cgate[at, :], diff[at, :].astype(F32)
                now = gk * share_k + gg * share_g
                back = gk * (1.0 - share_k) + gg * (1.0 - share_g)
                grad = now + shift_up(back, after)
                for p, part in enumerate((n0, n1, n2, n3)):
                    part[at, :] = grad[:, p * SR : (p + 1) * SR]
                return (
                    back[0:1, :],
                    gain_sum + jnp.sum(grad * hat[at, :].astype(F32), axis=0, keepdims=True),
                    bias_sum + jnp.sum(grad, axis=0, keepdims=True),
                    key_sum + jnp.sum(gk * d, axis=0, keepdims=True),
                    gate_sum + jnp.sum(gg * d, axis=0, keepdims=True),
                )

            front, *totals = lax.fori_loop(0, NT, tile, (zero, *totals))
            first_out[r : r + 1, :] = front
            totals[0] = totals[0] + front * (edge[r : r + 1, :] * flag)
            totals[1] = totals[1] + front * flag
        for i in range(4):
            sums[i : i + 1, :] = totals[i]

    grad_hidden, *grad_two, first_two, sums_two = launch(
        channel_backward,
        "s" + "v" * 9 + "h" * 10,
        (
            idx,
            grad_returned,
            grad_returned_other,
            grad_filter,
            active,
            diff_two,
            hat_two,
            hat_edge_two,
            params,
            params_other,
            *hidden_pieces,
            *return_pieces,
        ),
        [((T, FH), BF16)]
        + [((T, SR), F32)] * S
        + [((R, WIDTH), F32), ((4, WIDTH), F32)],
        [
            pltpu.VMEM((WIDTH, NF), BF16),
            pltpu.VMEM((S, FH, SR), BF16),
            pltpu.VMEM((T, WIDTH), F32),
            pltpu.VMEM((T, WIDTH), F32),
            pltpu.SemaphoreType.DMA((5,)),
            pltpu.SemaphoreType.DMA((5,)),
        ],
        after=(return_parts[0],),
    )
    grad_two, first_two, return_state = lax.optimization_barrier(
        (grad_two, first_two, return_state)
    )
    grad_two_other = swap_parts(grad_two)
    first_two_own = along_ctx(first_two, -1, False)
    first_two_other = along_ctx(first_two, -1, True)

    def sweep_again(*refs):
        inputs, (gated, out, *saved, starts) = refs[:7], refs[7:]
        sweep(*inputs, gated, out, starts, saved)

    gated, mixed_out, part_old, part_new, keep, fresh, nums, dens, fade = launch(
        sweep_again,
        "v" * 7,
        (key, value, opened, fading, bonus, states, hold(entering, grad_returned_other)),
        [((T, H), BF16), ((G, T, 128), F32)]
        + [((T, H), F32)] * 6
        + [((G, R * CHUNKS, 128), F32)],
        [pltpu.VMEM((G, 3 * R * CHUNKS, 128), F32)],
    )

    mixed_key, mixed_value, mixed_gate, hat_one, diff_one, root_one, _ = mixes(
        *hold((x_own, x_other), grad_returned_other)
    )

    part = NF // 2
    hidden_parts = weight_grads(
        [[channel_key], [channel_gate]],
        [grad_hidden, grad_filter],
        [
            (0, 0, 0, part, 0, 0),
            (0, 0, part, FH - part, 1, 0),
            (1, 1, 0, H, 1, FH - part),
        ],
        after=(gated, root_one),
    )
    hidden_state = square_start(*hidden_parts)
    return_turn = square_turn(return_state)
    return_cross = square_cross(*return_turn)

    def middle_backward(
        idx, m0, m1, m2, m3, t0, t1, t2, t3, e_own, e_other, hat, root, po, pp, uo, upp, opened, out,
        part_old, keep, fade, p0, p1, p2, p3, p4,
        grad_mid, grad_own, grad_res, grad_gate, adjoint, entry, w, gates, sems,
    ):
        copies = place_rows(idx, [p0, p1, p2, p3, p4], w, sems, 3 * H, 4 * H)
        begin(copies)
        gain = both(po, pp, 5)
        tail = e_own[...] + swapped(e_other[...])
        row = lax.broadcasted_iota(jnp.int32, (TB, 1), 0)
        for r in range(R):

            def tile(i, carry):
                at = rows_at(r, i)
                is_last = jnp.where((row == TB - 1) & (i == NT - 1), 1.0, 0.0).astype(F32)
                grad = columns((m0, m1, m2, m3), at) + columns((t0, t1, t2, t3), at)
                grad = grad + is_last * tail[r : r + 1, :]
                n = hat[at, :].astype(F32)
                scaled = grad * gain
                mean_one = jnp.sum(scaled, axis=-1, keepdims=True) * (1.0 / WIDTH)
                mean_two = jnp.sum(scaled * n, axis=-1, keepdims=True) * (1.0 / WIDTH)
                up = jnp.concatenate([uo[at, :], upp[at, :]], axis=1).astype(F32)
                full = live_rows(idx, r, i) * up + root[at, :] * (scaled - mean_one - n * mean_two)
                grad_mid[at, :] = full.astype(BF16)
                grad_own[at, :] = full[:, :H]
                return carry

            lax.fori_loop(0, NT, tile, 0)
        finish(copies)
        gates[...] = dot(grad_mid[...], w[...])
        for r in range(R):

            def gate_tile(i, carry):
                at = rows_at(r, i)
                g, s = gates[at, :], opened[at, :]
                put(grad_res, at, g * s)
                grad_gate[at, :] = (g * get(out, at) * s * (1.0 - s)).astype(BF16)
                return carry

            lax.fori_loop(0, NT, gate_tile, 0)

        def step(j, carry):
            t = ST - 1 - j
            new = []
            for r in range(R):
                alpha, beta = carry[r]
                at = scan_rows(r, t)
                direct = part_old[at, :] * get(grad_res, step_rows(r, t))
                a = keep[at, :]
                new.append(
                    (direct + a * alpha, a * beta - direct * get(out, step_rows(r, t)))
                )
            return tuple(new)

        zero = jnp.zeros((CHUNKS, H), F32)
        ends = lax.fori_loop(0, ST, step, ((zero, zero),) * R)
        for r in range(R):
            for k in range(2):
                put(adjoint, pl.ds((k * R + r) * CHUNKS, CHUNKS), ends[r][k])
        alpha = beta = jnp.zeros((R, H), F32)
        span = jnp.ones((R, H), F32)
        for i in range(CHUNKS - 1, -1, -1):
            f = get(fade, chunk_rows(0, i))
            alpha = get(adjoint, chunk_rows(0, i)) + f * alpha
            beta = get(adjoint, chunk_rows(1, i)) + f * beta
            span = span * f
        entry[pl.ds(0, R), :] = alpha
        entry[pl.ds(R, R), :] = beta
        entry[pl.ds(2 * R, R), :] = span

    grad_mid, grad_mid_own, grad_res, grad_gate, adjoint, entry = launch(
        middle_backward,
        "s" + "v" * 21 + "h" * 5,
        (
            idx,
            *grad_two,
            *grad_two_other,
            first_two_own,
            first_two_other,
            hat_two,
            root_two,
            params,
            params_other,
            up_own,
            up_other,
            opened,
            mixed_out,
            part_old,
            keep,
            fade,
            *time_pieces,
        ),
        [
            ((T, WIDTH), BF16),
            ((T, H), F32),
            ((G, T, 128), F32),
            ((T, H), BF16),
            ((G, 2 * R * CHUNKS, 128), F32),
            ((3 * R, H), F32),
        ],
        [
            pltpu.VMEM((WIDTH, H), BF16),
            pltpu.VMEM((T, H), F32),
            pltpu.SemaphoreType.DMA((5,)),
        ],
        after=(hidden_parts[1],),
    )

    def no_adjoint():
        zero = jnp.zeros((R, H), F32)
        return (zero, zero, zero + 1.0)

    def join_adjoints(idx, ld, bit, total, other, before):
        low = (idx[1] >> bit) & 1 == 0

        def follow(near, far):
            return (near[0] + near[2] * far[0], near[1] + near[2] * far[1], near[2] * far[2])

        as_near, as_far, with_other = follow(total, other), follow(other, total), follow(before, other)
        return (
            tuple(jnp.where(low, a, b) for a, b in zip(as_near, as_far)),
            tuple(jnp.where(low, a, b) for a, b in zip(with_other, before)),
        )

    late = scan_rounds(entry, no_adjoint, join_adjoints)

    def time_backward(
        idx, res, out, value, part_old, part_new, keep, fresh, nums, dens, fade, adjoint, late,
        ld, gate, diff, hat, edge, po, pp, p0, p1, p2, p3, p4,
        grad_key, grad_value, mine_own, s0, s1, stats, first_out, sums, sums_own,
        w, dk, dv, gk, gv, gg, starts, sems,
    ):
        copies = place_rows(idx, [p0, p1, p2, p3, p4], w, sems, 0, 3 * H)
        begin(copies)
        late_now = (late[pl.ds(0, R), :], late[pl.ds(R, R), :])
        for i in range(CHUNKS - 1, -1, -1):
            for k in range(2):
                put(starts, chunk_rows(k, i), late_now[k])
            f = get(fade, chunk_rows(0, i))
            late_now = tuple(get(adjoint, chunk_rows(k, i)) + f * late_now[k] for k in range(2))

        def step(j, carry):
            t = ST - 1 - j
            adj, fade_sum, bonus_sum = carry
            new = []
            for r in range(R):
                alpha, beta = adj[r]
                at, spread = scan_rows(r, t), step_rows(r, t)
                g, y, v = get(res, spread), get(out, spread), get(value, spread)
                b, a = fresh[at, :], keep[at, :]
                near = part_new[at, :] * g
                lift = near * (v - y)
                put(dv, spread, b * alpha + near)
                put(dk, spread, b * (v * alpha + beta) + lift)
                bonus_sum = bonus_sum + lift
                fade_sum = fade_sum - a * (nums[at, :] * alpha + dens[at, :] * beta)
                direct = part_old[at, :] * g
                new.append((direct + a * alpha, a * beta - direct * y))
            return (tuple(new), fade_sum, bonus_sum)

        first_adj = tuple(
            tuple(get(starts, pl.ds((k * R + r) * CHUNKS, CHUNKS)) for k in range(2))
            for r in range(R)
        )
        zero = jnp.zeros((CHUNKS, H), F32)
        _, fade_sum, bonus_sum = lax.fori_loop(0, ST, step, (first_adj, zero, zero))
        sums_own[0:1, :] = jnp.sum(fade_sum, axis=0, keepdims=True) * jnp.exp(ld[...])
        sums_own[1:2, :] = jnp.sum(bonus_sum, axis=0, keepdims=True)
        grad_key[...] = get(dk, EVERY).astype(BF16)
        grad_value[...] = get(dv, EVERY).astype(BF16)
        finish(copies)
        gk[...] = dot_t(grad_key[...], w[:, :H])
        gv[...] = dot_t(grad_value[...], w[:, H : 2 * H])
        gg[...] = dot_t(gate[...], w[:, 2 * H : 3 * H])
        gain = both(po, pp, 0)
        shares = [both(po, pp, i) for i in (2, 3, 4)]
        flag = jnp.where(idx[1] > 0, 1.0, 0.0).astype(F32)
        zero = jnp.zeros((1, WIDTH), F32)
        totals = (zero,) * 5
        lane = lax.broadcasted_iota(jnp.int32, (TB, 128), 1)
        for r in range(R):

            def tile(j, carry):
                after, gain_sum, bias_sum, *mix_sums = carry
                at = rows_at(r, NT - 1 - j)
                grads = (gk[at, :], gv[at, :], gg[at, :])
                d, n = diff[at, :].astype(F32), hat[at, :].astype(F32)
                now = back = None
                for share, grad in zip(shares, grads):
                    a, b = grad * share, grad * (1.0 - share)
                    now = a if now is None else now + a
                    back = b if back is None else back + b
                grad = now + shift_up(back, after)
                mine_own[at, :] = grad[:, :H]
                s0[at, :] = grad[:, H : H + SR]
                s1[at, :] = grad[:, H + SR :]
                scaled = grad * gain
                one = jnp.sum(scaled, axis=-1, keepdims=True)
                two = jnp.sum(scaled * n, axis=-1, keepdims=True)
                stats[at, :] = jnp.where(lane == 0, one, jnp.where(lane == 1, two, 0.0))
                return (
                    back[0:1, :],
                    gain_sum + jnp.sum(grad * n, axis=0, keepdims=True),
                    bias_sum + jnp.sum(grad, axis=0, keepdims=True),
                    *(
                        total + jnp.sum(one_grad * d, axis=0, keepdims=True)
                        for total, one_grad in zip(mix_sums, grads)
                    ),
                )

            front, *totals = lax.fori_loop(0, NT, tile, (zero, *totals))
            first_out[r : r + 1, :] = front
            totals[0] = totals[0] + front * edge[r : r + 1, :]
            totals[1] = totals[1] + front * flag
        for i in range(5):
            sums[i : i + 1, :] = totals[i]

    hidden_turn_out = square_turn(hidden_state)
    hidden_cross = square_cross(*hidden_turn_out)
    grad_key, grad_value, one_own, *one_send, first_one, sums_one, sums_own = launch(
        time_backward,
        "s" + "v" * 19 + "h" * 5,
        (
            idx,
            grad_res,
            mixed_out,
            value,
            part_old,
            part_new,
            keep,
            fresh,
            nums,
            dens,
            fade,
            adjoint,
            late,
            fading,
            grad_gate,
            diff_one,
            hat_one,
            hat_edge_one,
            params,
            params_other,
            *time_pieces,
        ),
        [
            ((T, H), BF16),
            ((T, H), BF16),
            ((T, H), F32),
            ((T, SR), F32),
            ((T, SR), F32),
            ((T, 128), F32),
            ((R, WIDTH), F32),
            ((5, WIDTH), F32),
            ((2, H), F32),
        ],
        [pltpu.VMEM((WIDTH, 3 * H), BF16)]
        + [pltpu.VMEM((G, T, 128), F32)] * 2
        + [pltpu.VMEM((T, WIDTH), F32)] * 3
        + [pltpu.VMEM((G, 2 * R * CHUNKS, 128), F32), pltpu.SemaphoreType.DMA((5,))],
        after=(hidden_turn_out[0], hidden_turn_out[2]),
    )
    one_other = [swap(part, "tp", 1) for part in one_send]
    first_one_own = along_ctx(first_one, -1, False)
    first_one_other = along_ctx(first_one, -1, True)

    sums_other = swap(jnp.concatenate([sums_one[:, H:], sums_two[:, H:]], axis=0), "tp", 1)
    late_parts = weight_grads(
        [[grad_mid], [mixed_gate], [mixed_key], [mixed_value]],
        [gated, grad_gate, grad_key, grad_value],
        [(0, 0, 0, H, 0, 0), (1, 1, 0, H, 0, H), (2, 2, 0, H, 1, 0), (3, 3, 0, H, 1, H)],
        after=(
            return_cross[1],
            return_cross[3],
            first_one_own,
            first_one_other,
            *one_other,
        ),
        riders=(sums_one, sums_two, sums_other, sums_own),
    )
    late_state = square_start(*late_parts)

    return_seen = []
    (return_w,) = scatter_line(*square_end(hold(return_cross, first_one_other)), seen=return_seen)

    def input_backward(
        mine, sent, t0, t1, theirs, e_own, e_other, hat, root, po, pp, gm, out
    ):
        gain_full = both(po, pp, 0)
        tail = e_own[...] + swapped(e_other[...])
        row = lax.broadcasted_iota(jnp.int32, (TB, 1), 0)
        for r in range(R):
            weighted = tail[r : r + 1, :] * gain_full
            tail_one = jnp.sum(weighted, axis=-1, keepdims=True)
            tail_two = jnp.sum(
                weighted * hat[(r + 1) * L - TB : (r + 1) * L, :].astype(F32)[TB - 1 :],
                axis=-1,
                keepdims=True,
            )

            def tile(i, carry):
                at = rows_at(r, i)
                is_last = jnp.where((row == TB - 1) & (i == NT - 1), 1.0, 0.0).astype(F32)
                grad = mine[at, :] + columns((t0, t1), at) + is_last * tail[r : r + 1, :H]
                stats = sent[at, :] + theirs[at, :]
                mean_one = (stats[:, 0:1] + is_last * tail_one) * (1.0 / WIDTH)
                mean_two = (stats[:, 1:2] + is_last * tail_two) * (1.0 / WIDTH)
                scaled = grad * gain_full[:, :H]
                out[at, :] = gm[at, :] + root[at, :] * (
                    scaled - mean_one - hat[at, :H].astype(F32) * mean_two
                )
                return carry

            lax.fori_loop(0, NT, tile, 0)

    (input_grad,) = launch(
        input_backward,
        "v" * 12,
        (
            one_own,
            one_send[2],
            *one_other,
            first_one_own,
            first_one_other,
            hat_one,
            root_one,
            params,
            params_other,
            grad_mid_own,
        ),
        [((T, H), F32)],
        after=(late_parts[1], return_seen[0]),
    )
    hidden_seen = []
    (hidden_w,) = scatter_line(*square_end(hold(hidden_cross, late_parts[1])), seen=hidden_seen)
    late_cross = square_cross(*square_turn(hold(late_state, hidden_seen[0], return_seen[-1])))
    late_w, vectors = scatter_line(*square_end(hold(late_cross, input_grad)))
    shape = block_entries.shape
    return (
        block_out.reshape(shape),
        input_grad.reshape(shape),
        vectors[0],
        vectors[1],
        vectors[2],
        vectors[3],
        vectors[4],
        vectors[9],
        vectors[10],
        late_w[:, H : 2 * H],
        late_w[:, 2 * H : 3 * H],
        late_w[:, 3 * H :],
        late_w[:, :H].T,
        vectors[5],
        vectors[6],
        vectors[7],
        vectors[8],
        hidden_w[:, :FH],
        hidden_w[:, FH:],
        return_w.T,
    )


def solution(mesh):
    token = P(None, "shard", "ctx", "tp")
    feature = P("tp")
    rows = P("shard", "tp")
    cols = P("tp", "shard")
    rows_out = P(("shard", "ctx"), "tp")
    cols_out = P("tp", ("shard", "ctx"))
    return jax.shard_map(
        per_device,
        mesh=mesh,
        in_specs=(
            (token, P(None, "shard"), token)
            + (feature,) * 7
            + (rows, rows, rows, cols)
            + (feature,) * 4
            + (rows, rows, cols)
        ),
        out_specs=(
            (token, token)
            + (feature,) * 7
            + (rows_out, rows_out, rows_out, cols_out)
            + (feature,) * 4
            + (rows_out, rows_out, cols_out)
        ),
        check_vma=False,
    )
```

```python
import jax
import jax.numpy as jnp
from jax import lax
from jax.experimental import pallas as pl
from jax.experimental.pallas import tpu as pltpu
from jax.sharding import PartitionSpec as P

F32, BF16 = jnp.float32, jnp.bfloat16
WIDTH = 1024
epsilon = 1e-05
lowest = -1e30
CHUNKS = 8
SPARE = 6 * 2**20

VMEM = pl.BlockSpec(memory_space=pltpu.VMEM)
SMEM = pl.BlockSpec(memory_space=pltpu.SMEM)
HBM = pl.BlockSpec(memory_space=pl.ANY)
KINDS = {"v": VMEM, "s": SMEM, "h": HBM}


def padded_bytes(shape, dtype):
    rows = -(-shape[-2] // 8) * 8
    lanes = -(-shape[-1] // 128) * 128
    size = rows * lanes * jnp.dtype(dtype).itemsize
    for dim in shape[:-2]:
        size *= dim
    return size


def launch(body, kinds, inputs, outs, scratch=(), after=()):
    count = len(kinds)
    room = sum(padded_bytes(x.shape, x.dtype) for x in scratch if len(x.shape) > 1) + SPARE

    def run(*refs):
        body(*refs[:count], *refs[count + len(after) :])

    return pl.pallas_call(
        run,
        out_shape=[
            jax.ShapeDtypeStruct(shape, dtype) for shape, dtype in outs
        ],
        in_specs=[KINDS[kind] for kind in kinds] + [HBM] * len(after),
        out_specs=[VMEM] * len(outs),
        scratch_shapes=list(scratch),
        name=body.__name__,
        compiler_params=pltpu.CompilerParams(vmem_limit_bytes=room),
    )(*inputs, *after)


def side_by_side(*parts):
    widths = [part.shape[1] for part in parts]

    def pack(*refs):
        sources, whole, sems = refs[: len(parts)], refs[-2], refs[-1]
        copies, at = [], 0
        for i, source in enumerate(sources):
            target = whole.at[:, pl.ds(at, widths[i])]
            copies.append(pltpu.make_async_copy(source, target, sems.at[i]))
            at += widths[i]
        begin(copies)
        finish(copies)

    (whole,) = launch(
        pack,
        "h" * len(parts),
        [pltpu.with_memory_space_constraint(part, pltpu.HBM) for part in parts],
        [((parts[0].shape[0], sum(widths)), parts[0].dtype)],
        [pltpu.SemaphoreType.DMA((len(parts),))],
    )
    return whole


def hold(values, *others):
    return lax.optimization_barrier((values, others))[0]


def bits_of(count):
    return count.bit_length() - 1


def swap(value, axis, step):
    size = lax.axis_size(axis)
    return lax.ppermute(value, axis, [(i, i ^ step) for i in range(size)])


def along_ctx(value, step, cross):
    count = lax.axis_size("ctx")
    if not cross:
        pairs = [(i, i + step) for i in range(count) if 0 <= i + step < count]
        return lax.ppermute(value, "ctx", pairs)
    pairs = []
    for i in range(count):
        if 0 <= i + step < count:
            for core in range(2):
                pairs.append((2 * i + core, 2 * (i + step) + 1 - core))
    return lax.ppermute(value, ("ctx", "tp"), pairs)


def gather_first(matrix):
    return swap(matrix, "shard", 1), swap(matrix, "shard", 2)


def gather_turn(across, cut):
    half = across[0].shape[cut] // 2
    return (
        lax.slice_in_dim(across[0], 0, half, axis=cut),
        lax.slice_in_dim(across[1], half, 2 * half, axis=cut),
    )


def gather_cross(turn):
    return swap(turn[0], "shard", 2), swap(turn[1], "shard", 1)


def place_rows(idx, pieces, whole, sems, start=0, stop=None):
    base = idx[0]
    rows, cols = pieces[0].shape
    half = cols // 2
    stop = cols if stop is None else stop

    def spot(step):
        return pl.ds(pl.multiple_of((base ^ step) * rows, rows), rows)

    copies = []
    for step in range(3):
        copies.append((pieces[step].at[:, pl.ds(start, stop - start)], whole.at[spot(step), :]))
    for i in range(2):
        low, high = max(start, i * half), min(stop, (i + 1) * half)
        if low < high:
            source = pieces[3 + i].at[:, pl.ds(low - i * half, high - low)]
            copies.append((source, whole.at[spot(3), pl.ds(low - start, high - low)]))
    return [
        pltpu.make_async_copy(source, target, sems.at[i])
        for i, (source, target) in enumerate(copies)
    ]


def place_blocks(idx, pieces, whole, sems):
    base = idx[0]
    half = pieces[0].shape[0] // 2
    targets = [
        whole.at[base],
        whole.at[base ^ 1],
        whole.at[base ^ 2],
        whole.at[base ^ 3, pl.ds(0, half), :],
        whole.at[base ^ 3, pl.ds(half, half), :],
    ]
    return [
        pltpu.make_async_copy(piece, target, sems.at[i])
        for i, (piece, target) in enumerate(zip(pieces, targets))
    ]


def begin(copies):
    for copy in copies:
        copy.start()


def finish(copies):
    for copy in copies:
        copy.wait()


def dot(left, right):
    return jnp.dot(left, right, preferred_element_type=F32)


def dot_t(left, right):
    return lax.dot_general(left, right, (((1,), (1,)), ((), ())), preferred_element_type=F32)


def norm(values):
    center = jnp.sum(values, axis=-1, keepdims=True) * (1.0 / WIDTH)
    squares = jnp.sum(values * values, axis=-1, keepdims=True) * (1.0 / WIDTH)
    root = lax.rsqrt(squares - center * center + epsilon)
    return (values - center) * root, root


def both(own, other, i):
    return jnp.concatenate([own[i : i + 1, :], other[i : i + 1, :]], axis=1)


def shift_down(values, first):
    row = lax.broadcasted_iota(jnp.int32, values.shape, 0)
    return jnp.where(row == 0, first, pltpu.roll(values, 1, 0))


def shift_up(values, last):
    count = values.shape[0]
    row = lax.broadcasted_iota(jnp.int32, values.shape, 0)
    return jnp.where(row == count - 1, last, pltpu.roll(values, count - 1, 0))


def combine(earlier, later, later_span):
    shifted = earlier[2] - later_span
    high = jnp.maximum(shifted, later[2])
    early = jnp.exp(shifted - high)
    late = jnp.exp(later[2] - high)
    return (earlier[0] * early + later[0] * late, earlier[1] * early + later[1] * late, high)


def get(ref, rows):
    return jnp.concatenate([ref[g, rows, :] for g in range(ref.shape[0])], axis=1)


def put(ref, rows, values):
    for g in range(ref.shape[0]):
        ref[g, rows, :] = values[:, g * 128 : (g + 1) * 128]


def columns(refs, rows):
    return jnp.concatenate([ref[rows, :] for ref in refs], axis=1)


def swap_parts(parts):
    half = len(parts) // 2
    got = [swap(part, "tp", 1) for part in parts]
    return got[half:] + got[:half]


def swapped(values):
    half = values.shape[1] // 2
    return jnp.concatenate([values[:, half:], values[:, :half]], axis=1)


def per_device(
    block_entries,
    row_extents,
    upstream_loss_deriv,
    earlier_layernorm_scaling,
    earlier_layernorm_offset,
    temporal_mix_lookup_fraction,
    temporal_mix_payload_fraction,
    temporal_mix_filter_fraction,
    logarithmic_fading_per_feature,
    present_entry_reward,
    filter_projection,
    lookup_projection,
    payload_projection,
    temporal_mix_emit_projection,
    later_layernorm_scaling,
    later_layernorm_offset,
    feature_mix_lookup_fraction,
    feature_mix_filter_fraction,
    feature_mix_lookup_proj,
    feature_mix_filter_proj,
    feature_mix_payload_proj,
):
    batches, rows_local, L, H = block_entries.shape
    R = batches * rows_local
    T = R * L
    S, C = lax.axis_size("shard"), lax.axis_size("ctx")
    FH = feature_mix_lookup_proj.shape[1]
    ST = L // CHUNKS
    TB = min(32, L)
    NT = L // TB
    G = H // 128
    EVERY = slice(None)
    BLOCKS = S * C
    BR = WIDTH // BLOCKS
    SR = WIDTH // S
    assert S == 4 and WIDTH == 2 * H
    s_at, c_at, t_at = lax.axis_index("shard"), lax.axis_index("ctx"), lax.axis_index("tp")
    idx = jnp.concatenate(
        [
            jnp.stack(
                [s_at ^ (2 * t_at), c_at, (s_at * C + c_at) ^ (t_at * (BLOCKS // 2))]
            ).astype(jnp.int32),
            row_extents.reshape(R).astype(jnp.int32),
        ]
    )

    def rows_at(r, i):
        return pl.ds(pl.multiple_of(r * L + i * TB, TB), TB)

    def scan_rows(r, t):
        return pl.ds(pl.multiple_of((r * ST + t) * CHUNKS, CHUNKS), CHUNKS)

    def step_rows(r, t):
        return pl.ds(r * L + t, CHUNKS, stride=ST)

    def chunk_rows(part, i):
        return pl.ds(part * R * CHUNKS + i, R, stride=CHUNKS)

    x_own = block_entries.reshape(T, H)
    up_own = upstream_loss_deriv.reshape(T, H)
    params = jnp.stack(
        [
            earlier_layernorm_scaling,
            earlier_layernorm_offset,
            temporal_mix_lookup_fraction,
            temporal_mix_payload_fraction,
            temporal_mix_filter_fraction,
            later_layernorm_scaling,
            later_layernorm_offset,
            feature_mix_lookup_fraction,
            feature_mix_filter_fraction,
        ]
    )
    fading = logarithmic_fading_per_feature.reshape(1, H)
    bonus = present_entry_reward.reshape(1, H)
    time_matrix = side_by_side(
        lookup_projection,
        payload_projection,
        filter_projection,
        temporal_mix_emit_projection.T,
    )
    time_first = gather_first(time_matrix)
    x_other = swap(x_own, "tp", 1)
    params_other = swap(params, "tp", 1)
    last_rows = [
        part.reshape(batches, rows_local, L, H)[:, :, L - 1, :].reshape(R, H)
        for part in (x_own, x_other)
    ]
    edge = along_ctx(jnp.concatenate(last_rows, axis=1), 1, False)
    up_other = swap(up_own, "tp", 1)

    def mix_time(
        idx, xo, xp, ed, po, pp, mixed_key, mixed_value, mixed_gate, hat, diff, root, hat_edge
    ):
        gain, bias = both(po, pp, 0), both(po, pp, 1)
        shares = [both(po, pp, i) for i in (2, 3, 4)]
        flag = jnp.where(idx[1] > 0, 1.0, 0.0).astype(F32)
        edge_hat, _ = norm(ed[...].astype(F32))
        hat_edge[...] = edge_hat * flag
        first = (edge_hat * gain + bias) * flag
        for r in range(R):

            def tile(i, last):
                at = rows_at(r, i)
                values = jnp.concatenate([xo[at, :], xp[at, :]], axis=1).astype(F32)
                n, q = norm(values)
                normed = n * gain + bias
                prev = shift_down(normed, last)
                hat[at, :] = n.astype(BF16)
                root[at, :] = q
                diff[at, :] = (normed - prev).astype(BF16)
                for share, target in zip(shares, (mixed_key, mixed_value, mixed_gate)):
                    target[at, :] = (normed * share + prev * (1.0 - share)).astype(BF16)
                return normed[TB - 1 : TB, :]

            lax.fori_loop(0, NT, tile, first[r : r + 1, :])

    def mixes(*tokens):
        return launch(
            mix_time,
            "svvvvv",
            (idx, *tokens, edge, params, params_other),
            [((T, WIDTH), BF16)] * 5 + [((T, 1), F32), ((R, WIDTH), F32)],
        )

    mixed_key, mixed_value, mixed_gate, *_, hat_edge_one = mixes(x_own, x_other)
    time_turn = gather_turn(hold(time_first, hat_edge_one), 1)
    time_across = gather_cross(time_turn)
    time_pieces = [time_matrix, *time_first, *time_across]
    hidden_matrix = side_by_side(feature_mix_lookup_proj, feature_mix_filter_proj)
    hidden_first = gather_first(hold(hidden_matrix, time_across))
    return_matrix = hold(feature_mix_payload_proj, time_across)
    return_first = gather_first(return_matrix)
    return_turn_in = gather_turn(return_first, 0)
    return_across = gather_cross(return_turn_in)
    return_pieces = [return_matrix, *return_first, *return_across]

    def project_time(
        idx, mk, mv, mg, ld, p0, p1, p2, p3, p4, key, value, opened, states, closing, w, sems
    ):
        copies = place_rows(idx, [p0, p1, p2, p3, p4], w, sems, 0, 3 * H)
        begin(copies)
        finish(copies)
        put(key, EVERY, dot(mk[...], w[:, :H]))
        put(value, EVERY, dot(mv[...], w[:, H : 2 * H]))
        rate = jnp.exp(ld[...])

        def step(t, carry):
            new = []
            for r in range(R):
                num, den, high = carry[r]
                k_now, v_now = get(key, step_rows(r, t)), get(value, step_rows(r, t))
                faded = high - rate
                top = jnp.maximum(faded, k_now)
                old, fresh = jnp.exp(faded - top), jnp.exp(k_now - top)
                new.append((old * num + fresh * v_now, old * den + fresh, top))
            return tuple(new)

        zero = jnp.zeros((CHUNKS, H), F32)
        ends = lax.fori_loop(0, ST, step, ((zero, zero, zero + lowest),) * R)
        for r in range(R):
            for part in range(3):
                put(states, pl.ds((part * R + r) * CHUNKS, CHUNKS), ends[r][part])
        total = tuple(get(states, chunk_rows(part, 0)) for part in range(3))
        for i in range(1, CHUNKS):
            total = combine(
                total, tuple(get(states, chunk_rows(part, i)) for part in range(3)), ST * rate
            )
        for part in range(3):
            closing[pl.ds(part * R, R), :] = total[part]
        opened[...] = jax.nn.sigmoid(dot(mg[...], w[:, 2 * H : 3 * H]))

    key, value, opened, states, closing = launch(
        project_time,
        "svvvv" + "h" * 5,
        (idx, mixed_key, mixed_value, mixed_gate, fading, *time_pieces),
        [((G, T, 128), F32)] * 2
        + [((T, H), F32), ((G, 3 * R * CHUNKS, 128), F32), ((3 * R, H), F32)],
        [pltpu.VMEM((WIDTH, 3 * H), BF16), pltpu.SemaphoreType.DMA((5,))],
        after=(up_other,),
    )

    def parts_of(ref):
        return tuple(ref[pl.ds(part * R, R), :] for part in range(3))

    def put_parts(ref, values):
        for part in range(3):
            ref[pl.ds(part * R, R), :] = values[part]

    def scan_rounds(first_total, empty, join):
        total, so_far = first_total, None
        for bit in range(bits_of(C)):
            other = swap(total, "ctx", 1 << bit)
            last = bit + 1 == bits_of(C)

            def join_round(idx, ld, total, other, *refs):
                if so_far is None:
                    before = empty()
                else:
                    before, refs = parts_of(refs[0]), refs[1:]
                new_total, new_before = join(
                    idx, ld, bit, parts_of(total), parts_of(other), before
                )
                put_parts(refs[0], new_before)
                if not last:
                    put_parts(refs[1], new_total)

            inputs = [idx, fading, total, other] + ([] if so_far is None else [so_far])
            so_far, *rest = launch(
                join_round, "s" + "v" * (len(inputs) - 1), inputs, [((3 * R, H), F32)] * (2 - last)
            )
            total = None if last else rest[0]
        return so_far

    def no_state():
        zero = jnp.zeros((R, H), F32)
        return (zero, zero, zero + lowest)

    def join_states(idx, ld, bit, total, other, before):
        up = (idx[1] >> bit) & 1 == 1
        rate = jnp.exp(ld[...])
        span = rate * float(L << bit)
        passed = (L * (idx[1] & ((1 << bit) - 1))).astype(F32)
        with_other = combine(other, before, rate * passed)
        as_later, as_earlier = combine(other, total, span), combine(total, other, span)
        return (
            tuple(jnp.where(up, a, b) for a, b in zip(as_later, as_earlier)),
            tuple(jnp.where(up, a, b) for a, b in zip(with_other, before)),
        )

    entering = scan_rounds(closing, no_state, join_states)

    hidden_turn = gather_turn(hold(hidden_first, entering), 1)
    hidden_across = gather_cross(hidden_turn)
    hidden_pieces = [hidden_matrix, *hidden_first, *hidden_across]

    def sweep(key, value, opened, ld, un, states, enter, gated, out, starts, saved=None):
        rate = jnp.exp(ld[...])
        reward = un[...]
        state = tuple(enter[pl.ds(part * R, R), :] for part in range(3))
        for i in range(CHUNKS):
            for part in range(3):
                put(starts, chunk_rows(part, i), state[part])
            state = combine(
                state, tuple(get(states, chunk_rows(part, i)) for part in range(3)), ST * rate
            )

        def step(t, carry):
            new = []
            for r in range(R):
                num, den, high = carry[r]
                k_now, v_now = get(key, step_rows(r, t)), get(value, step_rows(r, t))
                at = scan_rows(r, t)
                now = reward + k_now
                top = jnp.maximum(high, now)
                e_old, e_new = jnp.exp(high - top), jnp.exp(now - top)
                inverse = 1.0 / (e_old * den + e_new)
                e_old, e_new = e_old * inverse, e_new * inverse
                put(out, step_rows(r, t), e_old * num + e_new * v_now)
                if saved:
                    part_old, part_new, keep, fresh, nums, dens, fade = saved
                    part_old[at, :] = e_old
                    part_new[at, :] = e_new
                    nums[at, :] = num
                    dens[at, :] = den
                faded = high - rate
                peak = jnp.maximum(faded, k_now)
                a, b = jnp.exp(faded - peak), jnp.exp(k_now - peak)
                if saved:
                    keep[at, :] = a
                    fresh[at, :] = b
                new.append((a * num + b * v_now, a * den + b, peak))
            return tuple(new)

        begin_at = tuple(
            tuple(get(starts, pl.ds((part * R + r) * CHUNKS, CHUNKS)) for part in range(3))
            for r in range(R)
        )
        ends = lax.fori_loop(0, ST, step, begin_at)
        if saved:
            for r in range(R):
                put(
                    saved[-1],
                    pl.ds(r * CHUNKS, CHUNKS),
                    jnp.exp(begin_at[r][2] - ST * rate - ends[r][2]),
                )
        gated[...] = (opened[...] * get(out, EVERY)).astype(BF16)

    def sweep_time(
        idx, key, value, opened, ld, un, states, enter, p0, p1, p2, p3, p4,
        e0, e1, e2, e3, gated, out, starts, w, sems,
    ):
        copies = place_rows(idx, [p0, p1, p2, p3, p4], w, sems, 3 * H, 4 * H)
        begin(copies)
        sweep(key, value, opened, ld, un, states, enter, gated, out, starts)
        finish(copies)
        for p, part in enumerate((e0, e1, e2, e3)):
            part[...] = dot_t(gated[...], w[p * SR : (p + 1) * SR, :])

    emitted = launch(
        sweep_time,
        "s" + "v" * 7 + "h" * 5,
        (idx, key, value, opened, fading, bonus, states, entering, *time_pieces),
        [((T, SR), F32)] * S,
        [
            pltpu.VMEM((T, H), BF16),
            pltpu.VMEM((G, T, 128), F32),
            pltpu.VMEM((G, 3 * R * CHUNKS, 128), F32),
            pltpu.VMEM((WIDTH, H), BF16),
            pltpu.SemaphoreType.DMA((5,)),
        ],
        after=hidden_turn,
    )
    emitted_other = swap_parts(emitted)

    def middle_norm(xo, xp, *refs):
        mine, theirs, (middle, hat, root, last) = refs[:S], refs[S : 2 * S], refs[2 * S :]
        for r in range(R):

            def tile(i, carry):
                at = rows_at(r, i)
                values = jnp.concatenate([xo[at, :], xp[at, :]], axis=1).astype(F32)
                values = values + (columns(mine, at) + columns(theirs, at))
                n, q = norm(values)
                middle[at, :] = values[:, :H]
                hat[at, :] = n
                root[at, :] = q
                return n[TB - 1 : TB, :]

            last[r : r + 1, :] = lax.fori_loop(0, NT, tile, jnp.zeros((1, WIDTH), F32))

    middle, hat_two, root_two, hat_last = launch(
        middle_norm,
        "vv" + "v" * (2 * S),
        (x_own, x_other, *emitted, *emitted_other),
        [((T, H), F32), ((T, WIDTH), F32), ((T, 1), F32), ((R, WIDTH), F32)],
        after=return_turn_in,
    )
    hat_edge_two = along_ctx(hat_last, 1, False)
    NF = FH + H
    NB = min(512, FH)

    def channel_forward(
        idx, hat, edge, po, pp, h0, h1, h2, h3, h4,
        ckey, cgate, diff, hat_low, active, squared, opened, wh, sems_h,
    ):
        copies_h = place_rows(idx, [h0, h1, h2, h3, h4], wh, sems_h)
        begin(copies_h)
        gain, bias = both(po, pp, 5), both(po, pp, 6)
        shares = [both(po, pp, i) for i in (7, 8)]
        flag = jnp.where(idx[1] > 0, 1.0, 0.0).astype(F32)
        first = (edge[...] * gain + bias) * flag
        for r in range(R):

            def tile(i, last):
                at = rows_at(r, i)
                n = hat[at, :]
                hat_low[at, :] = n.astype(BF16)
                normed = n * gain + bias
                prev = shift_down(normed, last)
                diff[at, :] = (normed - prev).astype(BF16)
                for share, target in zip(shares, (ckey, cgate)):
                    target[at, :] = (normed * share + prev * (1.0 - share)).astype(BF16)
                return normed[TB - 1 : TB, :]

            lax.fori_loop(0, NT, tile, first[r : r + 1, :])
        finish(copies_h)
        for n in range(0, FH, NB):
            pre = jnp.maximum(dot(ckey[...], wh[:, n : n + NB]), 0.0)
            active[:, n : n + NB] = pre.astype(BF16)
            squared[:, n : n + NB] = (pre * pre).astype(BF16)
        opened[...] = jax.nn.sigmoid(dot(cgate[...], wh[:, FH:NF]))

    channel_key, channel_gate, diff_two, hat_two, active, squared, filter_open = launch(
        channel_forward,
        "svvvv" + "h" * 5,
        (idx, hat_two, hat_edge_two, params, params_other, *hidden_pieces),
        [((T, WIDTH), BF16)] * 4 + [((T, FH), BF16)] * 2 + [((T, H), F32)],
        [pltpu.VMEM((WIDTH, NF), BF16), pltpu.SemaphoreType.DMA((5,))],
    )

    def channel_return(idx, squared, r0, r1, r2, r3, r4, *rest):
        parts, (wr, sems_r) = rest[:S], rest[S:]
        copies_r = place_blocks(idx, [r0, r1, r2, r3, r4], wr, sems_r)
        begin(copies_r)
        finish(copies_r)
        for p in range(S):
            parts[p][...] = dot(squared[...], wr[p])

    returned = launch(
        channel_return,
        "sv" + "h" * 5,
        (idx, squared, *return_pieces),
        [((T, SR), F32)] * S,
        [pltpu.VMEM((S, FH, SR), BF16), pltpu.SemaphoreType.DMA((5,))],
    )
    ret_keep = returned[: S // 2]
    ret_other = [swap(part, "tp", 1) for part in returned[S // 2 :]]

    def live_rows(idx, r, i):
        at = lax.broadcasted_iota(jnp.int32, (TB, 1), 0) + (idx[1] * L + i * TB)
        return jnp.where(at < idx[3 + r], 1.0, 0.0).astype(F32)

    def close_block(idx, m0, m1, t0, t1, opened, middle, up, out, grad_ret, grad_fil):
        for r in range(R):

            def tile(i, carry):
                at = rows_at(r, i)
                live = live_rows(idx, r, i)
                returned = columns((m0, m1), at) + columns((t0, t1), at)
                s = opened[at, :]
                out[at, :] = (live * (middle[at, :] + s * returned)).astype(BF16)
                grad = live * up[at, :].astype(F32)
                grad_ret[at, :] = (grad * s).astype(BF16)
                grad_fil[at, :] = (grad * returned * s * (1.0 - s)).astype(BF16)
                return carry

            lax.fori_loop(0, NT, tile, 0)

    block_out, grad_returned, grad_filter = launch(
        close_block,
        "svvvvvvv",
        (idx, *ret_keep, *ret_other, filter_open, middle, up_own),
        [((T, H), BF16), ((T, H), BF16), ((T, H), BF16)],
    )
    grad_returned_other = swap(grad_returned, "tp", 1)

    order = []
    for spot in range(BLOCKS):
        high, low = spot // C, spot % C
        turned = 0
        for bit in range(bits_of(C)):
            turned = turned * 2 + ((low >> bit) & 1)
        order.append(high * C + turned)

    VR = 16

    def weight_grads(lefts, rights, jobs, after=(), riders=()):
        count_left = [len(group) for group in lefts]
        flat = [ref for group in lefts for ref in group]
        width = sum(job[3] for job in jobs if job[4] == 0)
        half, quarter = WIDTH // 2, WIDTH // 4

        def weight_products(idx, *refs):
            left_refs, refs = list(refs[: len(flat)]), refs[len(flat) :]
            right_refs, refs = refs[: len(rights)], refs[len(rights) :]
            rider_refs, refs = refs[: len(riders)], refs[len(riders) :]
            send_a, keep_a, send_b, keep_b, *mine, tall, turned = refs
            if riders:
                one, two, other, own = rider_refs
                total = mine[0]
                total[...] = jnp.zeros((VR, H), F32)
                total[0:5, :] = one[:, :H] + other[0:5, :]
                total[5:9, :] = two[:, :H] + other[5:9, :]
                total[9:11, :] = own[...]
                total[...] = write_pair(send_a, half, total[...])
            for g, count in enumerate(count_left):
                group, left_refs = left_refs[:count], left_refs[count:]
                row = 0
                for ref in group:
                    for lane in range(0, ref.shape[1], 128):
                        tall[row : row + 128, :] = ref[:, lane : lane + 128].astype(F32).T
                        row += 128
                for spot in range(BLOCKS):
                    block = order[spot] ^ idx[2]
                    turned[spot * BR : (spot + 1) * BR, :] = tall[
                        pl.ds(pl.multiple_of(block * BR, BR), BR), :
                    ].astype(BF16)
                for left, right, start, size, part, at in jobs:
                    if left != g:
                        continue
                    for n in range(0, size, 256):
                        to = slice(at + n, at + n + 256)
                        acc = dot(
                            turned[...], right_refs[right][:, start + n : start + n + 256]
                        ).astype(BF16)
                        if part == 0:
                            keep_a[:quarter, to] = acc[:quarter]
                            send_a[:quarter, to] = acc[quarter:half]
                            keep_a[quarter:, to] = acc[half : half + quarter]
                            send_a[quarter:half, to] = acc[half + quarter :]
                        else:
                            keep_b[:, to] = acc[:half]
                            send_b[:, to] = acc[half:]

        extra = 2 * VR if riders else 0
        return launch(
            weight_products,
            "s" + "v" * (len(flat) + len(rights) + len(riders)),
            (idx, *flat, *rights, *riders),
            [((half + extra, width), BF16)]
            + [((half, width), BF16)] * 3
            + ([((VR, H), F32)] if riders else []),
            [pltpu.VMEM((WIDTH, T), F32), pltpu.VMEM((WIDTH, T), BF16)],
            after=after,
        )

    def write_pair(ref, row, values):
        high = values.astype(BF16)
        low = (values - high.astype(F32)).astype(BF16)
        ref[row : row + VR, :H] = high
        ref[row + VR :, :H] = low
        if ref.shape[1] > H:
            ref[row:, H:] = jnp.zeros((2 * VR, ref.shape[1] - H), BF16)
        return high.astype(F32) + low.astype(F32)

    def read_pair(ref, row):
        return ref[row : row + VR, :H].astype(F32) + ref[row + VR :, :H].astype(F32)

    def add(mine, theirs):
        return mine.astype(F32) + theirs.astype(F32)

    def square_start(send_a, keep_a, send_b, keep_b, *mine):
        return [keep_a, swap(send_a, "shard", 1), keep_b, swap(send_b, "shard", 2), *mine]

    def square_turn(state):
        rows, width = state[0].shape
        half = rows // 2
        extra = 2 * VR if len(state) > 4 else 0

        def turn_square(keep_a, got_a, keep_b, got_b, *refs):
            if extra:
                mine, refs = refs[0], refs[1:]
            send_a, new_a, send_b, new_b, *total = refs
            low, high = slice(0, half), slice(half, rows)
            new_a[...] = add(keep_a[low, :], got_a[low, :]).astype(BF16)
            send_a[:half, :] = add(keep_a[high, :], got_a[high, :]).astype(BF16)
            new_b[...] = add(keep_b[low, :], got_b[low, :]).astype(BF16)
            send_b[...] = add(keep_b[high, :], got_b[high, :]).astype(BF16)
            if extra:
                total[0][...] = write_pair(send_a, half, mine[...] + read_pair(got_a, rows))

        return launch(
            turn_square,
            "v" * len(state),
            state,
            [((half + extra, width), BF16)]
            + [((half, width), BF16)] * 3
            + ([((VR, H), F32)] if extra else []),
        )

    def square_cross(send_a, keep_a, send_b, keep_b, *mine):
        return [keep_a, swap(send_a, "shard", 2), keep_b, swap(send_b, "shard", 1), *mine]

    def square_end(state):
        rows, width = state[0].shape
        half = rows // 2
        extra = 2 * VR if len(state) > 4 else 0

        def end_square(keep_a, got_a, keep_b, got_b, *refs):
            if extra:
                mine, refs = refs[0], refs[1:]
            send, new, *total = refs
            for part, (keep, got) in enumerate(((keep_a, got_a), (keep_b, got_b))):
                at = slice(part * width, (part + 1) * width)
                new[:, at] = add(keep[:half, :], got[:half, :]).astype(BF16)
                send[:half, at] = add(keep[half:, :], got[half:rows, :]).astype(BF16)
            if extra:
                total[0][...] = write_pair(send, half, mine[...] + read_pair(got_a, rows))

        return launch(
            end_square,
            "v" * len(state),
            state,
            [((half + extra, 2 * width), BF16), ((half, 2 * width), BF16)]
            + ([((VR, H), F32)] if extra else []),
        )

    def scatter_line(send, keep, *mine, widths, seen=None):
        extra = 2 * VR if mine else 0
        for bit in range(bits_of(C)):
            got = swap(send, "ctx", 1 << bit)
            if seen is not None:
                seen.append(got)
            rows, width = keep.shape
            last = bit + 1 == bits_of(C)
            half = rows if last else rows // 2

            def turn_line(keep, got, *refs):
                if extra:
                    own, refs = refs[0], refs[1:]
                if last:
                    news, refs = refs[: len(widths)], refs[len(widths) :]
                    at = 0
                    for new, size in zip(news, widths):
                        new[...] = add(keep[:, at : at + size], got[:rows, at : at + size])
                        at += size
                else:
                    new, send, *refs = refs
                    new[...] = add(keep[:half, :], got[:half, :]).astype(BF16)
                    send[:half, :] = add(keep[half:, :], got[half:rows, :]).astype(BF16)
                if extra:
                    total = own[...] + read_pair(got, rows)
                    refs[0][...] = total if last else write_pair(send, half, total)

            if last:
                outs = [((rows, size), F32) for size in widths]
            else:
                outs = [((half, width), BF16), ((half + extra, width), BF16)]
            if extra:
                outs.append(((VR, H), F32))
            result = launch(turn_line, "v" * (2 + len(mine)), (keep, got, *mine), outs)
            if not last:
                keep, send, *mine = result
        return result

    return_parts = weight_grads(
        [[grad_returned, grad_returned_other]],
        [squared],
        [(0, 0, 0, FH // 2, 0, 0), (0, 0, FH // 2, FH // 2, 1, 0)],
    )
    return_state = square_start(*return_parts)

    def channel_backward(
        idx, gro, grp, gf, active, diff, hat, edge, po, pp,
        h0, h1, h2, h3, h4, r0, r1, r2, r3, r4,
        grad_hidden, n0, n1, n2, n3, first_out, sums, wh, wr, ckey, cgate, sems_h, sems_r,
    ):
        copies_h = place_rows(idx, [h0, h1, h2, h3, h4], wh, sems_h)
        copies_r = place_blocks(idx, [r0, r1, r2, r3, r4], wr, sems_r)
        begin(copies_r)
        begin(copies_h)
        finish(copies_r)
        half = S // 2
        for n in range(0, FH, NB):
            acc = None
            for p in range(S):
                source = gro if p < half else grp
                at = (p % half) * SR
                term = dot_t(source[:, at : at + SR], wr[p, n : n + NB, :])
                acc = term if acc is None else acc + term
            grad_hidden[:, n : n + NB] = (
                acc * 2.0 * active[:, n : n + NB].astype(F32)
            ).astype(BF16)
        finish(copies_h)
        for p in range(S):
            at = slice(p * SR, (p + 1) * SR)
            ckey[:, at] = dot_t(grad_hidden[...], wh[at, :FH])
            cgate[:, at] = dot_t(gf[...], wh[at, FH:NF])
        share_k, share_g = both(po, pp, 7), both(po, pp, 8)
        flag = jnp.where(idx[1] > 0, 1.0, 0.0).astype(F32)
        zero = jnp.zeros((1, WIDTH), F32)
        totals = (zero, zero, zero, zero)
        for r in range(R):

            def tile(j, carry):
                after, gain_sum, bias_sum, key_sum, gate_sum = carry
                at = rows_at(r, NT - 1 - j)
                gk, gg, d = ckey[at, :], cgate[at, :], diff[at, :].astype(F32)
                now = gk * share_k + gg * share_g
                back = gk * (1.0 - share_k) + gg * (1.0 - share_g)
                grad = now + shift_up(back, after)
                for p, part in enumerate((n0, n1, n2, n3)):
                    part[at, :] = grad[:, p * SR : (p + 1) * SR]
                return (
                    back[0:1, :],
                    gain_sum + jnp.sum(grad * hat[at, :].astype(F32), axis=0, keepdims=True),
                    bias_sum + jnp.sum(grad, axis=0, keepdims=True),
                    key_sum + jnp.sum(gk * d, axis=0, keepdims=True),
                    gate_sum + jnp.sum(gg * d, axis=0, keepdims=True),
                )

            front, *totals = lax.fori_loop(0, NT, tile, (zero, *totals))
            first_out[r : r + 1, :] = front
            totals[0] = totals[0] + front * (edge[r : r + 1, :] * flag)
            totals[1] = totals[1] + front * flag
        for i in range(4):
            sums[i : i + 1, :] = totals[i]

    grad_hidden, *grad_two, first_two, sums_two = launch(
        channel_backward,
        "s" + "v" * 9 + "h" * 10,
        (
            idx,
            grad_returned,
            grad_returned_other,
            grad_filter,
            active,
            diff_two,
            hat_two,
            hat_edge_two,
            params,
            params_other,
            *hidden_pieces,
            *return_pieces,
        ),
        [((T, FH), BF16)]
        + [((T, SR), F32)] * S
        + [((R, WIDTH), F32), ((4, WIDTH), F32)],
        [
            pltpu.VMEM((WIDTH, NF), BF16),
            pltpu.VMEM((S, FH, SR), BF16),
            pltpu.VMEM((T, WIDTH), F32),
            pltpu.VMEM((T, WIDTH), F32),
            pltpu.SemaphoreType.DMA((5,)),
            pltpu.SemaphoreType.DMA((5,)),
        ],
        after=(return_parts[0],),
    )
    grad_two, first_two, return_state = lax.optimization_barrier(
        (grad_two, first_two, return_state)
    )
    grad_two_other = swap_parts(grad_two)
    first_two_own = along_ctx(first_two, -1, False)
    first_two_other = along_ctx(first_two, -1, True)

    def sweep_again(*refs):
        inputs, (gated, out, *saved, starts) = refs[:7], refs[7:]
        sweep(*inputs, gated, out, starts, saved)

    gated, mixed_out, part_old, part_new, keep, fresh, nums, dens, fade = launch(
        sweep_again,
        "v" * 7,
        (key, value, opened, fading, bonus, states, hold(entering, grad_returned_other)),
        [((T, H), BF16), ((G, T, 128), F32)]
        + [((T, H), F32)] * 6
        + [((G, R * CHUNKS, 128), F32)],
        [pltpu.VMEM((G, 3 * R * CHUNKS, 128), F32)],
    )

    mixed_key, mixed_value, mixed_gate, hat_one, diff_one, root_one, _ = mixes(
        *hold((x_own, x_other), grad_returned_other)
    )

    part = NF // 2
    hidden_parts = weight_grads(
        [[channel_key], [channel_gate]],
        [grad_hidden, grad_filter],
        [
            (0, 0, 0, part, 0, 0),
            (0, 0, part, FH - part, 1, 0),
            (1, 1, 0, H, 1, FH - part),
        ],
        after=(gated, root_one),
    )
    hidden_state = square_start(*hidden_parts)
    return_turn = square_turn(return_state)
    return_cross = square_cross(*return_turn)

    def middle_backward(
        idx, m0, m1, m2, m3, t0, t1, t2, t3, e_own, e_other, hat, root, po, pp, uo, upp, opened, out,
        part_old, keep, fade, p0, p1, p2, p3, p4,
        grad_mid, grad_own, grad_res, grad_gate, adjoint, entry, w, gates, sems,
    ):
        copies = place_rows(idx, [p0, p1, p2, p3, p4], w, sems, 3 * H, 4 * H)
        begin(copies)
        gain = both(po, pp, 5)
        tail = e_own[...] + swapped(e_other[...])
        row = lax.broadcasted_iota(jnp.int32, (TB, 1), 0)
        for r in range(R):

            def tile(i, carry):
                at = rows_at(r, i)
                is_last = jnp.where((row == TB - 1) & (i == NT - 1), 1.0, 0.0).astype(F32)
                grad = columns((m0, m1, m2, m3), at) + columns((t0, t1, t2, t3), at)
                grad = grad + is_last * tail[r : r + 1, :]
                n = hat[at, :].astype(F32)
                scaled = grad * gain
                mean_one = jnp.sum(scaled, axis=-1, keepdims=True) * (1.0 / WIDTH)
                mean_two = jnp.sum(scaled * n, axis=-1, keepdims=True) * (1.0 / WIDTH)
                up = jnp.concatenate([uo[at, :], upp[at, :]], axis=1).astype(F32)
                full = live_rows(idx, r, i) * up + root[at, :] * (scaled - mean_one - n * mean_two)
                grad_mid[at, :] = full.astype(BF16)
                grad_own[at, :] = full[:, :H]
                return carry

            lax.fori_loop(0, NT, tile, 0)
        finish(copies)
        gates[...] = dot(grad_mid[...], w[...])
        for r in range(R):

            def gate_tile(i, carry):
                at = rows_at(r, i)
                g, s = gates[at, :], opened[at, :]
                put(grad_res, at, g * s)
                grad_gate[at, :] = (g * get(out, at) * s * (1.0 - s)).astype(BF16)
                return carry

            lax.fori_loop(0, NT, gate_tile, 0)

        def step(j, carry):
            t = ST - 1 - j
            new = []
            for r in range(R):
                alpha, beta = carry[r]
                at = scan_rows(r, t)
                direct = part_old[at, :] * get(grad_res, step_rows(r, t))
                a = keep[at, :]
                new.append(
                    (direct + a * alpha, a * beta - direct * get(out, step_rows(r, t)))
                )
            return tuple(new)

        zero = jnp.zeros((CHUNKS, H), F32)
        ends = lax.fori_loop(0, ST, step, ((zero, zero),) * R)
        for r in range(R):
            for k in range(2):
                put(adjoint, pl.ds((k * R + r) * CHUNKS, CHUNKS), ends[r][k])
        alpha = beta = jnp.zeros((R, H), F32)
        span = jnp.ones((R, H), F32)
        for i in range(CHUNKS - 1, -1, -1):
            f = get(fade, chunk_rows(0, i))
            alpha = get(adjoint, chunk_rows(0, i)) + f * alpha
            beta = get(adjoint, chunk_rows(1, i)) + f * beta
            span = span * f
        entry[pl.ds(0, R), :] = alpha
        entry[pl.ds(R, R), :] = beta
        entry[pl.ds(2 * R, R), :] = span

    grad_mid, grad_mid_own, grad_res, grad_gate, adjoint, entry = launch(
        middle_backward,
        "s" + "v" * 21 + "h" * 5,
        (
            idx,
            *grad_two,
            *grad_two_other,
            first_two_own,
            first_two_other,
            hat_two,
            root_two,
            params,
            params_other,
            up_own,
            up_other,
            opened,
            mixed_out,
            part_old,
            keep,
            fade,
            *time_pieces,
        ),
        [
            ((T, WIDTH), BF16),
            ((T, H), F32),
            ((G, T, 128), F32),
            ((T, H), BF16),
            ((G, 2 * R * CHUNKS, 128), F32),
            ((3 * R, H), F32),
        ],
        [
            pltpu.VMEM((WIDTH, H), BF16),
            pltpu.VMEM((T, H), F32),
            pltpu.SemaphoreType.DMA((5,)),
        ],
        after=(hidden_parts[1],),
    )

    def no_adjoint():
        zero = jnp.zeros((R, H), F32)
        return (zero, zero, zero + 1.0)

    def join_adjoints(idx, ld, bit, total, other, before):
        low = (idx[1] >> bit) & 1 == 0

        def follow(near, far):
            return (near[0] + near[2] * far[0], near[1] + near[2] * far[1], near[2] * far[2])

        as_near, as_far, with_other = follow(total, other), follow(other, total), follow(before, other)
        return (
            tuple(jnp.where(low, a, b) for a, b in zip(as_near, as_far)),
            tuple(jnp.where(low, a, b) for a, b in zip(with_other, before)),
        )

    late = scan_rounds(entry, no_adjoint, join_adjoints)

    early_parts = weight_grads(
        [[grad_mid], [mixed_gate]],
        [gated, grad_gate],
        [(0, 0, 0, H, 0, 0), (1, 1, 0, H, 1, 0)],
    )
    early_state = square_start(*early_parts)

    def time_backward(
        idx, res, out, value, part_old, part_new, keep, fresh, nums, dens, fade, adjoint, late,
        ld, gate, diff, hat, edge, po, pp, p0, p1, p2, p3, p4,
        grad_key, grad_value, mine_own, s0, s1, stats, first_out, sums, sums_own,
        w, dk, dv, gk, gv, gg, starts, sems,
    ):
        copies = place_rows(idx, [p0, p1, p2, p3, p4], w, sems, 0, 3 * H)
        begin(copies)
        late_now = (late[pl.ds(0, R), :], late[pl.ds(R, R), :])
        for i in range(CHUNKS - 1, -1, -1):
            for k in range(2):
                put(starts, chunk_rows(k, i), late_now[k])
            f = get(fade, chunk_rows(0, i))
            late_now = tuple(get(adjoint, chunk_rows(k, i)) + f * late_now[k] for k in range(2))

        def step(j, carry):
            t = ST - 1 - j
            adj, fade_sum, bonus_sum = carry
            new = []
            for r in range(R):
                alpha, beta = adj[r]
                at, spread = scan_rows(r, t), step_rows(r, t)
                g, y, v = get(res, spread), get(out, spread), get(value, spread)
                b, a = fresh[at, :], keep[at, :]
                near = part_new[at, :] * g
                lift = near * (v - y)
                put(dv, spread, b * alpha + near)
                put(dk, spread, b * (v * alpha + beta) + lift)
                bonus_sum = bonus_sum + lift
                fade_sum = fade_sum - a * (nums[at, :] * alpha + dens[at, :] * beta)
                direct = part_old[at, :] * g
                new.append((direct + a * alpha, a * beta - direct * y))
            return (tuple(new), fade_sum, bonus_sum)

        first_adj = tuple(
            tuple(get(starts, pl.ds((k * R + r) * CHUNKS, CHUNKS)) for k in range(2))
            for r in range(R)
        )
        zero = jnp.zeros((CHUNKS, H), F32)
        _, fade_sum, bonus_sum = lax.fori_loop(0, ST, step, (first_adj, zero, zero))
        sums_own[0:1, :] = jnp.sum(fade_sum, axis=0, keepdims=True) * jnp.exp(ld[...])
        sums_own[1:2, :] = jnp.sum(bonus_sum, axis=0, keepdims=True)
        grad_key[...] = get(dk, EVERY).astype(BF16)
        grad_value[...] = get(dv, EVERY).astype(BF16)
        finish(copies)
        gk[...] = dot_t(grad_key[...], w[:, :H])
        gv[...] = dot_t(grad_value[...], w[:, H : 2 * H])
        gg[...] = dot_t(gate[...], w[:, 2 * H : 3 * H])
        gain = both(po, pp, 0)
        shares = [both(po, pp, i) for i in (2, 3, 4)]
        flag = jnp.where(idx[1] > 0, 1.0, 0.0).astype(F32)
        zero = jnp.zeros((1, WIDTH), F32)
        totals = (zero,) * 5
        lane = lax.broadcasted_iota(jnp.int32, (TB, 128), 1)
        for r in range(R):

            def tile(j, carry):
                after, gain_sum, bias_sum, *mix_sums = carry
                at = rows_at(r, NT - 1 - j)
                grads = (gk[at, :], gv[at, :], gg[at, :])
                d, n = diff[at, :].astype(F32), hat[at, :].astype(F32)
                now = back = None
                for share, grad in zip(shares, grads):
                    a, b = grad * share, grad * (1.0 - share)
                    now = a if now is None else now + a
                    back = b if back is None else back + b
                grad = now + shift_up(back, after)
                mine_own[at, :] = grad[:, :H]
                s0[at, :] = grad[:, H : H + SR]
                s1[at, :] = grad[:, H + SR :]
                scaled = grad * gain
                one = jnp.sum(scaled, axis=-1, keepdims=True)
                two = jnp.sum(scaled * n, axis=-1, keepdims=True)
                stats[at, :] = jnp.where(lane == 0, one, jnp.where(lane == 1, two, 0.0))
                return (
                    back[0:1, :],
                    gain_sum + jnp.sum(grad * n, axis=0, keepdims=True),
                    bias_sum + jnp.sum(grad, axis=0, keepdims=True),
                    *(
                        total + jnp.sum(one_grad * d, axis=0, keepdims=True)
                        for total, one_grad in zip(mix_sums, grads)
                    ),
                )

            front, *totals = lax.fori_loop(0, NT, tile, (zero, *totals))
            first_out[r : r + 1, :] = front
            totals[0] = totals[0] + front * edge[r : r + 1, :]
            totals[1] = totals[1] + front * flag
        for i in range(5):
            sums[i : i + 1, :] = totals[i]

    hidden_turn_out = square_turn(hold(hidden_state, late))
    hidden_cross = square_cross(*hidden_turn_out)
    grad_key, grad_value, one_own, *one_send, first_one, sums_one, sums_own = launch(
        time_backward,
        "s" + "v" * 19 + "h" * 5,
        (
            idx,
            grad_res,
            mixed_out,
            value,
            part_old,
            part_new,
            keep,
            fresh,
            nums,
            dens,
            fade,
            adjoint,
            late,
            fading,
            grad_gate,
            diff_one,
            hat_one,
            hat_edge_one,
            params,
            params_other,
            *time_pieces,
        ),
        [
            ((T, H), BF16),
            ((T, H), BF16),
            ((T, H), F32),
            ((T, SR), F32),
            ((T, SR), F32),
            ((T, 128), F32),
            ((R, WIDTH), F32),
            ((5, WIDTH), F32),
            ((2, H), F32),
        ],
        [pltpu.VMEM((WIDTH, 3 * H), BF16)]
        + [pltpu.VMEM((G, T, 128), F32)] * 2
        + [pltpu.VMEM((T, WIDTH), F32)] * 3
        + [pltpu.VMEM((G, 2 * R * CHUNKS, 128), F32), pltpu.SemaphoreType.DMA((5,))],
        after=(hidden_turn_out[0], hidden_turn_out[2], early_parts[1]),
    )
    one_other = [swap(part, "tp", 1) for part in one_send]
    first_one_own = along_ctx(first_one, -1, False)
    first_one_other = along_ctx(first_one, -1, True)

    sums_other = swap(jnp.concatenate([sums_one[:, H:], sums_two[:, H:]], axis=0), "tp", 1)
    late_parts = weight_grads(
        [[mixed_key], [mixed_value]],
        [grad_key, grad_value],
        [(0, 0, 0, H, 0, 0), (1, 1, 0, H, 1, 0)],
        after=(return_cross[1], return_cross[3], hidden_cross[1], hidden_cross[3]),
        riders=(sums_one, sums_two, sums_other, sums_own),
    )
    late_state = square_start(*late_parts)

    return_seen = []
    (return_w,) = scatter_line(
        *square_end(hold(return_cross, first_one_own, first_one_other)), widths=[FH], seen=return_seen
    )

    def input_backward(
        mine, sent, t0, t1, theirs, e_own, e_other, hat, root, po, pp, gm, out
    ):
        gain_full = both(po, pp, 0)
        tail = e_own[...] + swapped(e_other[...])
        row = lax.broadcasted_iota(jnp.int32, (TB, 1), 0)
        for r in range(R):
            weighted = tail[r : r + 1, :] * gain_full
            tail_one = jnp.sum(weighted, axis=-1, keepdims=True)
            tail_two = jnp.sum(
                weighted * hat[(r + 1) * L - TB : (r + 1) * L, :].astype(F32)[TB - 1 :],
                axis=-1,
                keepdims=True,
            )

            def tile(i, carry):
                at = rows_at(r, i)
                is_last = jnp.where((row == TB - 1) & (i == NT - 1), 1.0, 0.0).astype(F32)
                grad = mine[at, :] + columns((t0, t1), at) + is_last * tail[r : r + 1, :H]
                stats = sent[at, :] + theirs[at, :]
                mean_one = (stats[:, 0:1] + is_last * tail_one) * (1.0 / WIDTH)
                mean_two = (stats[:, 1:2] + is_last * tail_two) * (1.0 / WIDTH)
                scaled = grad * gain_full[:, :H]
                out[at, :] = gm[at, :] + root[at, :] * (
                    scaled - mean_one - hat[at, :H].astype(F32) * mean_two
                )
                return carry

            lax.fori_loop(0, NT, tile, 0)

    (input_grad,) = launch(
        input_backward,
        "v" * 12,
        (
            one_own,
            one_send[2],
            *one_other,
            first_one_own,
            first_one_other,
            hat_one,
            root_one,
            params,
            params_other,
            grad_mid_own,
        ),
        [((T, H), F32)],
        after=(late_parts[1], return_seen[0]),
    )
    hidden_seen = []
    hidden_w, filter_w = scatter_line(
        *square_end(hold(hidden_cross, late_parts[1])), widths=[FH, H], seen=hidden_seen
    )
    early_cross = square_cross(*square_turn(hold(early_state, hidden_seen[0], return_seen[-1])))
    late_cross = square_cross(*square_turn(late_state))
    output_w, gate_w = scatter_line(*square_end(hold(early_cross, input_grad)), widths=[H, H])
    key_w, value_w, vectors = scatter_line(*square_end(late_cross), widths=[H, H])
    shape = block_entries.shape
    return (
        block_out.reshape(shape),
        input_grad.reshape(shape),
        vectors[0],
        vectors[1],
        vectors[2],
        vectors[3],
        vectors[4],
        vectors[9],
        vectors[10],
        gate_w,
        key_w,
        value_w,
        output_w.T,
        vectors[5],
        vectors[6],
        vectors[7],
        vectors[8],
        hidden_w,
        filter_w,
        return_w.T,
    )


def solution(mesh):
    token = P(None, "shard", "ctx", "tp")
    feature = P("tp")
    rows = P("shard", "tp")
    cols = P("tp", "shard")
    rows_out = P(("shard", "ctx"), "tp")
    cols_out = P("tp", ("shard", "ctx"))
    return jax.shard_map(
        per_device,
        mesh=mesh,
        in_specs=(
            (token, P(None, "shard"), token)
            + (feature,) * 7
            + (rows, rows, rows, cols)
            + (feature,) * 4
            + (rows, rows, cols)
        ),
        out_specs=(
            (token, token)
            + (feature,) * 7
            + (rows_out, rows_out, rows_out, cols_out)
            + (feature,) * 4
            + (rows_out, rows_out, cols_out)
        ),
        check_vma=False,
    )
```

```python
import jax
import jax.numpy as jnp
from jax import lax
from jax.experimental import pallas as pl
from jax.experimental.pallas import tpu as pltpu
from jax.sharding import PartitionSpec as P

F32, BF16 = jnp.float32, jnp.bfloat16
WIDTH = 1024
epsilon = 1e-05
lowest = -1e30
CHUNKS = 8
SPARE = 6 * 2**20

VMEM = pl.BlockSpec(memory_space=pltpu.VMEM)
SMEM = pl.BlockSpec(memory_space=pltpu.SMEM)
HBM = pl.BlockSpec(memory_space=pl.ANY)
KINDS = {"v": VMEM, "s": SMEM, "h": HBM}


def padded_bytes(shape, dtype):
    rows = -(-shape[-2] // 8) * 8
    lanes = -(-shape[-1] // 128) * 128
    size = rows * lanes * jnp.dtype(dtype).itemsize
    for dim in shape[:-2]:
        size *= dim
    return size


def launch(body, kinds, inputs, outs, scratch=(), after=()):
    count = len(kinds)
    room = sum(padded_bytes(x.shape, x.dtype) for x in scratch if len(x.shape) > 1) + SPARE

    def run(*refs):
        body(*refs[:count], *refs[count + len(after) :])

    return pl.pallas_call(
        run,
        out_shape=[
            jax.ShapeDtypeStruct(shape, dtype) for shape, dtype in outs
        ],
        in_specs=[KINDS[kind] for kind in kinds] + [HBM] * len(after),
        out_specs=[VMEM] * len(outs),
        scratch_shapes=list(scratch),
        name=body.__name__,
        compiler_params=pltpu.CompilerParams(vmem_limit_bytes=room),
    )(*inputs, *after)


def side_by_side(*parts):
    widths = [part.shape[1] for part in parts]

    def pack(*refs):
        sources, whole, sems = refs[: len(parts)], refs[-2], refs[-1]
        copies, at = [], 0
        for i, source in enumerate(sources):
            target = whole.at[:, pl.ds(at, widths[i])]
            copies.append(pltpu.make_async_copy(source, target, sems.at[i]))
            at += widths[i]
        begin(copies)
        finish(copies)

    (whole,) = launch(
        pack,
        "h" * len(parts),
        [pltpu.with_memory_space_constraint(part, pltpu.HBM) for part in parts],
        [((parts[0].shape[0], sum(widths)), parts[0].dtype)],
        [pltpu.SemaphoreType.DMA((len(parts),))],
    )
    return whole


def hold(values, *others):
    return lax.optimization_barrier((values, others))[0]


def bits_of(count):
    return count.bit_length() - 1


def swap(value, axis, step):
    size = lax.axis_size(axis)
    return lax.ppermute(value, axis, [(i, i ^ step) for i in range(size)])


def along_ctx(value, step, cross):
    count = lax.axis_size("ctx")
    if not cross:
        pairs = [(i, i + step) for i in range(count) if 0 <= i + step < count]
        return lax.ppermute(value, "ctx", pairs)
    pairs = []
    for i in range(count):
        if 0 <= i + step < count:
            for core in range(2):
                pairs.append((2 * i + core, 2 * (i + step) + 1 - core))
    return lax.ppermute(value, ("ctx", "tp"), pairs)


def gather_first(matrix):
    return swap(matrix, "shard", 1), swap(matrix, "shard", 2)


def gather_turn(across, cut):
    half = across[0].shape[cut] // 2
    return (
        lax.slice_in_dim(across[0], 0, half, axis=cut),
        lax.slice_in_dim(across[1], half, 2 * half, axis=cut),
    )


def gather_cross(turn):
    return swap(turn[0], "shard", 2), swap(turn[1], "shard", 1)


def place_rows(idx, pieces, whole, sems, start=0, stop=None):
    base = idx[0]
    rows, cols = pieces[0].shape
    half = cols // 2
    stop = cols if stop is None else stop

    def spot(step):
        return pl.ds(pl.multiple_of((base ^ step) * rows, rows), rows)

    copies = []
    for step in range(3):
        copies.append((pieces[step].at[:, pl.ds(start, stop - start)], whole.at[spot(step), :]))
    for i in range(2):
        low, high = max(start, i * half), min(stop, (i + 1) * half)
        if low < high:
            source = pieces[3 + i].at[:, pl.ds(low - i * half, high - low)]
            copies.append((source, whole.at[spot(3), pl.ds(low - start, high - low)]))
    return [
        pltpu.make_async_copy(source, target, sems.at[i])
        for i, (source, target) in enumerate(copies)
    ]


def place_blocks(idx, pieces, whole, sems):
    base = idx[0]
    half = pieces[0].shape[0] // 2
    targets = [
        whole.at[base],
        whole.at[base ^ 1],
        whole.at[base ^ 2],
        whole.at[base ^ 3, pl.ds(0, half), :],
        whole.at[base ^ 3, pl.ds(half, half), :],
    ]
    return [
        pltpu.make_async_copy(piece, target, sems.at[i])
        for i, (piece, target) in enumerate(zip(pieces, targets))
    ]


def begin(copies):
    for copy in copies:
        copy.start()


def finish(copies):
    for copy in copies:
        copy.wait()


def dot(left, right):
    return jnp.dot(left, right, preferred_element_type=F32)


def dot_t(left, right):
    return lax.dot_general(left, right, (((1,), (1,)), ((), ())), preferred_element_type=F32)


def norm(values):
    center = jnp.sum(values, axis=-1, keepdims=True) * (1.0 / WIDTH)
    squares = jnp.sum(values * values, axis=-1, keepdims=True) * (1.0 / WIDTH)
    root = lax.rsqrt(squares - center * center + epsilon)
    return (values - center) * root, root


def both(own, other, i):
    return jnp.concatenate([own[i : i + 1, :], other[i : i + 1, :]], axis=1)


def shift_down(values, first):
    row = lax.broadcasted_iota(jnp.int32, values.shape, 0)
    return jnp.where(row == 0, first, pltpu.roll(values, 1, 0))


def shift_up(values, last):
    count = values.shape[0]
    row = lax.broadcasted_iota(jnp.int32, values.shape, 0)
    return jnp.where(row == count - 1, last, pltpu.roll(values, count - 1, 0))


def combine(earlier, later, later_span):
    shifted = earlier[2] - later_span
    high = jnp.maximum(shifted, later[2])
    early = jnp.exp(shifted - high)
    late = jnp.exp(later[2] - high)
    return (earlier[0] * early + later[0] * late, earlier[1] * early + later[1] * late, high)


def get(ref, rows):
    return jnp.concatenate([ref[g, rows, :] for g in range(ref.shape[0])], axis=1)


def put(ref, rows, values):
    for g in range(ref.shape[0]):
        ref[g, rows, :] = values[:, g * 128 : (g + 1) * 128]


def columns(refs, rows):
    return jnp.concatenate([ref[rows, :] for ref in refs], axis=1)


def swap_parts(parts):
    half = len(parts) // 2
    got = [swap(part, "tp", 1) for part in parts]
    return got[half:] + got[:half]


def swapped(values):
    half = values.shape[1] // 2
    return jnp.concatenate([values[:, half:], values[:, :half]], axis=1)


def per_device(
    block_entries,
    row_extents,
    upstream_loss_deriv,
    earlier_layernorm_scaling,
    earlier_layernorm_offset,
    temporal_mix_lookup_fraction,
    temporal_mix_payload_fraction,
    temporal_mix_filter_fraction,
    logarithmic_fading_per_feature,
    present_entry_reward,
    filter_projection,
    lookup_projection,
    payload_projection,
    temporal_mix_emit_projection,
    later_layernorm_scaling,
    later_layernorm_offset,
    feature_mix_lookup_fraction,
    feature_mix_filter_fraction,
    feature_mix_lookup_proj,
    feature_mix_filter_proj,
    feature_mix_payload_proj,
):
    batches, rows_local, L, H = block_entries.shape
    R = batches * rows_local
    T = R * L
    S, C = lax.axis_size("shard"), lax.axis_size("ctx")
    FH = feature_mix_lookup_proj.shape[1]
    ST = L // CHUNKS
    TB = min(32, L)
    NT = L // TB
    G = H // 128
    EVERY = slice(None)
    BLOCKS = S * C
    BR = WIDTH // BLOCKS
    SR = WIDTH // S
    assert S == 4 and WIDTH == 2 * H
    s_at, c_at, t_at = lax.axis_index("shard"), lax.axis_index("ctx"), lax.axis_index("tp")
    idx = jnp.concatenate(
        [
            jnp.stack(
                [s_at ^ (2 * t_at), c_at, (s_at * C + c_at) ^ (t_at * (BLOCKS // 2))]
            ).astype(jnp.int32),
            row_extents.reshape(R).astype(jnp.int32),
        ]
    )

    def rows_at(r, i):
        return pl.ds(pl.multiple_of(r * L + i * TB, TB), TB)

    def scan_rows(r, t):
        return pl.ds(pl.multiple_of((r * ST + t) * CHUNKS, CHUNKS), CHUNKS)

    def step_rows(r, t):
        return pl.ds(r * L + t, CHUNKS, stride=ST)

    def chunk_rows(part, i):
        return pl.ds(part * R * CHUNKS + i, R, stride=CHUNKS)

    x_own = block_entries.reshape(T, H)
    up_own = upstream_loss_deriv.reshape(T, H)
    params = jnp.stack(
        [
            earlier_layernorm_scaling,
            earlier_layernorm_offset,
            temporal_mix_lookup_fraction,
            temporal_mix_payload_fraction,
            temporal_mix_filter_fraction,
            later_layernorm_scaling,
            later_layernorm_offset,
            feature_mix_lookup_fraction,
            feature_mix_filter_fraction,
        ]
    )
    fading = logarithmic_fading_per_feature.reshape(1, H)
    bonus = present_entry_reward.reshape(1, H)
    def pack_time(key_part, value_part, gate_part, emit_part, whole, tall, sems):
        copies = [
            pltpu.make_async_copy(part, whole.at[:, pl.ds(i * H, H)], sems.at[i])
            for i, part in enumerate((key_part, value_part, gate_part))
        ]
        copies.append(pltpu.make_async_copy(emit_part, tall, sems.at[3]))
        begin(copies)
        copies[3].wait()
        whole[:, 3 * H :] = tall[...].astype(F32).T.astype(BF16)
        finish(copies[:3])

    time_parts = (
        lookup_projection, payload_projection, filter_projection, temporal_mix_emit_projection,
    )
    (time_matrix,) = launch(
        pack_time,
        "hhhh",
        [pltpu.with_memory_space_constraint(part, pltpu.HBM) for part in time_parts],
        [((SR, 4 * H), BF16)],
        [pltpu.VMEM((H, SR), BF16), pltpu.SemaphoreType.DMA((4,))],
    )
    time_first = gather_first(time_matrix)
    x_other = swap(x_own, "tp", 1)
    params_other = swap(params, "tp", 1)
    last_rows = [
        part.reshape(batches, rows_local, L, H)[:, :, L - 1, :].reshape(R, H)
        for part in (x_own, x_other)
    ]
    edge = along_ctx(jnp.concatenate(last_rows, axis=1), 1, False)
    up_other = swap(up_own, "tp", 1)

    def mix_time(
        idx, xo, xp, ed, po, pp, mixed_key, mixed_value, mixed_gate, hat, diff, root, hat_edge
    ):
        gain, bias = both(po, pp, 0), both(po, pp, 1)
        shares = [both(po, pp, i) for i in (2, 3, 4)]
        flag = jnp.where(idx[1] > 0, 1.0, 0.0).astype(F32)
        edge_hat, _ = norm(ed[...].astype(F32))
        hat_edge[...] = edge_hat * flag
        first = (edge_hat * gain + bias) * flag
        for r in range(R):

            def tile(i, last):
                at = rows_at(r, i)
                values = jnp.concatenate([xo[at, :], xp[at, :]], axis=1).astype(F32)
                n, q = norm(values)
                normed = n * gain + bias
                prev = shift_down(normed, last)
                hat[at, :] = n.astype(BF16)
                root[at, :] = q
                diff[at, :] = (normed - prev).astype(BF16)
                for share, target in zip(shares, (mixed_key, mixed_value, mixed_gate)):
                    target[at, :] = (normed * share + prev * (1.0 - share)).astype(BF16)
                return normed[TB - 1 : TB, :]

            lax.fori_loop(0, NT, tile, first[r : r + 1, :])

    def mixes(*tokens):
        return launch(
            mix_time,
            "svvvvv",
            (idx, *tokens, edge, params, params_other),
            [((T, WIDTH), BF16)] * 5 + [((T, 1), F32), ((R, WIDTH), F32)],
        )

    mixed_key, mixed_value, mixed_gate, *_, hat_edge_one = mixes(x_own, x_other)
    time_turn = gather_turn(hold(time_first, hat_edge_one), 1)
    time_across = gather_cross(time_turn)
    time_pieces = [time_matrix, *time_first, *time_across]
    hidden_matrix = side_by_side(feature_mix_lookup_proj, feature_mix_filter_proj)
    hidden_first = gather_first(hold(hidden_matrix, time_across))
    return_matrix = hold(feature_mix_payload_proj, time_across)
    return_first = gather_first(return_matrix)
    return_turn_in = gather_turn(return_first, 0)
    return_across = gather_cross(return_turn_in)
    return_pieces = [return_matrix, *return_first, *return_across]

    def project_time(
        idx, mk, mv, mg, ld, p0, p1, p2, p3, p4, key, value, opened, states, closing, w, sems
    ):
        copies = place_rows(idx, [p0, p1, p2, p3, p4], w, sems, 0, 3 * H)
        begin(copies)
        finish(copies)
        put(key, EVERY, dot(mk[...], w[:, :H]))
        put(value, EVERY, dot(mv[...], w[:, H : 2 * H]))
        rate = jnp.exp(ld[...])

        def step(t, carry):
            new = []
            for r in range(R):
                num, den, high = carry[r]
                k_now, v_now = get(key, step_rows(r, t)), get(value, step_rows(r, t))
                faded = high - rate
                top = jnp.maximum(faded, k_now)
                old, fresh = jnp.exp(faded - top), jnp.exp(k_now - top)
                new.append((old * num + fresh * v_now, old * den + fresh, top))
            return tuple(new)

        zero = jnp.zeros((CHUNKS, H), F32)
        ends = lax.fori_loop(0, ST, step, ((zero, zero, zero + lowest),) * R)
        for r in range(R):
            for part in range(3):
                put(states, pl.ds((part * R + r) * CHUNKS, CHUNKS), ends[r][part])
        total = tuple(get(states, chunk_rows(part, 0)) for part in range(3))
        for i in range(1, CHUNKS):
            total = combine(
                total, tuple(get(states, chunk_rows(part, i)) for part in range(3)), ST * rate
            )
        for part in range(3):
            closing[pl.ds(part * R, R), :] = total[part]
        opened[...] = jax.nn.sigmoid(dot(mg[...], w[:, 2 * H : 3 * H]))

    key, value, opened, states, closing = launch(
        project_time,
        "svvvv" + "h" * 5,
        (idx, mixed_key, mixed_value, mixed_gate, fading, *time_pieces),
        [((G, T, 128), F32)] * 2
        + [((T, H), F32), ((G, 3 * R * CHUNKS, 128), F32), ((3 * R, H), F32)],
        [pltpu.VMEM((WIDTH, 3 * H), BF16), pltpu.SemaphoreType.DMA((5,))],
        after=(up_other,),
    )

    def parts_of(ref):
        return tuple(ref[pl.ds(part * R, R), :] for part in range(3))

    def put_parts(ref, values):
        for part in range(3):
            ref[pl.ds(part * R, R), :] = values[part]

    def scan_rounds(first_total, empty, join):
        total, so_far = first_total, None
        for bit in range(bits_of(C)):
            other = swap(total, "ctx", 1 << bit)
            last = bit + 1 == bits_of(C)

            def join_round(idx, ld, total, other, *refs):
                if so_far is None:
                    before = empty()
                else:
                    before, refs = parts_of(refs[0]), refs[1:]
                new_total, new_before = join(
                    idx, ld, bit, parts_of(total), parts_of(other), before
                )
                put_parts(refs[0], new_before)
                if not last:
                    put_parts(refs[1], new_total)

            inputs = [idx, fading, total, other] + ([] if so_far is None else [so_far])
            so_far, *rest = launch(
                join_round, "s" + "v" * (len(inputs) - 1), inputs, [((3 * R, H), F32)] * (2 - last)
            )
            total = None if last else rest[0]
        return so_far

    def no_state():
        zero = jnp.zeros((R, H), F32)
        return (zero, zero, zero + lowest)

    def join_states(idx, ld, bit, total, other, before):
        up = (idx[1] >> bit) & 1 == 1
        rate = jnp.exp(ld[...])
        span = rate * float(L << bit)
        passed = (L * (idx[1] & ((1 << bit) - 1))).astype(F32)
        with_other = combine(other, before, rate * passed)
        as_later, as_earlier = combine(other, total, span), combine(total, other, span)
        return (
            tuple(jnp.where(up, a, b) for a, b in zip(as_later, as_earlier)),
            tuple(jnp.where(up, a, b) for a, b in zip(with_other, before)),
        )

    entering = scan_rounds(closing, no_state, join_states)

    hidden_turn = gather_turn(hold(hidden_first, entering), 1)
    hidden_across = gather_cross(hidden_turn)
    hidden_pieces = [hidden_matrix, *hidden_first, *hidden_across]

    def sweep(key, value, opened, ld, un, states, enter, gated, out, starts, saved=None):
        rate = jnp.exp(ld[...])
        reward = un[...]
        state = tuple(enter[pl.ds(part * R, R), :] for part in range(3))
        for i in range(CHUNKS):
            for part in range(3):
                put(starts, chunk_rows(part, i), state[part])
            state = combine(
                state, tuple(get(states, chunk_rows(part, i)) for part in range(3)), ST * rate
            )

        def step(t, carry):
            new = []
            for r in range(R):
                num, den, high = carry[r]
                k_now, v_now = get(key, step_rows(r, t)), get(value, step_rows(r, t))
                at = scan_rows(r, t)
                now = reward + k_now
                top = jnp.maximum(high, now)
                e_old, e_new = jnp.exp(high - top), jnp.exp(now - top)
                inverse = 1.0 / (e_old * den + e_new)
                e_old, e_new = e_old * inverse, e_new * inverse
                put(out, step_rows(r, t), e_old * num + e_new * v_now)
                if saved:
                    part_old, part_new, keep, fresh, nums, dens, fade = saved
                    part_old[at, :] = e_old
                    part_new[at, :] = e_new
                    nums[at, :] = num
                    dens[at, :] = den
                faded = high - rate
                peak = jnp.maximum(faded, k_now)
                a, b = jnp.exp(faded - peak), jnp.exp(k_now - peak)
                if saved:
                    keep[at, :] = a
                    fresh[at, :] = b
                new.append((a * num + b * v_now, a * den + b, peak))
            return tuple(new)

        begin_at = tuple(
            tuple(get(starts, pl.ds((part * R + r) * CHUNKS, CHUNKS)) for part in range(3))
            for r in range(R)
        )
        ends = lax.fori_loop(0, ST, step, begin_at)
        if saved:
            for r in range(R):
                put(
                    saved[-1],
                    pl.ds(r * CHUNKS, CHUNKS),
                    jnp.exp(begin_at[r][2] - ST * rate - ends[r][2]),
                )
        gated[...] = (opened[...] * get(out, EVERY)).astype(BF16)

    def sweep_time(
        idx, key, value, opened, ld, un, states, enter, p0, p1, p2, p3, p4,
        e0, e1, e2, e3, gated, out, starts, w, sems,
    ):
        copies = place_rows(idx, [p0, p1, p2, p3, p4], w, sems, 3 * H, 4 * H)
        begin(copies)
        sweep(key, value, opened, ld, un, states, enter, gated, out, starts)
        finish(copies)
        for p, part in enumerate((e0, e1, e2, e3)):
            part[...] = dot_t(gated[...], w[p * SR : (p + 1) * SR, :])

    emitted = launch(
        sweep_time,
        "s" + "v" * 7 + "h" * 5,
        (idx, key, value, opened, fading, bonus, states, entering, *time_pieces),
        [((T, SR), F32)] * S,
        [
            pltpu.VMEM((T, H), BF16),
            pltpu.VMEM((G, T, 128), F32),
            pltpu.VMEM((G, 3 * R * CHUNKS, 128), F32),
            pltpu.VMEM((WIDTH, H), BF16),
            pltpu.SemaphoreType.DMA((5,)),
        ],
        after=hidden_turn,
    )
    emitted_other = swap_parts(emitted)

    def middle_norm(xo, xp, *refs):
        mine, theirs, (middle, hat, root, last) = refs[:S], refs[S : 2 * S], refs[2 * S :]
        for r in range(R):

            def tile(i, carry):
                at = rows_at(r, i)
                values = jnp.concatenate([xo[at, :], xp[at, :]], axis=1).astype(F32)
                values = values + (columns(mine, at) + columns(theirs, at))
                n, q = norm(values)
                middle[at, :] = values[:, :H]
                hat[at, :] = n
                root[at, :] = q
                return n[TB - 1 : TB, :]

            last[r : r + 1, :] = lax.fori_loop(0, NT, tile, jnp.zeros((1, WIDTH), F32))

    middle, hat_two, root_two, hat_last = launch(
        middle_norm,
        "vv" + "v" * (2 * S),
        (x_own, x_other, *emitted, *emitted_other),
        [((T, H), F32), ((T, WIDTH), F32), ((T, 1), F32), ((R, WIDTH), F32)],
        after=return_turn_in,
    )
    hat_edge_two = along_ctx(hat_last, 1, False)
    NF = FH + H
    NB = min(512, FH)

    def channel_forward(
        idx, hat, edge, po, pp, h0, h1, h2, h3, h4,
        ckey, cgate, diff, hat_low, active, squared, opened, wh, sems_h,
    ):
        copies_h = place_rows(idx, [h0, h1, h2, h3, h4], wh, sems_h)
        begin(copies_h)
        gain, bias = both(po, pp, 5), both(po, pp, 6)
        shares = [both(po, pp, i) for i in (7, 8)]
        flag = jnp.where(idx[1] > 0, 1.0, 0.0).astype(F32)
        first = (edge[...] * gain + bias) * flag
        for r in range(R):

            def tile(i, last):
                at = rows_at(r, i)
                n = hat[at, :]
                hat_low[at, :] = n.astype(BF16)
                normed = n * gain + bias
                prev = shift_down(normed, last)
                diff[at, :] = (normed - prev).astype(BF16)
                for share, target in zip(shares, (ckey, cgate)):
                    target[at, :] = (normed * share + prev * (1.0 - share)).astype(BF16)
                return normed[TB - 1 : TB, :]

            lax.fori_loop(0, NT, tile, first[r : r + 1, :])
        finish(copies_h)
        for n in range(0, FH, NB):
            pre = jnp.maximum(dot(ckey[...], wh[:, n : n + NB]), 0.0)
            active[:, n : n + NB] = pre.astype(BF16)
            squared[:, n : n + NB] = (pre * pre).astype(BF16)
        opened[...] = jax.nn.sigmoid(dot(cgate[...], wh[:, FH:NF]))

    channel_key, channel_gate, diff_two, hat_two, active, squared, filter_open = launch(
        channel_forward,
        "svvvv" + "h" * 5,
        (idx, hat_two, hat_edge_two, params, params_other, *hidden_pieces),
        [((T, WIDTH), BF16)] * 4 + [((T, FH), BF16)] * 2 + [((T, H), F32)],
        [pltpu.VMEM((WIDTH, NF), BF16), pltpu.SemaphoreType.DMA((5,))],
    )

    def channel_return(idx, squared, r0, r1, r2, r3, r4, *rest):
        parts, (wr, sems_r) = rest[:S], rest[S:]
        copies_r = place_blocks(idx, [r0, r1, r2, r3, r4], wr, sems_r)
        begin(copies_r)
        finish(copies_r)
        for p in range(S):
            parts[p][...] = dot(squared[...], wr[p]).astype(parts[p].dtype)

    returned = launch(
        channel_return,
        "sv" + "h" * 5,
        (idx, squared, *return_pieces),
        [((T, SR), F32)] * (S // 2) + [((T, SR), BF16)] * (S // 2),
        [pltpu.VMEM((S, FH, SR), BF16), pltpu.SemaphoreType.DMA((5,))],
    )
    ret_keep = returned[: S // 2]
    ret_other = [swap(part, "tp", 1) for part in returned[S // 2 :]]

    def live_rows(idx, r, i):
        at = lax.broadcasted_iota(jnp.int32, (TB, 1), 0) + (idx[1] * L + i * TB)
        return jnp.where(at < idx[3 + r], 1.0, 0.0).astype(F32)

    def close_block(idx, m0, m1, t0, t1, opened, middle, up, out, grad_ret, grad_fil):
        for r in range(R):

            def tile(i, carry):
                at = rows_at(r, i)
                live = live_rows(idx, r, i)
                returned = columns((m0, m1), at) + columns((t0, t1), at).astype(F32)
                s = opened[at, :]
                out[at, :] = (live * (middle[at, :] + s * returned)).astype(BF16)
                grad = live * up[at, :].astype(F32)
                grad_ret[at, :] = (grad * s).astype(BF16)
                grad_fil[at, :] = (grad * returned * s * (1.0 - s)).astype(BF16)
                return carry

            lax.fori_loop(0, NT, tile, 0)

    block_out, grad_returned, grad_filter = launch(
        close_block,
        "svvvvvvv",
        (idx, *ret_keep, *ret_other, filter_open, middle, up_own),
        [((T, H), BF16), ((T, H), BF16), ((T, H), BF16)],
    )
    grad_returned_other = swap(grad_returned, "tp", 1)

    order = []
    for spot in range(BLOCKS):
        high, low = spot // C, spot % C
        turned = 0
        for bit in range(bits_of(C)):
            turned = turned * 2 + ((low >> bit) & 1)
        order.append(high * C + turned)

    VR = 16

    def weight_grads(lefts, rights, jobs, after=(), riders=()):
        count_left = [len(group) for group in lefts]
        flat = [ref for group in lefts for ref in group]
        width = sum(job[3] for job in jobs if job[4] == 0)
        half, quarter = WIDTH // 2, WIDTH // 4

        def weight_products(idx, *refs):
            left_refs, refs = list(refs[: len(flat)]), refs[len(flat) :]
            right_refs, refs = refs[: len(rights)], refs[len(rights) :]
            rider_refs, refs = refs[: len(riders)], refs[len(riders) :]
            send_a, keep_a, send_b, keep_b, *mine, tall, turned = refs
            if riders:
                one, two, other, own = rider_refs
                total = mine[0]
                total[...] = jnp.zeros((VR, H), F32)
                total[0:5, :] = one[:, :H] + other[0:5, :]
                total[5:9, :] = two[:, :H] + other[5:9, :]
                total[9:11, :] = own[...]
                total[...] = write_pair(send_a, half, total[...])
            for g, count in enumerate(count_left):
                group, left_refs = left_refs[:count], left_refs[count:]
                row = 0
                for ref in group:
                    for lane in range(0, ref.shape[1], 128):
                        tall[row : row + 128, :] = ref[:, lane : lane + 128].astype(F32).T
                        row += 128
                for spot in range(BLOCKS):
                    block = order[spot] ^ idx[2]
                    turned[spot * BR : (spot + 1) * BR, :] = tall[
                        pl.ds(pl.multiple_of(block * BR, BR), BR), :
                    ].astype(BF16)
                for left, right, start, size, part, at in jobs:
                    if left != g:
                        continue
                    for n in range(0, size, 256):
                        to = slice(at + n, at + n + 256)
                        acc = dot(
                            turned[...], right_refs[right][:, start + n : start + n + 256]
                        ).astype(BF16)
                        if part == 0:
                            keep_a[:quarter, to] = acc[:quarter]
                            send_a[:quarter, to] = acc[quarter:half]
                            keep_a[quarter:, to] = acc[half : half + quarter]
                            send_a[quarter:half, to] = acc[half + quarter :]
                        else:
                            keep_b[:, to] = acc[:half]
                            send_b[:, to] = acc[half:]

        extra = 2 * VR if riders else 0
        return launch(
            weight_products,
            "s" + "v" * (len(flat) + len(rights) + len(riders)),
            (idx, *flat, *rights, *riders),
            [((half + extra, width), BF16)]
            + [((half, width), BF16)] * 3
            + ([((VR, H), F32)] if riders else []),
            [pltpu.VMEM((WIDTH, T), F32), pltpu.VMEM((WIDTH, T), BF16)],
            after=after,
        )

    def write_pair(ref, row, values):
        high = values.astype(BF16)
        low = (values - high.astype(F32)).astype(BF16)
        ref[row : row + VR, :H] = high
        ref[row + VR :, :H] = low
        if ref.shape[1] > H:
            ref[row:, H:] = jnp.zeros((2 * VR, ref.shape[1] - H), BF16)
        return high.astype(F32) + low.astype(F32)

    def read_pair(ref, row):
        return ref[row : row + VR, :H].astype(F32) + ref[row + VR :, :H].astype(F32)

    def add(mine, theirs):
        return mine.astype(F32) + theirs.astype(F32)

    def square_start(send_a, keep_a, send_b, keep_b, *mine):
        return [keep_a, swap(send_a, "shard", 1), keep_b, swap(send_b, "shard", 2), *mine]

    def square_turn(state):
        rows, width = state[0].shape
        half = rows // 2
        extra = 2 * VR if len(state) > 4 else 0

        def turn_square(keep_a, got_a, keep_b, got_b, *refs):
            if extra:
                mine, refs = refs[0], refs[1:]
            send_a, new_a, send_b, new_b, *total = refs
            low, high = slice(0, half), slice(half, rows)
            new_a[...] = add(keep_a[low, :], got_a[low, :]).astype(BF16)
            send_a[:half, :] = add(keep_a[high, :], got_a[high, :]).astype(BF16)
            new_b[...] = add(keep_b[low, :], got_b[low, :]).astype(BF16)
            send_b[...] = add(keep_b[high, :], got_b[high, :]).astype(BF16)
            if extra:
                total[0][...] = write_pair(send_a, half, mine[...] + read_pair(got_a, rows))

        return launch(
            turn_square,
            "v" * len(state),
            state,
            [((half + extra, width), BF16)]
            + [((half, width), BF16)] * 3
            + ([((VR, H), F32)] if extra else []),
        )

    def square_cross(send_a, keep_a, send_b, keep_b, *mine):
        return [keep_a, swap(send_a, "shard", 2), keep_b, swap(send_b, "shard", 1), *mine]

    def square_end(state):
        rows, width = state[0].shape
        half = rows // 2
        extra = 2 * VR if len(state) > 4 else 0

        def end_square(keep_a, got_a, keep_b, got_b, *refs):
            if extra:
                mine, refs = refs[0], refs[1:]
            send, new, *total = refs
            for part, (keep, got) in enumerate(((keep_a, got_a), (keep_b, got_b))):
                at = slice(part * width, (part + 1) * width)
                new[:, at] = add(keep[:half, :], got[:half, :]).astype(BF16)
                send[:half, at] = add(keep[half:, :], got[half:rows, :]).astype(BF16)
            if extra:
                total[0][...] = write_pair(send, half, mine[...] + read_pair(got_a, rows))

        return launch(
            end_square,
            "v" * len(state),
            state,
            [((half + extra, 2 * width), BF16), ((half, 2 * width), BF16)]
            + ([((VR, H), F32)] if extra else []),
        )

    def scatter_line(send, keep, *mine, widths, seen=None):
        extra = 2 * VR if mine else 0
        for bit in range(bits_of(C)):
            got = swap(send, "ctx", 1 << bit)
            if seen is not None:
                seen.append(got)
            rows, width = keep.shape
            last = bit + 1 == bits_of(C)
            half = rows if last else rows // 2

            def turn_line(keep, got, *refs):
                if extra:
                    own, refs = refs[0], refs[1:]
                if last:
                    news, refs = refs[: len(widths)], refs[len(widths) :]
                    at = 0
                    for new, size in zip(news, widths):
                        new[...] = add(keep[:, at : at + size], got[:rows, at : at + size])
                        at += size
                else:
                    new, send, *refs = refs
                    new[...] = add(keep[:half, :], got[:half, :]).astype(BF16)
                    send[:half, :] = add(keep[half:, :], got[half:rows, :]).astype(BF16)
                if extra:
                    total = own[...] + read_pair(got, rows)
                    refs[0][...] = total if last else write_pair(send, half, total)

            if last:
                outs = [((rows, size), F32) for size in widths]
            else:
                outs = [((half, width), BF16), ((half + extra, width), BF16)]
            if extra:
                outs.append(((VR, H), F32))
            result = launch(turn_line, "v" * (2 + len(mine)), (keep, got, *mine), outs)
            if not last:
                keep, send, *mine = result
        return result

    return_parts = weight_grads(
        [[grad_returned, grad_returned_other]],
        [squared],
        [(0, 0, 0, FH // 2, 0, 0), (0, 0, FH // 2, FH // 2, 1, 0)],
    )
    return_state = square_start(*return_parts)

    def channel_backward(
        idx, gro, grp, gf, active, diff, hat, edge, po, pp,
        h0, h1, h2, h3, h4, r0, r1, r2, r3, r4,
        grad_hidden, n0, n1, n2, n3, first_out, sums, wh, wr, ckey, cgate, sems_h, sems_r,
    ):
        copies_h = place_rows(idx, [h0, h1, h2, h3, h4], wh, sems_h)
        copies_r = place_blocks(idx, [r0, r1, r2, r3, r4], wr, sems_r)
        begin(copies_r)
        begin(copies_h)
        finish(copies_r)
        half = S // 2
        for n in range(0, FH, NB):
            acc = None
            for p in range(S):
                source = gro if p < half else grp
                at = (p % half) * SR
                term = dot_t(source[:, at : at + SR], wr[p, n : n + NB, :])
                acc = term if acc is None else acc + term
            grad_hidden[:, n : n + NB] = (
                acc * 2.0 * active[:, n : n + NB].astype(F32)
            ).astype(BF16)
        finish(copies_h)
        for p in range(S):
            at = slice(p * SR, (p + 1) * SR)
            ckey[:, at] = dot_t(grad_hidden[...], wh[at, :FH])
            cgate[:, at] = dot_t(gf[...], wh[at, FH:NF])
        share_k, share_g = both(po, pp, 7), both(po, pp, 8)
        flag = jnp.where(idx[1] > 0, 1.0, 0.0).astype(F32)
        zero = jnp.zeros((1, WIDTH), F32)
        totals = (zero, zero, zero, zero)
        for r in range(R):

            def tile(j, carry):
                after, gain_sum, bias_sum, key_sum, gate_sum = carry
                at = rows_at(r, NT - 1 - j)
                gk, gg, d = ckey[at, :], cgate[at, :], diff[at, :].astype(F32)
                now = gk * share_k + gg * share_g
                back = gk * (1.0 - share_k) + gg * (1.0 - share_g)
                grad = now + shift_up(back, after)
                for p, part in enumerate((n0, n1, n2, n3)):
                    part[at, :] = grad[:, p * SR : (p + 1) * SR]
                return (
                    back[0:1, :],
                    gain_sum + jnp.sum(grad * hat[at, :].astype(F32), axis=0, keepdims=True),
                    bias_sum + jnp.sum(grad, axis=0, keepdims=True),
                    key_sum + jnp.sum(gk * d, axis=0, keepdims=True),
                    gate_sum + jnp.sum(gg * d, axis=0, keepdims=True),
                )

            front, *totals = lax.fori_loop(0, NT, tile, (zero, *totals))
            first_out[r : r + 1, :] = front
            totals[0] = totals[0] + front * (edge[r : r + 1, :] * flag)
            totals[1] = totals[1] + front * flag
        for i in range(4):
            sums[i : i + 1, :] = totals[i]

    grad_hidden, *grad_two, first_two, sums_two = launch(
        channel_backward,
        "s" + "v" * 9 + "h" * 10,
        (
            idx,
            grad_returned,
            grad_returned_other,
            grad_filter,
            active,
            diff_two,
            hat_two,
            hat_edge_two,
            params,
            params_other,
            *hidden_pieces,
            *return_pieces,
        ),
        [((T, FH), BF16)]
        + [((T, SR), F32)] * S
        + [((R, WIDTH), F32), ((4, WIDTH), F32)],
        [
            pltpu.VMEM((WIDTH, NF), BF16),
            pltpu.VMEM((S, FH, SR), BF16),
            pltpu.VMEM((T, WIDTH), F32),
            pltpu.VMEM((T, WIDTH), F32),
            pltpu.SemaphoreType.DMA((5,)),
            pltpu.SemaphoreType.DMA((5,)),
        ],
        after=(return_parts[0],),
    )
    grad_two, first_two, return_state = lax.optimization_barrier(
        (grad_two, first_two, return_state)
    )
    grad_two_other = swap_parts(grad_two)
    first_two_own = along_ctx(first_two, -1, False)
    first_two_other = along_ctx(first_two, -1, True)

    def sweep_again(*refs):
        inputs, (gated, out, *saved, starts) = refs[:7], refs[7:]
        sweep(*inputs, gated, out, starts, saved)

    gated, mixed_out, part_old, part_new, keep, fresh, nums, dens, fade = launch(
        sweep_again,
        "v" * 7,
        (key, value, opened, fading, bonus, states, hold(entering, grad_returned_other)),
        [((T, H), BF16), ((G, T, 128), F32)]
        + [((T, H), F32)] * 6
        + [((G, R * CHUNKS, 128), F32)],
        [pltpu.VMEM((G, 3 * R * CHUNKS, 128), F32)],
    )

    mixed_key, mixed_value, mixed_gate, hat_one, diff_one, root_one, _ = mixes(
        *hold((x_own, x_other), grad_returned_other)
    )

    part = NF // 2
    hidden_parts = weight_grads(
        [[channel_key], [channel_gate]],
        [grad_hidden, grad_filter],
        [
            (0, 0, 0, part, 0, 0),
            (0, 0, part, FH - part, 1, 0),
            (1, 1, 0, H, 1, FH - part),
        ],
        after=(gated, root_one,),
    )
    hidden_state = square_start(*hidden_parts)
    return_turn = square_turn(return_state)
    return_cross = square_cross(*return_turn)

    def middle_backward(
        idx, m0, m1, m2, m3, t0, t1, t2, t3, e_own, e_other, hat, root, po, pp, uo, upp, opened, out,
        part_old, keep, fade, p0, p1, p2, p3, p4,
        grad_mid, grad_own, grad_res, grad_gate, adjoint, entry, w, gates, sems,
    ):
        copies = place_rows(idx, [p0, p1, p2, p3, p4], w, sems, 3 * H, 4 * H)
        begin(copies)
        gain = both(po, pp, 5)
        tail = e_own[...] + swapped(e_other[...])
        row = lax.broadcasted_iota(jnp.int32, (TB, 1), 0)
        for r in range(R):

            def tile(i, carry):
                at = rows_at(r, i)
                is_last = jnp.where((row == TB - 1) & (i == NT - 1), 1.0, 0.0).astype(F32)
                grad = columns((m0, m1, m2, m3), at) + columns((t0, t1, t2, t3), at)
                grad = grad + is_last * tail[r : r + 1, :]
                n = hat[at, :].astype(F32)
                scaled = grad * gain
                mean_one = jnp.sum(scaled, axis=-1, keepdims=True) * (1.0 / WIDTH)
                mean_two = jnp.sum(scaled * n, axis=-1, keepdims=True) * (1.0 / WIDTH)
                up = jnp.concatenate([uo[at, :], upp[at, :]], axis=1).astype(F32)
                full = live_rows(idx, r, i) * up + root[at, :] * (scaled - mean_one - n * mean_two)
                grad_mid[at, :] = full.astype(BF16)
                grad_own[at, :] = full[:, :H]
                return carry

            lax.fori_loop(0, NT, tile, 0)
        finish(copies)
        gates[...] = dot(grad_mid[...], w[...])
        for r in range(R):

            def gate_tile(i, carry):
                at = rows_at(r, i)
                g, s = gates[at, :], opened[at, :]
                put(grad_res, at, g * s)
                grad_gate[at, :] = (g * get(out, at) * s * (1.0 - s)).astype(BF16)
                return carry

            lax.fori_loop(0, NT, gate_tile, 0)

        def step(j, carry):
            t = ST - 1 - j
            new = []
            for r in range(R):
                alpha, beta = carry[r]
                at = scan_rows(r, t)
                direct = part_old[at, :] * get(grad_res, step_rows(r, t))
                a = keep[at, :]
                new.append(
                    (direct + a * alpha, a * beta - direct * get(out, step_rows(r, t)))
                )
            return tuple(new)

        zero = jnp.zeros((CHUNKS, H), F32)
        ends = lax.fori_loop(0, ST, step, ((zero, zero),) * R)
        for r in range(R):
            for k in range(2):
                put(adjoint, pl.ds((k * R + r) * CHUNKS, CHUNKS), ends[r][k])
        alpha = beta = jnp.zeros((R, H), F32)
        span = jnp.ones((R, H), F32)
        for i in range(CHUNKS - 1, -1, -1):
            f = get(fade, chunk_rows(0, i))
            alpha = get(adjoint, chunk_rows(0, i)) + f * alpha
            beta = get(adjoint, chunk_rows(1, i)) + f * beta
            span = span * f
        entry[pl.ds(0, R), :] = alpha
        entry[pl.ds(R, R), :] = beta
        entry[pl.ds(2 * R, R), :] = span

    grad_mid, grad_mid_own, grad_res, grad_gate, adjoint, entry = launch(
        middle_backward,
        "s" + "v" * 21 + "h" * 5,
        (
            idx,
            *grad_two,
            *grad_two_other,
            first_two_own,
            first_two_other,
            hat_two,
            root_two,
            params,
            params_other,
            up_own,
            up_other,
            opened,
            mixed_out,
            part_old,
            keep,
            fade,
            *time_pieces,
        ),
        [
            ((T, WIDTH), BF16),
            ((T, H), F32),
            ((G, T, 128), F32),
            ((T, H), BF16),
            ((G, 2 * R * CHUNKS, 128), F32),
            ((3 * R, H), F32),
        ],
        [
            pltpu.VMEM((WIDTH, H), BF16),
            pltpu.VMEM((T, H), F32),
            pltpu.SemaphoreType.DMA((5,)),
        ],
        after=(hidden_parts[1], return_turn[0], return_turn[2],),
    )

    def no_adjoint():
        zero = jnp.zeros((R, H), F32)
        return (zero, zero, zero + 1.0)

    def join_adjoints(idx, ld, bit, total, other, before):
        low = (idx[1] >> bit) & 1 == 0

        def follow(near, far):
            return (near[0] + near[2] * far[0], near[1] + near[2] * far[1], near[2] * far[2])

        as_near, as_far, with_other = follow(total, other), follow(other, total), follow(before, other)
        return (
            tuple(jnp.where(low, a, b) for a, b in zip(as_near, as_far)),
            tuple(jnp.where(low, a, b) for a, b in zip(with_other, before)),
        )

    late = scan_rounds(entry, no_adjoint, join_adjoints)

    early_parts = weight_grads(
        [[grad_mid], [mixed_gate]],
        [gated, grad_gate],
        [(0, 0, 0, H, 0, 0), (1, 1, 0, H, 1, 0)],
    )
    early_state = square_start(*early_parts)

    def time_backward(
        idx, res, out, value, part_old, part_new, keep, fresh, nums, dens, fade, adjoint, late,
        ld, gate, diff, hat, edge, po, pp, p0, p1, p2, p3, p4,
        grad_key, grad_value, mine_own, s0, s1, stats, first_out, sums, sums_own,
        w, dk, dv, gk, gv, gg, starts, sems,
    ):
        copies = place_rows(idx, [p0, p1, p2, p3, p4], w, sems, 0, 3 * H)
        begin(copies)
        late_now = (late[pl.ds(0, R), :], late[pl.ds(R, R), :])
        for i in range(CHUNKS - 1, -1, -1):
            for k in range(2):
                put(starts, chunk_rows(k, i), late_now[k])
            f = get(fade, chunk_rows(0, i))
            late_now = tuple(get(adjoint, chunk_rows(k, i)) + f * late_now[k] for k in range(2))

        def step(j, carry):
            t = ST - 1 - j
            adj, fade_sum, bonus_sum = carry
            new = []
            for r in range(R):
                alpha, beta = adj[r]
                at, spread = scan_rows(r, t), step_rows(r, t)
                g, y, v = get(res, spread), get(out, spread), get(value, spread)
                b, a = fresh[at, :], keep[at, :]
                near = part_new[at, :] * g
                lift = near * (v - y)
                put(dv, spread, b * alpha + near)
                put(dk, spread, b * (v * alpha + beta) + lift)
                bonus_sum = bonus_sum + lift
                fade_sum = fade_sum - a * (nums[at, :] * alpha + dens[at, :] * beta)
                direct = part_old[at, :] * g
                new.append((direct + a * alpha, a * beta - direct * y))
            return (tuple(new), fade_sum, bonus_sum)

        first_adj = tuple(
            tuple(get(starts, pl.ds((k * R + r) * CHUNKS, CHUNKS)) for k in range(2))
            for r in range(R)
        )
        zero = jnp.zeros((CHUNKS, H), F32)
        _, fade_sum, bonus_sum = lax.fori_loop(0, ST, step, (first_adj, zero, zero))
        sums_own[0:1, :] = jnp.sum(fade_sum, axis=0, keepdims=True) * jnp.exp(ld[...])
        sums_own[1:2, :] = jnp.sum(bonus_sum, axis=0, keepdims=True)
        grad_key[...] = get(dk, EVERY).astype(BF16)
        grad_value[...] = get(dv, EVERY).astype(BF16)
        finish(copies)
        gk[...] = dot_t(grad_key[...], w[:, :H])
        gv[...] = dot_t(grad_value[...], w[:, H : 2 * H])
        gg[...] = dot_t(gate[...], w[:, 2 * H : 3 * H])
        gain = both(po, pp, 0)
        shares = [both(po, pp, i) for i in (2, 3, 4)]
        flag = jnp.where(idx[1] > 0, 1.0, 0.0).astype(F32)
        zero = jnp.zeros((1, WIDTH), F32)
        totals = (zero,) * 5
        lane = lax.broadcasted_iota(jnp.int32, (TB, 128), 1)
        for r in range(R):

            def tile(j, carry):
                after, gain_sum, bias_sum, *mix_sums = carry
                at = rows_at(r, NT - 1 - j)
                grads = (gk[at, :], gv[at, :], gg[at, :])
                d, n = diff[at, :].astype(F32), hat[at, :].astype(F32)
                now = back = None
                for share, grad in zip(shares, grads):
                    a, b = grad * share, grad * (1.0 - share)
                    now = a if now is None else now + a
                    back = b if back is None else back + b
                grad = now + shift_up(back, after)
                mine_own[at, :] = grad[:, :H]
                s0[at, :] = grad[:, H : H + SR]
                s1[at, :] = grad[:, H + SR :]
                scaled = grad * gain
                one = jnp.sum(scaled, axis=-1, keepdims=True)
                two = jnp.sum(scaled * n, axis=-1, keepdims=True)
                stats[at, :] = jnp.where(lane == 0, one, jnp.where(lane == 1, two, 0.0))
                return (
                    back[0:1, :],
                    gain_sum + jnp.sum(grad * n, axis=0, keepdims=True),
                    bias_sum + jnp.sum(grad, axis=0, keepdims=True),
                    *(
                        total + jnp.sum(one_grad * d, axis=0, keepdims=True)
                        for total, one_grad in zip(mix_sums, grads)
                    ),
                )

            front, *totals = lax.fori_loop(0, NT, tile, (zero, *totals))
            first_out[r : r + 1, :] = front
            totals[0] = totals[0] + front * edge[r : r + 1, :]
            totals[1] = totals[1] + front * flag
        for i in range(5):
            sums[i : i + 1, :] = totals[i]

    hidden_turn_out = square_turn(hold(hidden_state, late))
    hidden_cross = square_cross(*hidden_turn_out)
    grad_key, grad_value, one_own, *one_send, first_one, sums_one, sums_own = launch(
        time_backward,
        "s" + "v" * 19 + "h" * 5,
        (
            idx,
            grad_res,
            mixed_out,
            value,
            part_old,
            part_new,
            keep,
            fresh,
            nums,
            dens,
            fade,
            adjoint,
            late,
            fading,
            grad_gate,
            diff_one,
            hat_one,
            hat_edge_one,
            params,
            params_other,
            *time_pieces,
        ),
        [
            ((T, H), BF16),
            ((T, H), BF16),
            ((T, H), F32),
            ((T, SR), F32),
            ((T, SR), F32),
            ((T, 128), F32),
            ((R, WIDTH), F32),
            ((5, WIDTH), F32),
            ((2, H), F32),
        ],
        [pltpu.VMEM((WIDTH, 3 * H), BF16)]
        + [pltpu.VMEM((G, T, 128), F32)] * 2
        + [pltpu.VMEM((T, WIDTH), F32)] * 3
        + [pltpu.VMEM((G, 2 * R * CHUNKS, 128), F32), pltpu.SemaphoreType.DMA((5,))],
        after=(early_parts[1],),
    )
    one_other = [swap(part, "tp", 1) for part in one_send]
    first_one_own = along_ctx(first_one, -1, False)
    first_one_other = along_ctx(first_one, -1, True)

    sums_other = swap(jnp.concatenate([sums_one[:, H:], sums_two[:, H:]], axis=0), "tp", 1)
    late_parts = weight_grads(
        [[mixed_key], [mixed_value]],
        [grad_key, grad_value],
        [(0, 0, 0, H, 0, 0), (1, 1, 0, H, 1, 0)],
        after=(return_cross[1], return_cross[3], hidden_cross[1], hidden_cross[3],),
        riders=(sums_one, sums_two, sums_other, sums_own),
    )
    late_state = square_start(*late_parts)

    return_seen = []
    (return_w,) = scatter_line(
        *square_end(hold(return_cross, first_one_own, first_one_other)), widths=[FH], seen=return_seen
    )
    def input_backward(
        mine, sent, t0, t1, theirs, e_own, e_other, hat, root, po, pp, gm, out
    ):
        gain_full = both(po, pp, 0)
        tail = e_own[...] + swapped(e_other[...])
        row = lax.broadcasted_iota(jnp.int32, (TB, 1), 0)
        for r in range(R):
            weighted = tail[r : r + 1, :] * gain_full
            tail_one = jnp.sum(weighted, axis=-1, keepdims=True)
            tail_two = jnp.sum(
                weighted * hat[(r + 1) * L - TB : (r + 1) * L, :].astype(F32)[TB - 1 :],
                axis=-1,
                keepdims=True,
            )

            def tile(i, carry):
                at = rows_at(r, i)
                is_last = jnp.where((row == TB - 1) & (i == NT - 1), 1.0, 0.0).astype(F32)
                grad = mine[at, :] + columns((t0, t1), at) + is_last * tail[r : r + 1, :H]
                stats = sent[at, :] + theirs[at, :]
                mean_one = (stats[:, 0:1] + is_last * tail_one) * (1.0 / WIDTH)
                mean_two = (stats[:, 1:2] + is_last * tail_two) * (1.0 / WIDTH)
                scaled = grad * gain_full[:, :H]
                out[at, :] = gm[at, :] + root[at, :] * (
                    scaled - mean_one - hat[at, :H].astype(F32) * mean_two
                )
                return carry

            lax.fori_loop(0, NT, tile, 0)

    (input_grad,) = launch(
        input_backward,
        "v" * 12,
        (
            one_own,
            one_send[2],
            *one_other,
            first_one_own,
            first_one_other,
            hat_one,
            root_one,
            params,
            params_other,
            grad_mid_own,
        ),
        [((T, H), F32)],
        after=(late_parts[1],),
    )
    hidden_seen = []
    hidden_w, filter_w = scatter_line(
        *square_end(hidden_cross), widths=[FH, H], seen=hidden_seen
    )
    early_cross = square_cross(*square_turn(hold(early_state, hidden_seen[0], return_seen[-1])))
    late_cross = square_cross(*square_turn(late_state))
    early_seen = []
    output_w, gate_w = scatter_line(*square_end(hold(early_cross, late_cross[1], late_cross[3])), widths=[H, H], seen=early_seen)
    key_w, value_w, vectors = scatter_line(*square_end(late_cross), widths=[H, H])
    shape = block_entries.shape
    return (
        block_out.reshape(shape),
        input_grad.reshape(shape),
        vectors[0],
        vectors[1],
        vectors[2],
        vectors[3],
        vectors[4],
        vectors[9],
        vectors[10],
        gate_w,
        key_w,
        value_w,
        output_w.T,
        vectors[5],
        vectors[6],
        vectors[7],
        vectors[8],
        hidden_w,
        filter_w,
        return_w.T,
    )


def solution(mesh):
    token = P(None, "shard", "ctx", "tp")
    feature = P("tp")
    rows = P("shard", "tp")
    cols = P("tp", "shard")
    rows_out = P(("shard", "ctx"), "tp")
    cols_out = P("tp", ("shard", "ctx"))
    return jax.shard_map(
        per_device,
        mesh=mesh,
        in_specs=(
            (token, P(None, "shard"), token)
            + (feature,) * 7
            + (rows, rows, rows, cols)
            + (feature,) * 4
            + (rows, rows, cols)
        ),
        out_specs=(
            (token, token)
            + (feature,) * 7
            + (rows_out, rows_out, rows_out, cols_out)
            + (feature,) * 4
            + (rows_out, rows_out, cols_out)
        ),
        check_vma=False,
    )
```

```python
import jax
import jax.numpy as jnp
from jax import lax
from jax.experimental import pallas as pl
from jax.experimental.pallas import tpu as pltpu
from jax.sharding import PartitionSpec as P

F32, BF16 = jnp.float32, jnp.bfloat16
WIDTH = 1024
epsilon = 1e-05
lowest = -1e30
CHUNKS = 8
SPARE = 6 * 2**20

VMEM = pl.BlockSpec(memory_space=pltpu.VMEM)
SMEM = pl.BlockSpec(memory_space=pltpu.SMEM)
HBM = pl.BlockSpec(memory_space=pl.ANY)
KINDS = {"v": VMEM, "s": SMEM, "h": HBM}


def padded_bytes(shape, dtype):
    rows = -(-shape[-2] // 8) * 8
    lanes = -(-shape[-1] // 128) * 128
    size = rows * lanes * jnp.dtype(dtype).itemsize
    for dim in shape[:-2]:
        size *= dim
    return size


def launch(body, kinds, inputs, outs, scratch=(), after=()):
    count = len(kinds)
    room = sum(padded_bytes(x.shape, x.dtype) for x in scratch if len(x.shape) > 1) + SPARE

    def run(*refs):
        body(*refs[:count], *refs[count + len(after) :])

    return pl.pallas_call(
        run,
        out_shape=[
            jax.ShapeDtypeStruct(shape, dtype) for shape, dtype in outs
        ],
        in_specs=[KINDS[kind] for kind in kinds] + [HBM] * len(after),
        out_specs=[VMEM] * len(outs),
        scratch_shapes=list(scratch),
        name=body.__name__,
        compiler_params=pltpu.CompilerParams(vmem_limit_bytes=room),
    )(*inputs, *after)


def side_by_side(*parts):
    widths = [part.shape[1] for part in parts]

    def pack(*refs):
        sources, whole, sems = refs[: len(parts)], refs[-2], refs[-1]
        copies, at = [], 0
        for i, source in enumerate(sources):
            target = whole.at[:, pl.ds(at, widths[i])]
            copies.append(pltpu.make_async_copy(source, target, sems.at[i]))
            at += widths[i]
        begin(copies)
        finish(copies)

    (whole,) = launch(
        pack,
        "h" * len(parts),
        [pltpu.with_memory_space_constraint(part, pltpu.HBM) for part in parts],
        [((parts[0].shape[0], sum(widths)), parts[0].dtype)],
        [pltpu.SemaphoreType.DMA((len(parts),))],
    )
    return whole


def hold(values, *others):
    return lax.optimization_barrier((values, others))[0]


def bits_of(count):
    return count.bit_length() - 1


def swap(value, axis, step):
    size = lax.axis_size(axis)
    return lax.ppermute(value, axis, [(i, i ^ step) for i in range(size)])


def along_ctx(value, step, cross):
    count = lax.axis_size("ctx")
    if not cross:
        pairs = [(i, i + step) for i in range(count) if 0 <= i + step < count]
        return lax.ppermute(value, "ctx", pairs)
    pairs = []
    for i in range(count):
        if 0 <= i + step < count:
            for core in range(2):
                pairs.append((2 * i + core, 2 * (i + step) + 1 - core))
    return lax.ppermute(value, ("ctx", "tp"), pairs)


def gather_first(matrix):
    return swap(matrix, "shard", 1), swap(matrix, "shard", 2)


def gather_turn(across, cut):
    half = across[0].shape[cut] // 2
    return (
        lax.slice_in_dim(across[0], 0, half, axis=cut),
        lax.slice_in_dim(across[1], half, 2 * half, axis=cut),
    )


def gather_cross(turn):
    return swap(turn[0], "shard", 2), swap(turn[1], "shard", 1)


def place_rows(idx, pieces, whole, sems, start=0, stop=None):
    base = idx[0]
    rows, cols = pieces[0].shape
    half = cols // 2
    stop = cols if stop is None else stop

    def spot(step):
        return pl.ds(pl.multiple_of((base ^ step) * rows, rows), rows)

    copies = []
    for step in range(3):
        copies.append((pieces[step].at[:, pl.ds(start, stop - start)], whole.at[spot(step), :]))
    for i in range(2):
        low, high = max(start, i * half), min(stop, (i + 1) * half)
        if low < high:
            source = pieces[3 + i].at[:, pl.ds(low - i * half, high - low)]
            copies.append((source, whole.at[spot(3), pl.ds(low - start, high - low)]))
    return [
        pltpu.make_async_copy(source, target, sems.at[i])
        for i, (source, target) in enumerate(copies)
    ]


def place_blocks(idx, pieces, whole, sems):
    base = idx[0]
    half = pieces[0].shape[0] // 2
    targets = [
        whole.at[base],
        whole.at[base ^ 1],
        whole.at[base ^ 2],
        whole.at[base ^ 3, pl.ds(0, half), :],
        whole.at[base ^ 3, pl.ds(half, half), :],
    ]
    return [
        pltpu.make_async_copy(piece, target, sems.at[i])
        for i, (piece, target) in enumerate(zip(pieces, targets))
    ]


def begin(copies):
    for copy in copies:
        copy.start()


def finish(copies):
    for copy in copies:
        copy.wait()


def dot(left, right):
    return jnp.dot(left, right, preferred_element_type=F32)


def dot_t(left, right):
    return lax.dot_general(left, right, (((1,), (1,)), ((), ())), preferred_element_type=F32)


def norm(values):
    center = jnp.sum(values, axis=-1, keepdims=True) * (1.0 / WIDTH)
    squares = jnp.sum(values * values, axis=-1, keepdims=True) * (1.0 / WIDTH)
    root = lax.rsqrt(squares - center * center + epsilon)
    return (values - center) * root, root


def both(own, other, i):
    return jnp.concatenate([own[i : i + 1, :], other[i : i + 1, :]], axis=1)


def shift_down(values, first):
    row = lax.broadcasted_iota(jnp.int32, values.shape, 0)
    return jnp.where(row == 0, first, pltpu.roll(values, 1, 0))


def shift_up(values, last):
    count = values.shape[0]
    row = lax.broadcasted_iota(jnp.int32, values.shape, 0)
    return jnp.where(row == count - 1, last, pltpu.roll(values, count - 1, 0))


def combine(earlier, later, later_span):
    shifted = earlier[2] - later_span
    high = jnp.maximum(shifted, later[2])
    early = jnp.exp(shifted - high)
    late = jnp.exp(later[2] - high)
    return (earlier[0] * early + later[0] * late, earlier[1] * early + later[1] * late, high)


def get(ref, rows):
    return jnp.concatenate([ref[g, rows, :] for g in range(ref.shape[0])], axis=1)


def put(ref, rows, values):
    for g in range(ref.shape[0]):
        ref[g, rows, :] = values[:, g * 128 : (g + 1) * 128]


def columns(refs, rows):
    return jnp.concatenate([ref[rows, :] for ref in refs], axis=1)


def swap_parts(parts):
    half = len(parts) // 2
    got = [swap(part, "tp", 1) for part in parts]
    return got[half:] + got[:half]


def swapped(values):
    half = values.shape[1] // 2
    return jnp.concatenate([values[:, half:], values[:, :half]], axis=1)


def per_device(
    block_entries,
    row_extents,
    upstream_loss_deriv,
    earlier_layernorm_scaling,
    earlier_layernorm_offset,
    temporal_mix_lookup_fraction,
    temporal_mix_payload_fraction,
    temporal_mix_filter_fraction,
    logarithmic_fading_per_feature,
    present_entry_reward,
    filter_projection,
    lookup_projection,
    payload_projection,
    temporal_mix_emit_projection,
    later_layernorm_scaling,
    later_layernorm_offset,
    feature_mix_lookup_fraction,
    feature_mix_filter_fraction,
    feature_mix_lookup_proj,
    feature_mix_filter_proj,
    feature_mix_payload_proj,
):
    batches, rows_local, L, H = block_entries.shape
    R = batches * rows_local
    T = R * L
    S, C = lax.axis_size("shard"), lax.axis_size("ctx")
    FH = feature_mix_lookup_proj.shape[1]
    ST = L // CHUNKS
    TB = min(32, L)
    NT = L // TB
    G = H // 128
    EVERY = slice(None)
    BLOCKS = S * C
    BR = WIDTH // BLOCKS
    SR = WIDTH // S
    assert S == 4 and WIDTH == 2 * H
    s_at, c_at, t_at = lax.axis_index("shard"), lax.axis_index("ctx"), lax.axis_index("tp")
    idx = jnp.concatenate(
        [
            jnp.stack(
                [s_at ^ (2 * t_at), c_at, (s_at * C + c_at) ^ (t_at * (BLOCKS // 2))]
            ).astype(jnp.int32),
            row_extents.reshape(R).astype(jnp.int32),
        ]
    )

    def rows_at(r, i):
        return pl.ds(pl.multiple_of(r * L + i * TB, TB), TB)

    def scan_rows(r, t):
        return pl.ds(pl.multiple_of((r * ST + t) * CHUNKS, CHUNKS), CHUNKS)

    def step_rows(r, t):
        return pl.ds(r * L + t, CHUNKS, stride=ST)

    def chunk_rows(part, i):
        return pl.ds(part * R * CHUNKS + i, R, stride=CHUNKS)

    x_own = block_entries.reshape(T, H)
    up_own = upstream_loss_deriv.reshape(T, H)
    params = jnp.stack(
        [
            earlier_layernorm_scaling,
            earlier_layernorm_offset,
            temporal_mix_lookup_fraction,
            temporal_mix_payload_fraction,
            temporal_mix_filter_fraction,
            later_layernorm_scaling,
            later_layernorm_offset,
            feature_mix_lookup_fraction,
            feature_mix_filter_fraction,
        ]
    )
    fading = logarithmic_fading_per_feature.reshape(1, H)
    bonus = present_entry_reward.reshape(1, H)
    def pack_time(key_part, value_part, gate_part, emit_part, whole, tall, sems):
        copies = [
            pltpu.make_async_copy(part, whole.at[:, pl.ds(i * H, H)], sems.at[i])
            for i, part in enumerate((key_part, value_part, gate_part))
        ]
        copies.append(pltpu.make_async_copy(emit_part, tall, sems.at[3]))
        begin(copies)
        copies[3].wait()
        whole[:, 3 * H :] = tall[...].astype(F32).T.astype(BF16)
        finish(copies[:3])

    time_parts = (
        lookup_projection, payload_projection, filter_projection, temporal_mix_emit_projection,
    )
    (time_matrix,) = launch(
        pack_time,
        "hhhh",
        [pltpu.with_memory_space_constraint(part, pltpu.HBM) for part in time_parts],
        [((SR, 4 * H), BF16)],
        [pltpu.VMEM((H, SR), BF16), pltpu.SemaphoreType.DMA((4,))],
    )
    time_first = gather_first(time_matrix)
    x_other = swap(x_own, "tp", 1)
    params_other = swap(params, "tp", 1)
    last_rows = [
        part.reshape(batches, rows_local, L, H)[:, :, L - 1, :].reshape(R, H)
        for part in (x_own, x_other)
    ]
    edge = along_ctx(jnp.concatenate(last_rows, axis=1), 1, False)
    up_other = swap(up_own, "tp", 1)

    def mix_time(
        idx, xo, xp, ed, po, pp, mixed_key, mixed_value, mixed_gate, hat, diff, root, hat_edge
    ):
        gain, bias = both(po, pp, 0), both(po, pp, 1)
        shares = [both(po, pp, i) for i in (2, 3, 4)]
        flag = jnp.where(idx[1] > 0, 1.0, 0.0).astype(F32)
        edge_hat, _ = norm(ed[...].astype(F32))
        hat_edge[...] = edge_hat * flag
        first = (edge_hat * gain + bias) * flag
        for r in range(R):

            def tile(i, last):
                at = rows_at(r, i)
                values = jnp.concatenate([xo[at, :], xp[at, :]], axis=1).astype(F32)
                n, q = norm(values)
                normed = n * gain + bias
                prev = shift_down(normed, last)
                hat[at, :] = n.astype(BF16)
                root[at, :] = q
                diff[at, :] = (normed - prev).astype(BF16)
                for share, target in zip(shares, (mixed_key, mixed_value, mixed_gate)):
                    target[at, :] = (normed * share + prev * (1.0 - share)).astype(BF16)
                return normed[TB - 1 : TB, :]

            lax.fori_loop(0, NT, tile, first[r : r + 1, :])

    def mixes(*tokens):
        return launch(
            mix_time,
            "svvvvv",
            (idx, *tokens, edge, params, params_other),
            [((T, WIDTH), BF16)] * 5 + [((T, 1), F32), ((R, WIDTH), F32)],
        )

    mixed_key, mixed_value, mixed_gate, *_, hat_edge_one = mixes(x_own, x_other)
    time_turn = gather_turn(hold(time_first, hat_edge_one), 1)
    time_across = gather_cross(time_turn)
    time_pieces = [time_matrix, *time_first, *time_across]
    hidden_matrix = side_by_side(feature_mix_lookup_proj, feature_mix_filter_proj)
    hidden_first = gather_first(hold(hidden_matrix, time_across))
    return_matrix = hold(feature_mix_payload_proj, time_across)
    return_first = gather_first(return_matrix)
    return_turn_in = gather_turn(return_first, 0)
    return_across = gather_cross(return_turn_in)
    return_pieces = [return_matrix, *return_first, *return_across]

    def project_time(
        idx, mk, mv, mg, ld, p0, p1, p2, p3, p4, key, value, opened, states, closing, w, sems
    ):
        copies = place_rows(idx, [p0, p1, p2, p3, p4], w, sems, 0, 3 * H)
        begin(copies)
        finish(copies)
        put(key, EVERY, dot(mk[...], w[:, :H]))
        put(value, EVERY, dot(mv[...], w[:, H : 2 * H]))
        rate = jnp.exp(ld[...])

        def step(t, carry):
            new = []
            for r in range(R):
                num, den, high = carry[r]
                k_now, v_now = get(key, step_rows(r, t)), get(value, step_rows(r, t))
                faded = high - rate
                top = jnp.maximum(faded, k_now)
                old, fresh = jnp.exp(faded - top), jnp.exp(k_now - top)
                new.append((old * num + fresh * v_now, old * den + fresh, top))
            return tuple(new)

        zero = jnp.zeros((CHUNKS, H), F32)
        ends = lax.fori_loop(0, ST, step, ((zero, zero, zero + lowest),) * R)
        for r in range(R):
            for part in range(3):
                put(states, pl.ds((part * R + r) * CHUNKS, CHUNKS), ends[r][part])
        total = tuple(get(states, chunk_rows(part, 0)) for part in range(3))
        for i in range(1, CHUNKS):
            total = combine(
                total, tuple(get(states, chunk_rows(part, i)) for part in range(3)), ST * rate
            )
        for part in range(3):
            closing[pl.ds(part * R, R), :] = total[part]
        opened[...] = jax.nn.sigmoid(dot(mg[...], w[:, 2 * H : 3 * H]))

    key, value, opened, states, closing = launch(
        project_time,
        "svvvv" + "h" * 5,
        (idx, mixed_key, mixed_value, mixed_gate, fading, *time_pieces),
        [((G, T, 128), F32)] * 2
        + [((T, H), F32), ((G, 3 * R * CHUNKS, 128), F32), ((3 * R, H), F32)],
        [pltpu.VMEM((WIDTH, 3 * H), BF16), pltpu.SemaphoreType.DMA((5,))],
        after=(up_other,),
    )

    def parts_of(ref):
        return tuple(ref[pl.ds(part * R, R), :] for part in range(3))

    def put_parts(ref, values):
        for part in range(3):
            ref[pl.ds(part * R, R), :] = values[part]

    def scan_rounds(first_total, empty, join):
        total, so_far = first_total, None
        for bit in range(bits_of(C)):
            other = swap(total, "ctx", 1 << bit)
            last = bit + 1 == bits_of(C)

            def join_round(idx, ld, total, other, *refs):
                if so_far is None:
                    before = empty()
                else:
                    before, refs = parts_of(refs[0]), refs[1:]
                new_total, new_before = join(
                    idx, ld, bit, parts_of(total), parts_of(other), before
                )
                put_parts(refs[0], new_before)
                if not last:
                    put_parts(refs[1], new_total)

            inputs = [idx, fading, total, other] + ([] if so_far is None else [so_far])
            so_far, *rest = launch(
                join_round, "s" + "v" * (len(inputs) - 1), inputs, [((3 * R, H), F32)] * (2 - last)
            )
            total = None if last else rest[0]
        return so_far

    def no_state():
        zero = jnp.zeros((R, H), F32)
        return (zero, zero, zero + lowest)

    def join_states(idx, ld, bit, total, other, before):
        up = (idx[1] >> bit) & 1 == 1
        rate = jnp.exp(ld[...])
        span = rate * float(L << bit)
        passed = (L * (idx[1] & ((1 << bit) - 1))).astype(F32)
        with_other = combine(other, before, rate * passed)
        as_later, as_earlier = combine(other, total, span), combine(total, other, span)
        return (
            tuple(jnp.where(up, a, b) for a, b in zip(as_later, as_earlier)),
            tuple(jnp.where(up, a, b) for a, b in zip(with_other, before)),
        )

    entering = scan_rounds(closing, no_state, join_states)

    hidden_turn = gather_turn(hold(hidden_first, entering), 1)
    hidden_across = gather_cross(hidden_turn)
    hidden_pieces = [hidden_matrix, *hidden_first, *hidden_across]

    def sweep(key, value, opened, ld, un, states, enter, gated, out, starts, saved=None):
        rate = jnp.exp(ld[...])
        reward = un[...]
        state = tuple(enter[pl.ds(part * R, R), :] for part in range(3))
        for i in range(CHUNKS):
            for part in range(3):
                put(starts, chunk_rows(part, i), state[part])
            state = combine(
                state, tuple(get(states, chunk_rows(part, i)) for part in range(3)), ST * rate
            )

        def step(t, carry):
            new = []
            for r in range(R):
                num, den, high = carry[r]
                k_now, v_now = get(key, step_rows(r, t)), get(value, step_rows(r, t))
                at = scan_rows(r, t)
                now = reward + k_now
                top = jnp.maximum(high, now)
                e_old, e_new = jnp.exp(high - top), jnp.exp(now - top)
                inverse = 1.0 / (e_old * den + e_new)
                e_old, e_new = e_old * inverse, e_new * inverse
                put(out, step_rows(r, t), e_old * num + e_new * v_now)
                if saved:
                    part_old, part_new, keep, fresh, nums, dens, fade = saved
                    part_old[at, :] = e_old
                    part_new[at, :] = e_new
                    nums[at, :] = num
                    dens[at, :] = den
                faded = high - rate
                peak = jnp.maximum(faded, k_now)
                a, b = jnp.exp(faded - peak), jnp.exp(k_now - peak)
                if saved:
                    keep[at, :] = a
                    fresh[at, :] = b
                new.append((a * num + b * v_now, a * den + b, peak))
            return tuple(new)

        begin_at = tuple(
            tuple(get(starts, pl.ds((part * R + r) * CHUNKS, CHUNKS)) for part in range(3))
            for r in range(R)
        )
        ends = lax.fori_loop(0, ST, step, begin_at)
        if saved:
            for r in range(R):
                put(
                    saved[-1],
                    pl.ds(r * CHUNKS, CHUNKS),
                    jnp.exp(begin_at[r][2] - ST * rate - ends[r][2]),
                )
        gated[...] = (opened[...] * get(out, EVERY)).astype(BF16)

    def sweep_time(
        idx, key, value, opened, ld, un, states, enter, p0, p1, p2, p3, p4,
        e0, e1, e2, e3, gated, out, starts, w, sems,
    ):
        copies = place_rows(idx, [p0, p1, p2, p3, p4], w, sems, 3 * H, 4 * H)
        begin(copies)
        sweep(key, value, opened, ld, un, states, enter, gated, out, starts)
        finish(copies)
        for p, part in enumerate((e0, e1, e2, e3)):
            part[...] = dot_t(gated[...], w[p * SR : (p + 1) * SR, :])

    emitted = launch(
        sweep_time,
        "s" + "v" * 7 + "h" * 5,
        (idx, key, value, opened, fading, bonus, states, entering, *time_pieces),
        [((T, SR), F32)] * S,
        [
            pltpu.VMEM((T, H), BF16),
            pltpu.VMEM((G, T, 128), F32),
            pltpu.VMEM((G, 3 * R * CHUNKS, 128), F32),
            pltpu.VMEM((WIDTH, H), BF16),
            pltpu.SemaphoreType.DMA((5,)),
        ],
        after=hidden_turn,
    )
    emitted_other = swap_parts(emitted)

    def middle_norm(xo, xp, *refs):
        mine, theirs, (middle, hat, root, last) = refs[:S], refs[S : 2 * S], refs[2 * S :]
        for r in range(R):

            def tile(i, carry):
                at = rows_at(r, i)
                values = jnp.concatenate([xo[at, :], xp[at, :]], axis=1).astype(F32)
                values = values + (columns(mine, at) + columns(theirs, at))
                n, q = norm(values)
                middle[at, :] = values[:, :H]
                hat[at, :] = n
                root[at, :] = q
                return n[TB - 1 : TB, :]

            last[r : r + 1, :] = lax.fori_loop(0, NT, tile, jnp.zeros((1, WIDTH), F32))

    middle, hat_two, root_two, hat_last = launch(
        middle_norm,
        "vv" + "v" * (2 * S),
        (x_own, x_other, *emitted, *emitted_other),
        [((T, H), F32), ((T, WIDTH), F32), ((T, 1), F32), ((R, WIDTH), F32)],
        after=return_turn_in,
    )
    hat_edge_two = along_ctx(hat_last, 1, False)
    NF = FH + H
    NB = min(512, FH)

    def channel_forward(
        idx, hat, edge, po, pp, h0, h1, h2, h3, h4,
        ckey, cgate, diff, hat_low, active, squared, opened, wh, sems_h,
    ):
        copies_h = place_rows(idx, [h0, h1, h2, h3, h4], wh, sems_h)
        begin(copies_h)
        gain, bias = both(po, pp, 5), both(po, pp, 6)
        shares = [both(po, pp, i) for i in (7, 8)]
        flag = jnp.where(idx[1] > 0, 1.0, 0.0).astype(F32)
        first = (edge[...] * gain + bias) * flag
        for r in range(R):

            def tile(i, last):
                at = rows_at(r, i)
                n = hat[at, :]
                hat_low[at, :] = n.astype(BF16)
                normed = n * gain + bias
                prev = shift_down(normed, last)
                diff[at, :] = (normed - prev).astype(BF16)
                for share, target in zip(shares, (ckey, cgate)):
                    target[at, :] = (normed * share + prev * (1.0 - share)).astype(BF16)
                return normed[TB - 1 : TB, :]

            lax.fori_loop(0, NT, tile, first[r : r + 1, :])
        finish(copies_h)
        for n in range(0, FH, NB):
            pre = jnp.maximum(dot(ckey[...], wh[:, n : n + NB]), 0.0)
            active[:, n : n + NB] = pre.astype(BF16)
            squared[:, n : n + NB] = (pre * pre).astype(BF16)
        opened[...] = jax.nn.sigmoid(dot(cgate[...], wh[:, FH:NF]))

    channel_key, channel_gate, diff_two, hat_two, active, squared, filter_open = launch(
        channel_forward,
        "svvvv" + "h" * 5,
        (idx, hat_two, hat_edge_two, params, params_other, *hidden_pieces),
        [((T, WIDTH), BF16)] * 4 + [((T, FH), BF16)] * 2 + [((T, H), F32)],
        [pltpu.VMEM((WIDTH, NF), BF16), pltpu.SemaphoreType.DMA((5,))],
    )

    def channel_return(idx, squared, r0, r1, r2, r3, r4, *rest):
        parts, (wr, sems_r) = rest[:S], rest[S:]
        copies_r = place_blocks(idx, [r0, r1, r2, r3, r4], wr, sems_r)
        begin(copies_r)
        finish(copies_r)
        for p in range(S):
            parts[p][...] = dot(squared[...], wr[p]).astype(parts[p].dtype)

    returned = launch(
        channel_return,
        "sv" + "h" * 5,
        (idx, squared, *return_pieces),
        [((T, SR), F32)] * (S // 2) + [((T, SR), BF16)] * (S // 2),
        [pltpu.VMEM((S, FH, SR), BF16), pltpu.SemaphoreType.DMA((5,))],
    )
    ret_keep = returned[: S // 2]
    ret_other = [swap(part, "tp", 1) for part in returned[S // 2 :]]

    def live_rows(idx, r, i):
        at = lax.broadcasted_iota(jnp.int32, (TB, 1), 0) + (idx[1] * L + i * TB)
        return jnp.where(at < idx[3 + r], 1.0, 0.0).astype(F32)

    def close_block(idx, m0, m1, t0, t1, opened, middle, up, out, grad_ret, grad_fil):
        for r in range(R):

            def tile(i, carry):
                at = rows_at(r, i)
                live = live_rows(idx, r, i)
                returned = columns((m0, m1), at) + columns((t0, t1), at).astype(F32)
                s = opened[at, :]
                out[at, :] = (live * (middle[at, :] + s * returned)).astype(BF16)
                grad = live * up[at, :].astype(F32)
                grad_ret[at, :] = (grad * s).astype(BF16)
                grad_fil[at, :] = (grad * returned * s * (1.0 - s)).astype(BF16)
                return carry

            lax.fori_loop(0, NT, tile, 0)

    block_out, grad_returned, grad_filter = launch(
        close_block,
        "svvvvvvv",
        (idx, *ret_keep, *ret_other, filter_open, middle, up_own),
        [((T, H), BF16), ((T, H), BF16), ((T, H), BF16)],
    )
    grad_returned_other = swap(grad_returned, "tp", 1)

    order = []
    for spot in range(BLOCKS):
        high, low = spot // C, spot % C
        turned = 0
        for bit in range(bits_of(C)):
            turned = turned * 2 + ((low >> bit) & 1)
        order.append(high * C + turned)

    VR = 16

    def weight_grads(lefts, rights, jobs, after=(), riders=()):
        count_left = [len(group) for group in lefts]
        flat = [ref for group in lefts for ref in group]
        width = sum(job[3] for job in jobs if job[4] == 0)
        half, quarter = WIDTH // 2, WIDTH // 4

        def weight_products(idx, *refs):
            left_refs, refs = list(refs[: len(flat)]), refs[len(flat) :]
            right_refs, refs = refs[: len(rights)], refs[len(rights) :]
            rider_refs, refs = refs[: len(riders)], refs[len(riders) :]
            send_a, keep_a, send_b, keep_b, *mine, tall, turned = refs
            if riders:
                one, two, other, own = rider_refs
                total = mine[0]
                total[...] = jnp.zeros((VR, H), F32)
                total[0:5, :] = one[:, :H] + other[0:5, :]
                total[5:9, :] = two[:, :H] + other[5:9, :]
                total[9:11, :] = own[...]
                total[...] = write_pair(send_a, half, total[...])
            for g, count in enumerate(count_left):
                group, left_refs = left_refs[:count], left_refs[count:]
                row = 0
                for ref in group:
                    for lane in range(0, ref.shape[1], 128):
                        tall[row : row + 128, :] = ref[:, lane : lane + 128].astype(F32).T
                        row += 128
                for spot in range(BLOCKS):
                    block = order[spot] ^ idx[2]
                    turned[spot * BR : (spot + 1) * BR, :] = tall[
                        pl.ds(pl.multiple_of(block * BR, BR), BR), :
                    ].astype(BF16)
                for left, right, start, size, part, at in jobs:
                    if left != g:
                        continue
                    for n in range(0, size, 256):
                        to = slice(at + n, at + n + 256)
                        acc = dot(
                            turned[...], right_refs[right][:, start + n : start + n + 256]
                        ).astype(BF16)
                        if part == 0:
                            keep_a[:quarter, to] = acc[:quarter]
                            send_a[:quarter, to] = acc[quarter:half]
                            keep_a[quarter:, to] = acc[half : half + quarter]
                            send_a[quarter:half, to] = acc[half + quarter :]
                        else:
                            keep_b[:, to] = acc[:half]
                            send_b[:, to] = acc[half:]

        extra = 2 * VR if riders else 0
        return launch(
            weight_products,
            "s" + "v" * (len(flat) + len(rights) + len(riders)),
            (idx, *flat, *rights, *riders),
            [((half + extra, width), BF16)]
            + [((half, width), BF16)] * 3
            + ([((VR, H), F32)] if riders else []),
            [pltpu.VMEM((WIDTH, T), F32), pltpu.VMEM((WIDTH, T), BF16)],
            after=after,
        )

    def write_pair(ref, row, values):
        high = values.astype(BF16)
        low = (values - high.astype(F32)).astype(BF16)
        ref[row : row + VR, :H] = high
        ref[row + VR :, :H] = low
        if ref.shape[1] > H:
            ref[row:, H:] = jnp.zeros((2 * VR, ref.shape[1] - H), BF16)
        return high.astype(F32) + low.astype(F32)

    def read_pair(ref, row):
        return ref[row : row + VR, :H].astype(F32) + ref[row + VR :, :H].astype(F32)

    def add(mine, theirs):
        return mine.astype(F32) + theirs.astype(F32)

    def square_start(send_a, keep_a, send_b, keep_b, *mine):
        return [keep_a, swap(send_a, "shard", 1), keep_b, swap(send_b, "shard", 2), *mine]

    def square_turn(state):
        rows, width = state[0].shape
        half = rows // 2
        extra = 2 * VR if len(state) > 4 else 0

        def turn_square(keep_a, got_a, keep_b, got_b, *refs):
            if extra:
                mine, refs = refs[0], refs[1:]
            send_a, new_a, send_b, new_b, *total = refs
            low, high = slice(0, half), slice(half, rows)
            new_a[...] = add(keep_a[low, :], got_a[low, :]).astype(BF16)
            send_a[:half, :] = add(keep_a[high, :], got_a[high, :]).astype(BF16)
            new_b[...] = add(keep_b[low, :], got_b[low, :]).astype(BF16)
            send_b[...] = add(keep_b[high, :], got_b[high, :]).astype(BF16)
            if extra:
                total[0][...] = write_pair(send_a, half, mine[...] + read_pair(got_a, rows))

        return launch(
            turn_square,
            "v" * len(state),
            state,
            [((half + extra, width), BF16)]
            + [((half, width), BF16)] * 3
            + ([((VR, H), F32)] if extra else []),
        )

    def square_cross(send_a, keep_a, send_b, keep_b, *mine):
        return [keep_a, swap(send_a, "shard", 2), keep_b, swap(send_b, "shard", 1), *mine]

    def square_end(state):
        rows, width = state[0].shape
        half = rows // 2
        extra = 2 * VR if len(state) > 4 else 0

        def end_square(keep_a, got_a, keep_b, got_b, *refs):
            if extra:
                mine, refs = refs[0], refs[1:]
            send, new, *total = refs
            for part, (keep, got) in enumerate(((keep_a, got_a), (keep_b, got_b))):
                at = slice(part * width, (part + 1) * width)
                new[:, at] = add(keep[:half, :], got[:half, :]).astype(BF16)
                send[:half, at] = add(keep[half:, :], got[half:rows, :]).astype(BF16)
            if extra:
                total[0][...] = write_pair(send, half, mine[...] + read_pair(got_a, rows))

        return launch(
            end_square,
            "v" * len(state),
            state,
            [((half + extra, 2 * width), BF16), ((half, 2 * width), BF16)]
            + ([((VR, H), F32)] if extra else []),
        )

    def scatter_line(send, keep, *mine, widths, seen=None, behind=None):
        extra = 2 * VR if mine else 0
        for bit in range(bits_of(C)):
            if behind is not None and bit + 1 == bits_of(C):
                send = hold(send, behind)
            got = swap(send, "ctx", 1 << bit)
            if seen is not None:
                seen.append(got)
            rows, width = keep.shape
            last = bit + 1 == bits_of(C)
            half = rows if last else rows // 2

            def turn_line(keep, got, *refs):
                if extra:
                    own, refs = refs[0], refs[1:]
                if last:
                    news, refs = refs[: len(widths)], refs[len(widths) :]
                    at = 0
                    for new, size in zip(news, widths):
                        new[...] = add(keep[:, at : at + size], got[:rows, at : at + size])
                        at += size
                else:
                    new, send, *refs = refs
                    new[...] = add(keep[:half, :], got[:half, :]).astype(BF16)
                    send[:half, :] = add(keep[half:, :], got[half:rows, :]).astype(BF16)
                if extra:
                    total = own[...] + read_pair(got, rows)
                    refs[0][...] = total if last else write_pair(send, half, total)

            if last:
                outs = [((rows, size), F32) for size in widths]
            else:
                outs = [((half, width), BF16), ((half + extra, width), BF16)]
            if extra:
                outs.append(((VR, H), F32))
            result = launch(turn_line, "v" * (2 + len(mine)), (keep, got, *mine), outs)
            if not last:
                keep, send, *mine = result
        return result

    return_parts = weight_grads(
        [[grad_returned, grad_returned_other]],
        [squared],
        [(0, 0, 0, FH // 2, 0, 0), (0, 0, FH // 2, FH // 2, 1, 0)],
    )
    return_state = square_start(*return_parts)

    def channel_backward(
        idx, gro, grp, gf, active, diff, hat, edge, po, pp,
        h0, h1, h2, h3, h4, r0, r1, r2, r3, r4,
        grad_hidden, n0, n1, n2, n3, first_out, sums, wh, wr, ckey, cgate, sems_h, sems_r,
    ):
        copies_h = place_rows(idx, [h0, h1, h2, h3, h4], wh, sems_h)
        copies_r = place_blocks(idx, [r0, r1, r2, r3, r4], wr, sems_r)
        begin(copies_r)
        begin(copies_h)
        finish(copies_r)
        half = S // 2
        for n in range(0, FH, NB):
            acc = None
            for p in range(S):
                source = gro if p < half else grp
                at = (p % half) * SR
                term = dot_t(source[:, at : at + SR], wr[p, n : n + NB, :])
                acc = term if acc is None else acc + term
            grad_hidden[:, n : n + NB] = (
                acc * 2.0 * active[:, n : n + NB].astype(F32)
            ).astype(BF16)
        finish(copies_h)
        for p in range(S):
            at = slice(p * SR, (p + 1) * SR)
            ckey[:, at] = dot_t(grad_hidden[...], wh[at, :FH])
            cgate[:, at] = dot_t(gf[...], wh[at, FH:NF])
        share_k, share_g = both(po, pp, 7), both(po, pp, 8)
        flag = jnp.where(idx[1] > 0, 1.0, 0.0).astype(F32)
        zero = jnp.zeros((1, WIDTH), F32)
        totals = (zero, zero, zero, zero)
        for r in range(R):

            def tile(j, carry):
                after, gain_sum, bias_sum, key_sum, gate_sum = carry
                at = rows_at(r, NT - 1 - j)
                gk, gg, d = ckey[at, :], cgate[at, :], diff[at, :].astype(F32)
                now = gk * share_k + gg * share_g
                back = gk * (1.0 - share_k) + gg * (1.0 - share_g)
                grad = now + shift_up(back, after)
                for p, part in enumerate((n0, n1, n2, n3)):
                    part[at, :] = grad[:, p * SR : (p + 1) * SR]
                return (
                    back[0:1, :],
                    gain_sum + jnp.sum(grad * hat[at, :].astype(F32), axis=0, keepdims=True),
                    bias_sum + jnp.sum(grad, axis=0, keepdims=True),
                    key_sum + jnp.sum(gk * d, axis=0, keepdims=True),
                    gate_sum + jnp.sum(gg * d, axis=0, keepdims=True),
                )

            front, *totals = lax.fori_loop(0, NT, tile, (zero, *totals))
            first_out[r : r + 1, :] = front
            totals[0] = totals[0] + front * (edge[r : r + 1, :] * flag)
            totals[1] = totals[1] + front * flag
        for i in range(4):
            sums[i : i + 1, :] = totals[i]

    grad_hidden, *grad_two, first_two, sums_two = launch(
        channel_backward,
        "s" + "v" * 9 + "h" * 10,
        (
            idx,
            grad_returned,
            grad_returned_other,
            grad_filter,
            active,
            diff_two,
            hat_two,
            hat_edge_two,
            params,
            params_other,
            *hidden_pieces,
            *return_pieces,
        ),
        [((T, FH), BF16)]
        + [((T, SR), F32)] * S
        + [((R, WIDTH), F32), ((4, WIDTH), F32)],
        [
            pltpu.VMEM((WIDTH, NF), BF16),
            pltpu.VMEM((S, FH, SR), BF16),
            pltpu.VMEM((T, WIDTH), F32),
            pltpu.VMEM((T, WIDTH), F32),
            pltpu.SemaphoreType.DMA((5,)),
            pltpu.SemaphoreType.DMA((5,)),
        ],
        after=(return_parts[0],),
    )
    grad_two, first_two, return_state = lax.optimization_barrier(
        (grad_two, first_two, return_state)
    )
    grad_two_other = swap_parts(grad_two)
    first_two_own = along_ctx(first_two, -1, False)
    first_two_other = along_ctx(first_two, -1, True)

    def sweep_again(*refs):
        inputs, (gated, out, *saved, starts) = refs[:7], refs[7:]
        sweep(*inputs, gated, out, starts, saved)

    gated, mixed_out, part_old, part_new, keep, fresh, nums, dens, fade = launch(
        sweep_again,
        "v" * 7,
        (key, value, opened, fading, bonus, states, hold(entering, grad_returned_other)),
        [((T, H), BF16), ((G, T, 128), F32)]
        + [((T, H), F32)] * 6
        + [((G, R * CHUNKS, 128), F32)],
        [pltpu.VMEM((G, 3 * R * CHUNKS, 128), F32)],
    )

    mixed_key, mixed_value, mixed_gate, hat_one, diff_one, root_one, _ = mixes(
        *hold((x_own, x_other), grad_returned_other)
    )

    part = NF // 2
    hidden_parts = weight_grads(
        [[channel_key], [channel_gate]],
        [grad_hidden, grad_filter],
        [
            (0, 0, 0, part, 0, 0),
            (0, 0, part, FH - part, 1, 0),
            (1, 1, 0, H, 1, FH - part),
        ],
        after=(gated, root_one,),
    )
    hidden_state = square_start(*hidden_parts)
    return_turn = square_turn(return_state)
    return_cross = square_cross(*return_turn)

    def middle_backward(
        idx, m0, m1, m2, m3, t0, t1, t2, t3, e_own, e_other, hat, root, po, pp, uo, upp, opened, out,
        part_old, keep, fade, p0, p1, p2, p3, p4,
        grad_mid, grad_own, grad_res, grad_gate, adjoint, entry, w, gates, sems,
    ):
        copies = place_rows(idx, [p0, p1, p2, p3, p4], w, sems, 3 * H, 4 * H)
        begin(copies)
        gain = both(po, pp, 5)
        tail = e_own[...] + swapped(e_other[...])
        row = lax.broadcasted_iota(jnp.int32, (TB, 1), 0)
        for r in range(R):

            def tile(i, carry):
                at = rows_at(r, i)
                is_last = jnp.where((row == TB - 1) & (i == NT - 1), 1.0, 0.0).astype(F32)
                grad = columns((m0, m1, m2, m3), at) + columns((t0, t1, t2, t3), at)
                grad = grad + is_last * tail[r : r + 1, :]
                n = hat[at, :].astype(F32)
                scaled = grad * gain
                mean_one = jnp.sum(scaled, axis=-1, keepdims=True) * (1.0 / WIDTH)
                mean_two = jnp.sum(scaled * n, axis=-1, keepdims=True) * (1.0 / WIDTH)
                up = jnp.concatenate([uo[at, :], upp[at, :]], axis=1).astype(F32)
                full = live_rows(idx, r, i) * up + root[at, :] * (scaled - mean_one - n * mean_two)
                grad_mid[at, :] = full.astype(BF16)
                grad_own[at, :] = full[:, :H]
                return carry

            lax.fori_loop(0, NT, tile, 0)
        finish(copies)
        gates[...] = dot(grad_mid[...], w[...])
        for r in range(R):

            def gate_tile(i, carry):
                at = rows_at(r, i)
                g, s = gates[at, :], opened[at, :]
                put(grad_res, at, g * s)
                grad_gate[at, :] = (g * get(out, at) * s * (1.0 - s)).astype(BF16)
                return carry

            lax.fori_loop(0, NT, gate_tile, 0)

        def step(j, carry):
            t = ST - 1 - j
            new = []
            for r in range(R):
                alpha, beta = carry[r]
                at = scan_rows(r, t)
                direct = part_old[at, :] * get(grad_res, step_rows(r, t))
                a = keep[at, :]
                new.append(
                    (direct + a * alpha, a * beta - direct * get(out, step_rows(r, t)))
                )
            return tuple(new)

        zero = jnp.zeros((CHUNKS, H), F32)
        ends = lax.fori_loop(0, ST, step, ((zero, zero),) * R)
        for r in range(R):
            for k in range(2):
                put(adjoint, pl.ds((k * R + r) * CHUNKS, CHUNKS), ends[r][k])
        alpha = beta = jnp.zeros((R, H), F32)
        span = jnp.ones((R, H), F32)
        for i in range(CHUNKS - 1, -1, -1):
            f = get(fade, chunk_rows(0, i))
            alpha = get(adjoint, chunk_rows(0, i)) + f * alpha
            beta = get(adjoint, chunk_rows(1, i)) + f * beta
            span = span * f
        entry[pl.ds(0, R), :] = alpha
        entry[pl.ds(R, R), :] = beta
        entry[pl.ds(2 * R, R), :] = span

    grad_mid, grad_mid_own, grad_res, grad_gate, adjoint, entry = launch(
        middle_backward,
        "s" + "v" * 21 + "h" * 5,
        (
            idx,
            *grad_two,
            *grad_two_other,
            first_two_own,
            first_two_other,
            hat_two,
            root_two,
            params,
            params_other,
            up_own,
            up_other,
            opened,
            mixed_out,
            part_old,
            keep,
            fade,
            *time_pieces,
        ),
        [
            ((T, WIDTH), BF16),
            ((T, H), F32),
            ((G, T, 128), F32),
            ((T, H), BF16),
            ((G, 2 * R * CHUNKS, 128), F32),
            ((3 * R, H), F32),
        ],
        [
            pltpu.VMEM((WIDTH, H), BF16),
            pltpu.VMEM((T, H), F32),
            pltpu.SemaphoreType.DMA((5,)),
        ],
        after=(hidden_parts[1], return_turn[0], return_turn[2],),
    )

    def no_adjoint():
        zero = jnp.zeros((R, H), F32)
        return (zero, zero, zero + 1.0)

    def join_adjoints(idx, ld, bit, total, other, before):
        low = (idx[1] >> bit) & 1 == 0

        def follow(near, far):
            return (near[0] + near[2] * far[0], near[1] + near[2] * far[1], near[2] * far[2])

        as_near, as_far, with_other = follow(total, other), follow(other, total), follow(before, other)
        return (
            tuple(jnp.where(low, a, b) for a, b in zip(as_near, as_far)),
            tuple(jnp.where(low, a, b) for a, b in zip(with_other, before)),
        )

    late = scan_rounds(entry, no_adjoint, join_adjoints)

    early_parts = weight_grads(
        [[grad_mid], [mixed_gate]],
        [gated, grad_gate],
        [(0, 0, 0, H, 0, 0), (1, 1, 0, H, 1, 0)],
    )
    early_state = square_start(*early_parts)

    def time_backward(
        idx, res, out, value, part_old, part_new, keep, fresh, nums, dens, fade, adjoint, late,
        ld, gate, diff, hat, edge, po, pp, p0, p1, p2, p3, p4,
        grad_key, grad_value, mine_own, s0, s1, stats, first_out, sums, sums_own,
        w, dk, dv, gk, gv, gg, starts, sems,
    ):
        copies = place_rows(idx, [p0, p1, p2, p3, p4], w, sems, 0, 3 * H)
        begin(copies)
        late_now = (late[pl.ds(0, R), :], late[pl.ds(R, R), :])
        for i in range(CHUNKS - 1, -1, -1):
            for k in range(2):
                put(starts, chunk_rows(k, i), late_now[k])
            f = get(fade, chunk_rows(0, i))
            late_now = tuple(get(adjoint, chunk_rows(k, i)) + f * late_now[k] for k in range(2))

        def step(j, carry):
            t = ST - 1 - j
            adj, fade_sum, bonus_sum = carry
            new = []
            for r in range(R):
                alpha, beta = adj[r]
                at, spread = scan_rows(r, t), step_rows(r, t)
                g, y, v = get(res, spread), get(out, spread), get(value, spread)
                b, a = fresh[at, :], keep[at, :]
                near = part_new[at, :] * g
                lift = near * (v - y)
                put(dv, spread, b * alpha + near)
                put(dk, spread, b * (v * alpha + beta) + lift)
                bonus_sum = bonus_sum + lift
                fade_sum = fade_sum - a * (nums[at, :] * alpha + dens[at, :] * beta)
                direct = part_old[at, :] * g
                new.append((direct + a * alpha, a * beta - direct * y))
            return (tuple(new), fade_sum, bonus_sum)

        first_adj = tuple(
            tuple(get(starts, pl.ds((k * R + r) * CHUNKS, CHUNKS)) for k in range(2))
            for r in range(R)
        )
        zero = jnp.zeros((CHUNKS, H), F32)
        _, fade_sum, bonus_sum = lax.fori_loop(0, ST, step, (first_adj, zero, zero))
        sums_own[0:1, :] = jnp.sum(fade_sum, axis=0, keepdims=True) * jnp.exp(ld[...])
        sums_own[1:2, :] = jnp.sum(bonus_sum, axis=0, keepdims=True)
        grad_key[...] = get(dk, EVERY).astype(BF16)
        grad_value[...] = get(dv, EVERY).astype(BF16)
        finish(copies)
        gk[...] = dot_t(grad_key[...], w[:, :H])
        gv[...] = dot_t(grad_value[...], w[:, H : 2 * H])
        gg[...] = dot_t(gate[...], w[:, 2 * H : 3 * H])
        gain = both(po, pp, 0)
        shares = [both(po, pp, i) for i in (2, 3, 4)]
        flag = jnp.where(idx[1] > 0, 1.0, 0.0).astype(F32)
        zero = jnp.zeros((1, WIDTH), F32)
        totals = (zero,) * 5
        lane = lax.broadcasted_iota(jnp.int32, (TB, 128), 1)
        for r in range(R):

            def tile(j, carry):
                after, gain_sum, bias_sum, *mix_sums = carry
                at = rows_at(r, NT - 1 - j)
                grads = (gk[at, :], gv[at, :], gg[at, :])
                d, n = diff[at, :].astype(F32), hat[at, :].astype(F32)
                now = back = None
                for share, grad in zip(shares, grads):
                    a, b = grad * share, grad * (1.0 - share)
                    now = a if now is None else now + a
                    back = b if back is None else back + b
                grad = now + shift_up(back, after)
                mine_own[at, :] = grad[:, :H]
                s0[at, :] = grad[:, H : H + SR]
                s1[at, :] = grad[:, H + SR :]
                scaled = grad * gain
                one = jnp.sum(scaled, axis=-1, keepdims=True)
                two = jnp.sum(scaled * n, axis=-1, keepdims=True)
                stats[at, :] = jnp.where(lane == 0, one, jnp.where(lane == 1, two, 0.0))
                return (
                    back[0:1, :],
                    gain_sum + jnp.sum(grad * n, axis=0, keepdims=True),
                    bias_sum + jnp.sum(grad, axis=0, keepdims=True),
                    *(
                        total + jnp.sum(one_grad * d, axis=0, keepdims=True)
                        for total, one_grad in zip(mix_sums, grads)
                    ),
                )

            front, *totals = lax.fori_loop(0, NT, tile, (zero, *totals))
            first_out[r : r + 1, :] = front
            totals[0] = totals[0] + front * edge[r : r + 1, :]
            totals[1] = totals[1] + front * flag
        for i in range(5):
            sums[i : i + 1, :] = totals[i]

    hidden_turn_out = square_turn(hold(hidden_state, late))
    hidden_cross = square_cross(*hidden_turn_out)
    grad_key, grad_value, one_own, *one_send, first_one, sums_one, sums_own = launch(
        time_backward,
        "s" + "v" * 19 + "h" * 5,
        (
            idx,
            grad_res,
            mixed_out,
            value,
            part_old,
            part_new,
            keep,
            fresh,
            nums,
            dens,
            fade,
            adjoint,
            late,
            fading,
            grad_gate,
            diff_one,
            hat_one,
            hat_edge_one,
            params,
            params_other,
            *time_pieces,
        ),
        [
            ((T, H), BF16),
            ((T, H), BF16),
            ((T, H), F32),
            ((T, SR), F32),
            ((T, SR), F32),
            ((T, 128), F32),
            ((R, WIDTH), F32),
            ((5, WIDTH), F32),
            ((2, H), F32),
        ],
        [pltpu.VMEM((WIDTH, 3 * H), BF16)]
        + [pltpu.VMEM((G, T, 128), F32)] * 2
        + [pltpu.VMEM((T, WIDTH), F32)] * 3
        + [pltpu.VMEM((G, 2 * R * CHUNKS, 128), F32), pltpu.SemaphoreType.DMA((5,))],
        after=(early_parts[1],),
    )
    one_other = [swap(part, "tp", 1) for part in one_send]
    first_one_own = along_ctx(first_one, -1, False)
    first_one_other = along_ctx(first_one, -1, True)

    sums_other = swap(jnp.concatenate([sums_one[:, H:], sums_two[:, H:]], axis=0), "tp", 1)
    late_parts = weight_grads(
        [[mixed_key], [mixed_value]],
        [grad_key, grad_value],
        [(0, 0, 0, H, 0, 0), (1, 1, 0, H, 1, 0)],
        after=(return_cross[1], return_cross[3], hidden_cross[1], hidden_cross[3],),
        riders=(sums_one, sums_two, sums_other, sums_own),
    )
    late_state = square_start(*late_parts)

    return_seen = []
    (return_w,) = scatter_line(
        *square_end(hold(return_cross, first_one_own, first_one_other)), widths=[FH], seen=return_seen
    )
    def input_backward(
        mine, sent, t0, t1, theirs, e_own, e_other, hat, root, po, pp, gm, out
    ):
        gain_full = both(po, pp, 0)
        tail = e_own[...] + swapped(e_other[...])
        row = lax.broadcasted_iota(jnp.int32, (TB, 1), 0)
        for r in range(R):
            weighted = tail[r : r + 1, :] * gain_full
            tail_one = jnp.sum(weighted, axis=-1, keepdims=True)
            tail_two = jnp.sum(
                weighted * hat[(r + 1) * L - TB : (r + 1) * L, :].astype(F32)[TB - 1 :],
                axis=-1,
                keepdims=True,
            )

            def tile(i, carry):
                at = rows_at(r, i)
                is_last = jnp.where((row == TB - 1) & (i == NT - 1), 1.0, 0.0).astype(F32)
                grad = mine[at, :] + columns((t0, t1), at) + is_last * tail[r : r + 1, :H]
                stats = sent[at, :] + theirs[at, :]
                mean_one = (stats[:, 0:1] + is_last * tail_one) * (1.0 / WIDTH)
                mean_two = (stats[:, 1:2] + is_last * tail_two) * (1.0 / WIDTH)
                scaled = grad * gain_full[:, :H]
                out[at, :] = gm[at, :] + root[at, :] * (
                    scaled - mean_one - hat[at, :H].astype(F32) * mean_two
                )
                return carry

            lax.fori_loop(0, NT, tile, 0)

    (input_grad,) = launch(
        input_backward,
        "v" * 12,
        (
            one_own,
            one_send[2],
            *one_other,
            first_one_own,
            first_one_other,
            hat_one,
            root_one,
            params,
            params_other,
            grad_mid_own,
        ),
        [((T, H), F32)],
        after=(late_parts[1],),
    )
    hidden_seen = []
    hidden_w, filter_w = scatter_line(
        *square_end(hidden_cross), widths=[FH, H], seen=hidden_seen
    )
    early_cross = square_cross(*square_turn(hold(early_state, hidden_seen[0], return_seen[-1])))
    late_cross = square_cross(*square_turn(late_state))
    early_seen = []
    output_w, gate_w = scatter_line(*square_end(hold(early_cross, late_cross[1], late_cross[3])), widths=[H, H], behind=hidden_seen[-1], seen=early_seen)
    key_w, value_w, vectors = scatter_line(*square_end(late_cross), widths=[H, H])
    shape = block_entries.shape
    return (
        block_out.reshape(shape),
        input_grad.reshape(shape),
        vectors[0],
        vectors[1],
        vectors[2],
        vectors[3],
        vectors[4],
        vectors[9],
        vectors[10],
        gate_w,
        key_w,
        value_w,
        output_w.T,
        vectors[5],
        vectors[6],
        vectors[7],
        vectors[8],
        hidden_w,
        filter_w,
        return_w.T,
    )


def solution(mesh):
    token = P(None, "shard", "ctx", "tp")
    feature = P("tp")
    rows = P("shard", "tp")
    cols = P("tp", "shard")
    rows_out = P(("shard", "ctx"), "tp")
    cols_out = P("tp", ("shard", "ctx"))
    return jax.shard_map(
        per_device,
        mesh=mesh,
        in_specs=(
            (token, P(None, "shard"), token)
            + (feature,) * 7
            + (rows, rows, rows, cols)
            + (feature,) * 4
            + (rows, rows, cols)
        ),
        out_specs=(
            (token, token)
            + (feature,) * 7
            + (rows_out, rows_out, rows_out, cols_out)
            + (feature,) * 4
            + (rows_out, rows_out, cols_out)
        ),
        check_vma=False,
    )
```

```python
import jax
import jax.numpy as jnp
from jax import lax
from jax.experimental import pallas as pl
from jax.experimental.pallas import tpu as pltpu
from jax.sharding import PartitionSpec as P

F32, BF16 = jnp.float32, jnp.bfloat16
WIDTH = 1024
epsilon = 1e-05
lowest = -1e30
CHUNKS = 8
SPARE = 6 * 2**20

VMEM = pl.BlockSpec(memory_space=pltpu.VMEM)
SMEM = pl.BlockSpec(memory_space=pltpu.SMEM)
HBM = pl.BlockSpec(memory_space=pl.ANY)
KINDS = {"v": VMEM, "s": SMEM, "h": HBM}


def padded_bytes(shape, dtype):
    rows = -(-shape[-2] // 8) * 8
    lanes = -(-shape[-1] // 128) * 128
    size = rows * lanes * jnp.dtype(dtype).itemsize
    for dim in shape[:-2]:
        size *= dim
    return size


def launch(body, kinds, inputs, outs, scratch=(), after=()):
    count = len(kinds)
    room = sum(padded_bytes(x.shape, x.dtype) for x in scratch if len(x.shape) > 1) + SPARE

    def run(*refs):
        body(*refs[:count], *refs[count + len(after) :])

    return pl.pallas_call(
        run,
        out_shape=[
            jax.ShapeDtypeStruct(shape, dtype) for shape, dtype in outs
        ],
        in_specs=[KINDS[kind] for kind in kinds] + [HBM] * len(after),
        out_specs=[VMEM] * len(outs),
        scratch_shapes=list(scratch),
        name=body.__name__,
        compiler_params=pltpu.CompilerParams(vmem_limit_bytes=room),
    )(*inputs, *after)


def side_by_side(*parts):
    widths = [part.shape[1] for part in parts]

    def pack(*refs):
        sources, whole, sems = refs[: len(parts)], refs[-2], refs[-1]
        copies, at = [], 0
        for i, source in enumerate(sources):
            target = whole.at[:, pl.ds(at, widths[i])]
            copies.append(pltpu.make_async_copy(source, target, sems.at[i]))
            at += widths[i]
        begin(copies)
        finish(copies)

    (whole,) = launch(
        pack,
        "h" * len(parts),
        [pltpu.with_memory_space_constraint(part, pltpu.HBM) for part in parts],
        [((parts[0].shape[0], sum(widths)), parts[0].dtype)],
        [pltpu.SemaphoreType.DMA((len(parts),))],
    )
    return whole


def hold(values, *others):
    return lax.optimization_barrier((values, others))[0]


def bits_of(count):
    return count.bit_length() - 1


def swap(value, axis, step):
    size = lax.axis_size(axis)
    return lax.ppermute(value, axis, [(i, i ^ step) for i in range(size)])


def along_ctx(value, step, cross):
    count = lax.axis_size("ctx")
    if not cross:
        pairs = [(i, i + step) for i in range(count) if 0 <= i + step < count]
        return lax.ppermute(value, "ctx", pairs)
    pairs = []
    for i in range(count):
        if 0 <= i + step < count:
            for core in range(2):
                pairs.append((2 * i + core, 2 * (i + step) + 1 - core))
    return lax.ppermute(value, ("ctx", "tp"), pairs)


def gather_first(matrix):
    return swap(matrix, "shard", 1), swap(matrix, "shard", 2)


def gather_turn(across, cut):
    half = across[0].shape[cut] // 2
    return (
        lax.slice_in_dim(across[0], 0, half, axis=cut),
        lax.slice_in_dim(across[1], half, 2 * half, axis=cut),
    )


def gather_cross(turn):
    return swap(turn[0], "shard", 2), swap(turn[1], "shard", 1)


def place_rows(idx, pieces, whole, sems, start=0, stop=None):
    base = idx[0]
    rows, cols = pieces[0].shape
    half = cols // 2
    stop = cols if stop is None else stop

    def spot(step):
        return pl.ds(pl.multiple_of((base ^ step) * rows, rows), rows)

    copies = []
    for step in range(3):
        copies.append((pieces[step].at[:, pl.ds(start, stop - start)], whole.at[spot(step), :]))
    for i in range(2):
        low, high = max(start, i * half), min(stop, (i + 1) * half)
        if low < high:
            source = pieces[3 + i].at[:, pl.ds(low - i * half, high - low)]
            copies.append((source, whole.at[spot(3), pl.ds(low - start, high - low)]))
    return [
        pltpu.make_async_copy(source, target, sems.at[i])
        for i, (source, target) in enumerate(copies)
    ]


def place_blocks(idx, pieces, whole, sems):
    base = idx[0]
    half = pieces[0].shape[0] // 2
    targets = [
        whole.at[base],
        whole.at[base ^ 1],
        whole.at[base ^ 2],
        whole.at[base ^ 3, pl.ds(0, half), :],
        whole.at[base ^ 3, pl.ds(half, half), :],
    ]
    return [
        pltpu.make_async_copy(piece, target, sems.at[i])
        for i, (piece, target) in enumerate(zip(pieces, targets))
    ]


def begin(copies):
    for copy in copies:
        copy.start()


def finish(copies):
    for copy in copies:
        copy.wait()


def dot(left, right):
    return jnp.dot(left, right, preferred_element_type=F32)


def dot_t(left, right):
    return lax.dot_general(left, right, (((1,), (1,)), ((), ())), preferred_element_type=F32)


def norm(values):
    center = jnp.sum(values, axis=-1, keepdims=True) * (1.0 / WIDTH)
    squares = jnp.sum(values * values, axis=-1, keepdims=True) * (1.0 / WIDTH)
    root = lax.rsqrt(squares - center * center + epsilon)
    return (values - center) * root, root


def both(own, other, i):
    return jnp.concatenate([own[i : i + 1, :], other[i : i + 1, :]], axis=1)


def shift_down(values, first):
    row = lax.broadcasted_iota(jnp.int32, values.shape, 0)
    return jnp.where(row == 0, first, pltpu.roll(values, 1, 0))


def shift_up(values, last):
    count = values.shape[0]
    row = lax.broadcasted_iota(jnp.int32, values.shape, 0)
    return jnp.where(row == count - 1, last, pltpu.roll(values, count - 1, 0))


def combine(earlier, later, later_span):
    shifted = earlier[2] - later_span
    high = jnp.maximum(shifted, later[2])
    early = jnp.exp(shifted - high)
    late = jnp.exp(later[2] - high)
    return (earlier[0] * early + later[0] * late, earlier[1] * early + later[1] * late, high)


def get(ref, rows):
    return jnp.concatenate([ref[g, rows, :] for g in range(ref.shape[0])], axis=1)


def put(ref, rows, values):
    for g in range(ref.shape[0]):
        ref[g, rows, :] = values[:, g * 128 : (g + 1) * 128]


def columns(refs, rows):
    return jnp.concatenate([ref[rows, :] for ref in refs], axis=1)


def swap_parts(parts):
    half = len(parts) // 2
    got = [swap(part, "tp", 1) for part in parts]
    return got[half:] + got[:half]


def swapped(values):
    half = values.shape[1] // 2
    return jnp.concatenate([values[:, half:], values[:, :half]], axis=1)


def per_device(
    block_entries,
    row_extents,
    upstream_loss_deriv,
    earlier_layernorm_scaling,
    earlier_layernorm_offset,
    temporal_mix_lookup_fraction,
    temporal_mix_payload_fraction,
    temporal_mix_filter_fraction,
    logarithmic_fading_per_feature,
    present_entry_reward,
    filter_projection,
    lookup_projection,
    payload_projection,
    temporal_mix_emit_projection,
    later_layernorm_scaling,
    later_layernorm_offset,
    feature_mix_lookup_fraction,
    feature_mix_filter_fraction,
    feature_mix_lookup_proj,
    feature_mix_filter_proj,
    feature_mix_payload_proj,
):
    batches, rows_local, L, H = block_entries.shape
    R = batches * rows_local
    T = R * L
    S, C = lax.axis_size("shard"), lax.axis_size("ctx")
    FH = feature_mix_lookup_proj.shape[1]
    ST = L // CHUNKS
    TB = min(32, L)
    NT = L // TB
    G = H // 128
    EVERY = slice(None)
    BLOCKS = S * C
    BR = WIDTH // BLOCKS
    SR = WIDTH // S
    assert S == 4 and WIDTH == 2 * H
    s_at, c_at, t_at = lax.axis_index("shard"), lax.axis_index("ctx"), lax.axis_index("tp")
    idx = jnp.concatenate(
        [
            jnp.stack(
                [s_at ^ (2 * t_at), c_at, (s_at * C + c_at) ^ (t_at * (BLOCKS // 2))]
            ).astype(jnp.int32),
            row_extents.reshape(R).astype(jnp.int32),
        ]
    )

    def rows_at(r, i):
        return pl.ds(pl.multiple_of(r * L + i * TB, TB), TB)

    def scan_rows(r, t):
        return pl.ds(pl.multiple_of((r * ST + t) * CHUNKS, CHUNKS), CHUNKS)

    def step_rows(r, t):
        return pl.ds(r * L + t, CHUNKS, stride=ST)

    def chunk_rows(part, i):
        return pl.ds(part * R * CHUNKS + i, R, stride=CHUNKS)

    x_own = block_entries.reshape(T, H)
    up_own = upstream_loss_deriv.reshape(T, H)
    params = jnp.stack(
        [
            earlier_layernorm_scaling,
            earlier_layernorm_offset,
            temporal_mix_lookup_fraction,
            temporal_mix_payload_fraction,
            temporal_mix_filter_fraction,
            later_layernorm_scaling,
            later_layernorm_offset,
            feature_mix_lookup_fraction,
            feature_mix_filter_fraction,
        ]
    )
    fading = logarithmic_fading_per_feature.reshape(1, H)
    bonus = present_entry_reward.reshape(1, H)
    def pack_time(key_part, value_part, gate_part, emit_part, whole, tall, sems):
        copies = [
            pltpu.make_async_copy(part, whole.at[:, pl.ds(i * H, H)], sems.at[i])
            for i, part in enumerate((key_part, value_part, gate_part))
        ]
        copies.append(pltpu.make_async_copy(emit_part, tall, sems.at[3]))
        begin(copies)
        copies[3].wait()
        whole[:, 3 * H :] = tall[...].astype(F32).T.astype(BF16)
        finish(copies[:3])

    time_parts = (
        lookup_projection, payload_projection, filter_projection, temporal_mix_emit_projection,
    )
    (time_matrix,) = launch(
        pack_time,
        "hhhh",
        [pltpu.with_memory_space_constraint(part, pltpu.HBM) for part in time_parts],
        [((SR, 4 * H), BF16)],
        [pltpu.VMEM((H, SR), BF16), pltpu.SemaphoreType.DMA((4,))],
    )
    time_first = gather_first(time_matrix)
    x_other = swap(x_own, "tp", 1)
    params_other = swap(params, "tp", 1)
    last_rows = [
        part.reshape(batches, rows_local, L, H)[:, :, L - 1, :].reshape(R, H)
        for part in (x_own, x_other)
    ]
    edge = along_ctx(jnp.concatenate(last_rows, axis=1), 1, False)
    up_other = swap(up_own, "tp", 1)

    def mix_time(
        idx, xo, xp, ed, po, pp, mixed_key, mixed_value, mixed_gate, hat, diff, root, hat_edge
    ):
        gain, bias = both(po, pp, 0), both(po, pp, 1)
        shares = [both(po, pp, i) for i in (2, 3, 4)]
        flag = jnp.where(idx[1] > 0, 1.0, 0.0).astype(F32)
        edge_hat, _ = norm(ed[...].astype(F32))
        hat_edge[...] = edge_hat * flag
        first = (edge_hat * gain + bias) * flag
        for r in range(R):

            def tile(i, last):
                at = rows_at(r, i)
                values = jnp.concatenate([xo[at, :], xp[at, :]], axis=1).astype(F32)
                n, q = norm(values)
                normed = n * gain + bias
                prev = shift_down(normed, last)
                hat[at, :] = n.astype(BF16)
                root[at, :] = q
                diff[at, :] = (normed - prev).astype(BF16)
                for share, target in zip(shares, (mixed_key, mixed_value, mixed_gate)):
                    target[at, :] = (normed * share + prev * (1.0 - share)).astype(BF16)
                return normed[TB - 1 : TB, :]

            lax.fori_loop(0, NT, tile, first[r : r + 1, :])

    def mixes(*tokens):
        return launch(
            mix_time,
            "svvvvv",
            (idx, *tokens, edge, params, params_other),
            [((T, WIDTH), BF16)] * 5 + [((T, 1), F32), ((R, WIDTH), F32)],
        )

    mixed_key, mixed_value, mixed_gate, *_, hat_edge_one = mixes(x_own, x_other)
    time_turn = gather_turn(hold(time_first, hat_edge_one), 1)
    time_across = gather_cross(time_turn)
    time_pieces = [time_matrix, *time_first, *time_across]
    hidden_matrix = side_by_side(feature_mix_lookup_proj, feature_mix_filter_proj)
    hidden_first = gather_first(hold(hidden_matrix, time_across))
    return_matrix = hold(feature_mix_payload_proj, time_across)
    return_first = gather_first(return_matrix)
    return_turn_in = gather_turn(return_first, 0)
    return_across = gather_cross(return_turn_in)
    return_pieces = [return_matrix, *return_first, *return_across]

    def project_time(
        idx, mk, mv, mg, ld, p0, p1, p2, p3, p4, key, value, opened, states, closing, w, sems
    ):
        copies = place_rows(idx, [p0, p1, p2, p3, p4], w, sems, 0, 3 * H)
        begin(copies)
        finish(copies)
        put(key, EVERY, dot(mk[...], w[:, :H]))
        put(value, EVERY, dot(mv[...], w[:, H : 2 * H]))
        rate = jnp.exp(ld[...])

        def step(t, carry):
            new = []
            for r in range(R):
                num, den, high = carry[r]
                k_now, v_now = get(key, step_rows(r, t)), get(value, step_rows(r, t))
                faded = high - rate
                top = jnp.maximum(faded, k_now)
                old, fresh = jnp.exp(faded - top), jnp.exp(k_now - top)
                new.append((old * num + fresh * v_now, old * den + fresh, top))
            return tuple(new)

        zero = jnp.zeros((CHUNKS, H), F32)
        ends = lax.fori_loop(0, ST, step, ((zero, zero, zero + lowest),) * R)
        for r in range(R):
            for part in range(3):
                put(states, pl.ds((part * R + r) * CHUNKS, CHUNKS), ends[r][part])
        total = tuple(get(states, chunk_rows(part, 0)) for part in range(3))
        for i in range(1, CHUNKS):
            total = combine(
                total, tuple(get(states, chunk_rows(part, i)) for part in range(3)), ST * rate
            )
        for part in range(3):
            closing[pl.ds(part * R, R), :] = total[part]
        opened[...] = jax.nn.sigmoid(dot(mg[...], w[:, 2 * H : 3 * H]))

    key, value, opened, states, closing = launch(
        project_time,
        "svvvv" + "h" * 5,
        (idx, mixed_key, mixed_value, mixed_gate, fading, *time_pieces),
        [((G, T, 128), F32)] * 2
        + [((T, H), F32), ((G, 3 * R * CHUNKS, 128), F32), ((3 * R, H), F32)],
        [pltpu.VMEM((WIDTH, 3 * H), BF16), pltpu.SemaphoreType.DMA((5,))],
        after=(up_other,),
    )

    def parts_of(ref):
        return tuple(ref[pl.ds(part * R, R), :] for part in range(3))

    def put_parts(ref, values):
        for part in range(3):
            ref[pl.ds(part * R, R), :] = values[part]

    def scan_rounds(first_total, empty, join):
        total, so_far = first_total, None
        for bit in range(bits_of(C)):
            other = swap(total, "ctx", 1 << bit)
            last = bit + 1 == bits_of(C)

            def join_round(idx, ld, total, other, *refs):
                if so_far is None:
                    before = empty()
                else:
                    before, refs = parts_of(refs[0]), refs[1:]
                new_total, new_before = join(
                    idx, ld, bit, parts_of(total), parts_of(other), before
                )
                put_parts(refs[0], new_before)
                if not last:
                    put_parts(refs[1], new_total)

            inputs = [idx, fading, total, other] + ([] if so_far is None else [so_far])
            so_far, *rest = launch(
                join_round, "s" + "v" * (len(inputs) - 1), inputs, [((3 * R, H), F32)] * (2 - last)
            )
            total = None if last else rest[0]
        return so_far

    def no_state():
        zero = jnp.zeros((R, H), F32)
        return (zero, zero, zero + lowest)

    def join_states(idx, ld, bit, total, other, before):
        up = (idx[1] >> bit) & 1 == 1
        rate = jnp.exp(ld[...])
        span = rate * float(L << bit)
        passed = (L * (idx[1] & ((1 << bit) - 1))).astype(F32)
        with_other = combine(other, before, rate * passed)
        as_later, as_earlier = combine(other, total, span), combine(total, other, span)
        return (
            tuple(jnp.where(up, a, b) for a, b in zip(as_later, as_earlier)),
            tuple(jnp.where(up, a, b) for a, b in zip(with_other, before)),
        )

    entering = scan_rounds(closing, no_state, join_states)

    hidden_turn = gather_turn(hold(hidden_first, entering), 1)
    hidden_across = gather_cross(hidden_turn)
    hidden_pieces = [hidden_matrix, *hidden_first, *hidden_across]

    def sweep(key, value, opened, ld, un, states, enter, gated, out, starts, saved=None):
        rate = jnp.exp(ld[...])
        reward = un[...]
        state = tuple(enter[pl.ds(part * R, R), :] for part in range(3))
        for i in range(CHUNKS):
            for part in range(3):
                put(starts, chunk_rows(part, i), state[part])
            state = combine(
                state, tuple(get(states, chunk_rows(part, i)) for part in range(3)), ST * rate
            )

        def step(t, carry):
            new = []
            for r in range(R):
                num, den, high = carry[r]
                k_now, v_now = get(key, step_rows(r, t)), get(value, step_rows(r, t))
                at = scan_rows(r, t)
                now = reward + k_now
                top = jnp.maximum(high, now)
                e_old, e_new = jnp.exp(high - top), jnp.exp(now - top)
                inverse = 1.0 / (e_old * den + e_new)
                e_old, e_new = e_old * inverse, e_new * inverse
                put(out, step_rows(r, t), e_old * num + e_new * v_now)
                if saved:
                    part_old, part_new, keep, fresh, nums, dens, fade = saved
                    part_old[at, :] = e_old
                    part_new[at, :] = e_new
                    nums[at, :] = num
                    dens[at, :] = den
                faded = high - rate
                peak = jnp.maximum(faded, k_now)
                a, b = jnp.exp(faded - peak), jnp.exp(k_now - peak)
                if saved:
                    keep[at, :] = a
                    fresh[at, :] = b
                new.append((a * num + b * v_now, a * den + b, peak))
            return tuple(new)

        begin_at = tuple(
            tuple(get(starts, pl.ds((part * R + r) * CHUNKS, CHUNKS)) for part in range(3))
            for r in range(R)
        )
        ends = lax.fori_loop(0, ST, step, begin_at)
        if saved:
            for r in range(R):
                put(
                    saved[-1],
                    pl.ds(r * CHUNKS, CHUNKS),
                    jnp.exp(begin_at[r][2] - ST * rate - ends[r][2]),
                )
        gated[...] = (opened[...] * get(out, EVERY)).astype(BF16)

    def sweep_time(
        idx, key, value, opened, ld, un, states, enter, p0, p1, p2, p3, p4,
        e0, e1, e2, e3, gated, out, starts, w, sems,
    ):
        copies = place_rows(idx, [p0, p1, p2, p3, p4], w, sems, 3 * H, 4 * H)
        begin(copies)
        sweep(key, value, opened, ld, un, states, enter, gated, out, starts)
        finish(copies)
        for p, part in enumerate((e0, e1, e2, e3)):
            part[...] = dot_t(gated[...], w[p * SR : (p + 1) * SR, :])

    emitted = launch(
        sweep_time,
        "s" + "v" * 7 + "h" * 5,
        (idx, key, value, opened, fading, bonus, states, entering, *time_pieces),
        [((T, SR), F32)] * S,
        [
            pltpu.VMEM((T, H), BF16),
            pltpu.VMEM((G, T, 128), F32),
            pltpu.VMEM((G, 3 * R * CHUNKS, 128), F32),
            pltpu.VMEM((WIDTH, H), BF16),
            pltpu.SemaphoreType.DMA((5,)),
        ],
        after=hidden_turn,
    )
    emitted_other = swap_parts(emitted)

    def middle_norm(xo, xp, *refs):
        mine, theirs, (middle, hat, root, last) = refs[:S], refs[S : 2 * S], refs[2 * S :]
        for r in range(R):

            def tile(i, carry):
                at = rows_at(r, i)
                values = jnp.concatenate([xo[at, :], xp[at, :]], axis=1).astype(F32)
                values = values + (columns(mine, at) + columns(theirs, at))
                n, q = norm(values)
                middle[at, :] = values[:, :H]
                hat[at, :] = n
                root[at, :] = q
                return n[TB - 1 : TB, :]

            last[r : r + 1, :] = lax.fori_loop(0, NT, tile, jnp.zeros((1, WIDTH), F32))

    middle, hat_two, root_two, hat_last = launch(
        middle_norm,
        "vv" + "v" * (2 * S),
        (x_own, x_other, *emitted, *emitted_other),
        [((T, H), F32), ((T, WIDTH), F32), ((T, 1), F32), ((R, WIDTH), F32)],
        after=return_turn_in,
    )
    hat_edge_two = along_ctx(hat_last, 1, False)
    NF = FH + H
    NB = min(512, FH)

    def channel_forward(
        idx, hat, edge, po, pp, h0, h1, h2, h3, h4,
        ckey, cgate, diff, hat_low, active, squared, opened, wh, sems_h,
    ):
        copies_h = place_rows(idx, [h0, h1, h2, h3, h4], wh, sems_h)
        begin(copies_h)
        gain, bias = both(po, pp, 5), both(po, pp, 6)
        shares = [both(po, pp, i) for i in (7, 8)]
        flag = jnp.where(idx[1] > 0, 1.0, 0.0).astype(F32)
        first = (edge[...] * gain + bias) * flag
        for r in range(R):

            def tile(i, last):
                at = rows_at(r, i)
                n = hat[at, :]
                hat_low[at, :] = n.astype(BF16)
                normed = n * gain + bias
                prev = shift_down(normed, last)
                diff[at, :] = (normed - prev).astype(BF16)
                for share, target in zip(shares, (ckey, cgate)):
                    target[at, :] = (normed * share + prev * (1.0 - share)).astype(BF16)
                return normed[TB - 1 : TB, :]

            lax.fori_loop(0, NT, tile, first[r : r + 1, :])
        finish(copies_h)
        for n in range(0, FH, NB):
            pre = jnp.maximum(dot(ckey[...], wh[:, n : n + NB]), 0.0)
            active[:, n : n + NB] = pre.astype(BF16)
            squared[:, n : n + NB] = (pre * pre).astype(BF16)
        opened[...] = jax.nn.sigmoid(dot(cgate[...], wh[:, FH:NF]))

    channel_key, channel_gate, diff_two, hat_two, active, squared, filter_open = launch(
        channel_forward,
        "svvvv" + "h" * 5,
        (idx, hat_two, hat_edge_two, params, params_other, *hidden_pieces),
        [((T, WIDTH), BF16)] * 4 + [((T, FH), BF16)] * 2 + [((T, H), F32)],
        [pltpu.VMEM((WIDTH, NF), BF16), pltpu.SemaphoreType.DMA((5,))],
    )

    def channel_return(idx, squared, r0, r1, r2, r3, r4, *rest):
        parts, (wr, sems_r) = rest[:S], rest[S:]
        copies_r = place_blocks(idx, [r0, r1, r2, r3, r4], wr, sems_r)
        begin(copies_r)
        finish(copies_r)
        for p in range(S):
            parts[p][...] = dot(squared[...], wr[p]).astype(parts[p].dtype)

    returned = launch(
        channel_return,
        "sv" + "h" * 5,
        (idx, squared, *return_pieces),
        [((T, SR), F32)] * (S // 2) + [((T, SR), BF16)] * (S // 2),
        [pltpu.VMEM((S, FH, SR), BF16), pltpu.SemaphoreType.DMA((5,))],
    )
    ret_keep = returned[: S // 2]
    ret_other = [swap(part, "tp", 1) for part in returned[S // 2 :]]

    def live_rows(idx, r, i):
        at = lax.broadcasted_iota(jnp.int32, (TB, 1), 0) + (idx[1] * L + i * TB)
        return jnp.where(at < idx[3 + r], 1.0, 0.0).astype(F32)

    def close_block(idx, m0, m1, t0, t1, opened, middle, up, out, grad_ret, grad_fil):
        for r in range(R):

            def tile(i, carry):
                at = rows_at(r, i)
                live = live_rows(idx, r, i)
                returned = columns((m0, m1), at) + columns((t0, t1), at).astype(F32)
                s = opened[at, :]
                out[at, :] = (live * (middle[at, :] + s * returned)).astype(BF16)
                grad = live * up[at, :].astype(F32)
                grad_ret[at, :] = (grad * s).astype(BF16)
                grad_fil[at, :] = (grad * returned * s * (1.0 - s)).astype(BF16)
                return carry

            lax.fori_loop(0, NT, tile, 0)

    block_out, grad_returned, grad_filter = launch(
        close_block,
        "svvvvvvv",
        (idx, *ret_keep, *ret_other, filter_open, middle, up_own),
        [((T, H), BF16), ((T, H), BF16), ((T, H), BF16)],
    )
    grad_returned_other = swap(grad_returned, "tp", 1)

    order = []
    for spot in range(BLOCKS):
        high, low = spot // C, spot % C
        turned = 0
        for bit in range(bits_of(C)):
            turned = turned * 2 + ((low >> bit) & 1)
        order.append(high * C + turned)

    VR = 16

    def weight_grads(lefts, rights, jobs, after=(), riders=()):
        count_left = [len(group) for group in lefts]
        flat = [ref for group in lefts for ref in group]
        width = sum(job[3] for job in jobs if job[4] == 0)
        half, quarter = WIDTH // 2, WIDTH // 4

        def weight_products(idx, *refs):
            left_refs, refs = list(refs[: len(flat)]), refs[len(flat) :]
            right_refs, refs = refs[: len(rights)], refs[len(rights) :]
            rider_refs, refs = refs[: len(riders)], refs[len(riders) :]
            send_a, keep_a, send_b, keep_b, *mine, tall, turned = refs
            if riders:
                one, two, other, own = rider_refs
                total = mine[0]
                total[...] = jnp.zeros((VR, H), F32)
                total[0:5, :] = one[:, :H] + other[0:5, :]
                total[5:9, :] = two[:, :H] + other[5:9, :]
                total[9:11, :] = own[...]
                total[...] = write_pair(send_a, half, total[...])
            for g, count in enumerate(count_left):
                group, left_refs = left_refs[:count], left_refs[count:]
                row = 0
                for ref in group:
                    for lane in range(0, ref.shape[1], 128):
                        tall[row : row + 128, :] = ref[:, lane : lane + 128].astype(F32).T
                        row += 128
                for spot in range(BLOCKS):
                    block = order[spot] ^ idx[2]
                    turned[spot * BR : (spot + 1) * BR, :] = tall[
                        pl.ds(pl.multiple_of(block * BR, BR), BR), :
                    ].astype(BF16)
                for left, right, start, size, part, at in jobs:
                    if left != g:
                        continue
                    for n in range(0, size, 256):
                        to = slice(at + n, at + n + 256)
                        acc = dot(
                            turned[...], right_refs[right][:, start + n : start + n + 256]
                        ).astype(BF16)
                        if part == 0:
                            keep_a[:quarter, to] = acc[:quarter]
                            send_a[:quarter, to] = acc[quarter:half]
                            keep_a[quarter:, to] = acc[half : half + quarter]
                            send_a[quarter:half, to] = acc[half + quarter :]
                        else:
                            keep_b[:, to] = acc[:half]
                            send_b[:, to] = acc[half:]

        extra = 2 * VR if riders else 0
        return launch(
            weight_products,
            "s" + "v" * (len(flat) + len(rights) + len(riders)),
            (idx, *flat, *rights, *riders),
            [((half + extra, width), BF16)]
            + [((half, width), BF16)] * 3
            + ([((VR, H), F32)] if riders else []),
            [pltpu.VMEM((WIDTH, T), F32), pltpu.VMEM((WIDTH, T), BF16)],
            after=after,
        )

    def write_pair(ref, row, values):
        high = values.astype(BF16)
        low = (values - high.astype(F32)).astype(BF16)
        ref[row : row + VR, :H] = high
        ref[row + VR :, :H] = low
        if ref.shape[1] > H:
            ref[row:, H:] = jnp.zeros((2 * VR, ref.shape[1] - H), BF16)
        return high.astype(F32) + low.astype(F32)

    def read_pair(ref, row):
        return ref[row : row + VR, :H].astype(F32) + ref[row + VR :, :H].astype(F32)

    def add(mine, theirs):
        return mine.astype(F32) + theirs.astype(F32)

    def square_start(send_a, keep_a, send_b, keep_b, *mine):
        return [keep_a, swap(send_a, "shard", 1), keep_b, swap(send_b, "shard", 2), *mine]

    def square_turn(state):
        rows, width = state[0].shape
        half = rows // 2
        extra = 2 * VR if len(state) > 4 else 0

        def turn_square(keep_a, got_a, keep_b, got_b, *refs):
            if extra:
                mine, refs = refs[0], refs[1:]
            send_a, new_a, send_b, new_b, *total = refs
            low, high = slice(0, half), slice(half, rows)
            new_a[...] = add(keep_a[low, :], got_a[low, :]).astype(BF16)
            send_a[:half, :] = add(keep_a[high, :], got_a[high, :]).astype(BF16)
            new_b[...] = add(keep_b[low, :], got_b[low, :]).astype(BF16)
            send_b[...] = add(keep_b[high, :], got_b[high, :]).astype(BF16)
            if extra:
                total[0][...] = write_pair(send_a, half, mine[...] + read_pair(got_a, rows))

        return launch(
            turn_square,
            "v" * len(state),
            state,
            [((half + extra, width), BF16)]
            + [((half, width), BF16)] * 3
            + ([((VR, H), F32)] if extra else []),
        )

    def square_cross(send_a, keep_a, send_b, keep_b, *mine):
        return [keep_a, swap(send_a, "shard", 2), keep_b, swap(send_b, "shard", 1), *mine]

    def square_end(state):
        rows, width = state[0].shape
        half = rows // 2
        extra = 2 * VR if len(state) > 4 else 0

        def end_square(keep_a, got_a, keep_b, got_b, *refs):
            if extra:
                mine, refs = refs[0], refs[1:]
            send, new, *total = refs
            for part, (keep, got) in enumerate(((keep_a, got_a), (keep_b, got_b))):
                at = slice(part * width, (part + 1) * width)
                new[:, at] = add(keep[:half, :], got[:half, :]).astype(BF16)
                send[:half, at] = add(keep[half:, :], got[half:rows, :]).astype(BF16)
            if extra:
                total[0][...] = write_pair(send, half, mine[...] + read_pair(got_a, rows))

        return launch(
            end_square,
            "v" * len(state),
            state,
            [((half + extra, 2 * width), BF16), ((half, 2 * width), BF16)]
            + ([((VR, H), F32)] if extra else []),
        )

    def scatter_line(send, keep, *mine, widths, seen=None, behind=None):
        extra = 2 * VR if mine else 0
        for bit in range(bits_of(C)):
            if behind is not None and bit + 1 == bits_of(C):
                send = hold(send, behind)
            got = swap(send, "ctx", 1 << bit)
            if seen is not None:
                seen.append(got)
            rows, width = keep.shape
            last = bit + 1 == bits_of(C)
            half = rows if last else rows // 2

            def turn_line(keep, got, *refs):
                if extra:
                    own, refs = refs[0], refs[1:]
                if last:
                    news, refs = refs[: len(widths)], refs[len(widths) :]
                    at = 0
                    for new, size in zip(news, widths):
                        new[...] = add(keep[:, at : at + size], got[:rows, at : at + size])
                        at += size
                else:
                    new, send, *refs = refs
                    new[...] = add(keep[:half, :], got[:half, :]).astype(BF16)
                    send[:half, :] = add(keep[half:, :], got[half:rows, :]).astype(BF16)
                if extra:
                    total = own[...] + read_pair(got, rows)
                    if last:
                        for i, ref in enumerate(refs):
                            ref[...] = total[i : i + 1, :]
                    else:
                        refs[0][...] = write_pair(send, half, total)

            if last:
                outs = [((rows, size), F32) for size in widths]
            else:
                outs = [((half, width), BF16), ((half + extra, width), BF16)]
            if extra:
                outs += [((1, H), F32)] * 11 if last else [((VR, H), F32)]
            result = launch(turn_line, "v" * (2 + len(mine)), (keep, got, *mine), outs)
            if not last:
                keep, send, *mine = result
        return result

    return_parts = weight_grads(
        [[grad_returned, grad_returned_other]],
        [squared],
        [(0, 0, 0, FH // 2, 0, 0), (0, 0, FH // 2, FH // 2, 1, 0)],
    )
    return_state = square_start(*return_parts)

    def channel_backward(
        idx, gro, grp, gf, active, diff, hat, edge, po, pp,
        h0, h1, h2, h3, h4, r0, r1, r2, r3, r4,
        grad_hidden, n0, n1, n2, n3, first_out, sums, wh, wr, ckey, cgate, sems_h, sems_r,
    ):
        copies_h = place_rows(idx, [h0, h1, h2, h3, h4], wh, sems_h)
        copies_r = place_blocks(idx, [r0, r1, r2, r3, r4], wr, sems_r)
        begin(copies_r)
        begin(copies_h)
        finish(copies_r)
        half = S // 2
        for n in range(0, FH, NB):
            acc = None
            for p in range(S):
                source = gro if p < half else grp
                at = (p % half) * SR
                term = dot_t(source[:, at : at + SR], wr[p, n : n + NB, :])
                acc = term if acc is None else acc + term
            grad_hidden[:, n : n + NB] = (
                acc * 2.0 * active[:, n : n + NB].astype(F32)
            ).astype(BF16)
        finish(copies_h)
        for p in range(S):
            at = slice(p * SR, (p + 1) * SR)
            ckey[:, at] = dot_t(grad_hidden[...], wh[at, :FH])
            cgate[:, at] = dot_t(gf[...], wh[at, FH:NF])
        share_k, share_g = both(po, pp, 7), both(po, pp, 8)
        flag = jnp.where(idx[1] > 0, 1.0, 0.0).astype(F32)
        zero = jnp.zeros((1, WIDTH), F32)
        totals = (zero, zero, zero, zero)
        for r in range(R):

            def tile(j, carry):
                after, gain_sum, bias_sum, key_sum, gate_sum = carry
                at = rows_at(r, NT - 1 - j)
                gk, gg, d = ckey[at, :], cgate[at, :], diff[at, :].astype(F32)
                now = gk * share_k + gg * share_g
                back = gk * (1.0 - share_k) + gg * (1.0 - share_g)
                grad = now + shift_up(back, after)
                for p, part in enumerate((n0, n1, n2, n3)):
                    part[at, :] = grad[:, p * SR : (p + 1) * SR]
                return (
                    back[0:1, :],
                    gain_sum + jnp.sum(grad * hat[at, :].astype(F32), axis=0, keepdims=True),
                    bias_sum + jnp.sum(grad, axis=0, keepdims=True),
                    key_sum + jnp.sum(gk * d, axis=0, keepdims=True),
                    gate_sum + jnp.sum(gg * d, axis=0, keepdims=True),
                )

            front, *totals = lax.fori_loop(0, NT, tile, (zero, *totals))
            first_out[r : r + 1, :] = front
            totals[0] = totals[0] + front * (edge[r : r + 1, :] * flag)
            totals[1] = totals[1] + front * flag
        for i in range(4):
            sums[i : i + 1, :] = totals[i]

    grad_hidden, *grad_two, first_two, sums_two = launch(
        channel_backward,
        "s" + "v" * 9 + "h" * 10,
        (
            idx,
            grad_returned,
            grad_returned_other,
            grad_filter,
            active,
            diff_two,
            hat_two,
            hat_edge_two,
            params,
            params_other,
            *hidden_pieces,
            *return_pieces,
        ),
        [((T, FH), BF16)]
        + [((T, SR), F32)] * S
        + [((R, WIDTH), F32), ((4, WIDTH), F32)],
        [
            pltpu.VMEM((WIDTH, NF), BF16),
            pltpu.VMEM((S, FH, SR), BF16),
            pltpu.VMEM((T, WIDTH), F32),
            pltpu.VMEM((T, WIDTH), F32),
            pltpu.SemaphoreType.DMA((5,)),
            pltpu.SemaphoreType.DMA((5,)),
        ],
        after=(return_parts[0],),
    )
    grad_two, first_two, return_state = lax.optimization_barrier(
        (grad_two, first_two, return_state)
    )
    grad_two_other = swap_parts(grad_two)
    first_two_own = along_ctx(first_two, -1, False)
    first_two_other = along_ctx(first_two, -1, True)

    def sweep_again(*refs):
        inputs, (gated, out, *saved, starts) = refs[:7], refs[7:]
        sweep(*inputs, gated, out, starts, saved)

    gated, mixed_out, part_old, part_new, keep, fresh, nums, dens, fade = launch(
        sweep_again,
        "v" * 7,
        (key, value, opened, fading, bonus, states, hold(entering, grad_returned_other)),
        [((T, H), BF16), ((G, T, 128), F32)]
        + [((T, H), F32)] * 6
        + [((G, R * CHUNKS, 128), F32)],
        [pltpu.VMEM((G, 3 * R * CHUNKS, 128), F32)],
    )

    mixed_key, mixed_value, mixed_gate, hat_one, diff_one, root_one, _ = mixes(
        *hold((x_own, x_other), grad_returned_other)
    )

    part = NF // 2
    hidden_parts = weight_grads(
        [[channel_key], [channel_gate]],
        [grad_hidden, grad_filter],
        [
            (0, 0, 0, part, 0, 0),
            (0, 0, part, FH - part, 1, 0),
            (1, 1, 0, H, 1, FH - part),
        ],
        after=(gated, root_one,),
    )
    hidden_state = square_start(*hidden_parts)
    return_turn = square_turn(return_state)
    return_cross = square_cross(*return_turn)

    def middle_backward(
        idx, m0, m1, m2, m3, t0, t1, t2, t3, e_own, e_other, hat, root, po, pp, uo, upp, opened, out,
        part_old, keep, fade, p0, p1, p2, p3, p4,
        grad_mid, grad_own, grad_res, grad_gate, adjoint, entry, w, gates, sems,
    ):
        copies = place_rows(idx, [p0, p1, p2, p3, p4], w, sems, 3 * H, 4 * H)
        begin(copies)
        gain = both(po, pp, 5)
        tail = e_own[...] + swapped(e_other[...])
        row = lax.broadcasted_iota(jnp.int32, (TB, 1), 0)
        for r in range(R):

            def tile(i, carry):
                at = rows_at(r, i)
                is_last = jnp.where((row == TB - 1) & (i == NT - 1), 1.0, 0.0).astype(F32)
                grad = columns((m0, m1, m2, m3), at) + columns((t0, t1, t2, t3), at)
                grad = grad + is_last * tail[r : r + 1, :]
                n = hat[at, :].astype(F32)
                scaled = grad * gain
                mean_one = jnp.sum(scaled, axis=-1, keepdims=True) * (1.0 / WIDTH)
                mean_two = jnp.sum(scaled * n, axis=-1, keepdims=True) * (1.0 / WIDTH)
                up = jnp.concatenate([uo[at, :], upp[at, :]], axis=1).astype(F32)
                full = live_rows(idx, r, i) * up + root[at, :] * (scaled - mean_one - n * mean_two)
                grad_mid[at, :] = full.astype(BF16)
                grad_own[at, :] = full[:, :H]
                return carry

            lax.fori_loop(0, NT, tile, 0)
        finish(copies)
        gates[...] = dot(grad_mid[...], w[...])
        for r in range(R):

            def gate_tile(i, carry):
                at = rows_at(r, i)
                g, s = gates[at, :], opened[at, :]
                put(grad_res, at, g * s)
                grad_gate[at, :] = (g * get(out, at) * s * (1.0 - s)).astype(BF16)
                return carry

            lax.fori_loop(0, NT, gate_tile, 0)

        def step(j, carry):
            t = ST - 1 - j
            new = []
            for r in range(R):
                alpha, beta = carry[r]
                at = scan_rows(r, t)
                direct = part_old[at, :] * get(grad_res, step_rows(r, t))
                a = keep[at, :]
                new.append(
                    (direct + a * alpha, a * beta - direct * get(out, step_rows(r, t)))
                )
            return tuple(new)

        zero = jnp.zeros((CHUNKS, H), F32)
        ends = lax.fori_loop(0, ST, step, ((zero, zero),) * R)
        for r in range(R):
            for k in range(2):
                put(adjoint, pl.ds((k * R + r) * CHUNKS, CHUNKS), ends[r][k])
        alpha = beta = jnp.zeros((R, H), F32)
        span = jnp.ones((R, H), F32)
        for i in range(CHUNKS - 1, -1, -1):
            f = get(fade, chunk_rows(0, i))
            alpha = get(adjoint, chunk_rows(0, i)) + f * alpha
            beta = get(adjoint, chunk_rows(1, i)) + f * beta
            span = span * f
        entry[pl.ds(0, R), :] = alpha
        entry[pl.ds(R, R), :] = beta
        entry[pl.ds(2 * R, R), :] = span

    grad_mid, grad_mid_own, grad_res, grad_gate, adjoint, entry = launch(
        middle_backward,
        "s" + "v" * 21 + "h" * 5,
        (
            idx,
            *grad_two,
            *grad_two_other,
            first_two_own,
            first_two_other,
            hat_two,
            root_two,
            params,
            params_other,
            up_own,
            up_other,
            opened,
            mixed_out,
            part_old,
            keep,
            fade,
            *time_pieces,
        ),
        [
            ((T, WIDTH), BF16),
            ((T, H), F32),
            ((G, T, 128), F32),
            ((T, H), BF16),
            ((G, 2 * R * CHUNKS, 128), F32),
            ((3 * R, H), F32),
        ],
        [
            pltpu.VMEM((WIDTH, H), BF16),
            pltpu.VMEM((T, H), F32),
            pltpu.SemaphoreType.DMA((5,)),
        ],
        after=(hidden_parts[1], return_turn[0], return_turn[2],),
    )

    def no_adjoint():
        zero = jnp.zeros((R, H), F32)
        return (zero, zero, zero + 1.0)

    def join_adjoints(idx, ld, bit, total, other, before):
        low = (idx[1] >> bit) & 1 == 0

        def follow(near, far):
            return (near[0] + near[2] * far[0], near[1] + near[2] * far[1], near[2] * far[2])

        as_near, as_far, with_other = follow(total, other), follow(other, total), follow(before, other)
        return (
            tuple(jnp.where(low, a, b) for a, b in zip(as_near, as_far)),
            tuple(jnp.where(low, a, b) for a, b in zip(with_other, before)),
        )

    late = scan_rounds(entry, no_adjoint, join_adjoints)

    early_parts = weight_grads(
        [[grad_mid], [mixed_gate]],
        [gated, grad_gate],
        [(0, 0, 0, H, 0, 0), (1, 1, 0, H, 1, 0)],
    )
    early_state = square_start(*early_parts)

    def time_backward(
        idx, res, out, value, part_old, part_new, keep, fresh, nums, dens, fade, adjoint, late,
        ld, gate, diff, hat, edge, po, pp, p0, p1, p2, p3, p4,
        grad_key, grad_value, mine_own, s0, s1, stats, first_out, sums, sums_own,
        w, dk, dv, gk, gv, gg, starts, sems,
    ):
        copies = place_rows(idx, [p0, p1, p2, p3, p4], w, sems, 0, 3 * H)
        begin(copies)
        late_now = (late[pl.ds(0, R), :], late[pl.ds(R, R), :])
        for i in range(CHUNKS - 1, -1, -1):
            for k in range(2):
                put(starts, chunk_rows(k, i), late_now[k])
            f = get(fade, chunk_rows(0, i))
            late_now = tuple(get(adjoint, chunk_rows(k, i)) + f * late_now[k] for k in range(2))

        def step(j, carry):
            t = ST - 1 - j
            adj, fade_sum, bonus_sum = carry
            new = []
            for r in range(R):
                alpha, beta = adj[r]
                at, spread = scan_rows(r, t), step_rows(r, t)
                g, y, v = get(res, spread), get(out, spread), get(value, spread)
                b, a = fresh[at, :], keep[at, :]
                near = part_new[at, :] * g
                lift = near * (v - y)
                put(dv, spread, b * alpha + near)
                put(dk, spread, b * (v * alpha + beta) + lift)
                bonus_sum = bonus_sum + lift
                fade_sum = fade_sum - a * (nums[at, :] * alpha + dens[at, :] * beta)
                direct = part_old[at, :] * g
                new.append((direct + a * alpha, a * beta - direct * y))
            return (tuple(new), fade_sum, bonus_sum)

        first_adj = tuple(
            tuple(get(starts, pl.ds((k * R + r) * CHUNKS, CHUNKS)) for k in range(2))
            for r in range(R)
        )
        zero = jnp.zeros((CHUNKS, H), F32)
        _, fade_sum, bonus_sum = lax.fori_loop(0, ST, step, (first_adj, zero, zero))
        sums_own[0:1, :] = jnp.sum(fade_sum, axis=0, keepdims=True) * jnp.exp(ld[...])
        sums_own[1:2, :] = jnp.sum(bonus_sum, axis=0, keepdims=True)
        grad_key[...] = get(dk, EVERY).astype(BF16)
        grad_value[...] = get(dv, EVERY).astype(BF16)
        finish(copies)
        gk[...] = dot_t(grad_key[...], w[:, :H])
        gv[...] = dot_t(grad_value[...], w[:, H : 2 * H])
        gg[...] = dot_t(gate[...], w[:, 2 * H : 3 * H])
        gain = both(po, pp, 0)
        shares = [both(po, pp, i) for i in (2, 3, 4)]
        flag = jnp.where(idx[1] > 0, 1.0, 0.0).astype(F32)
        zero = jnp.zeros((1, WIDTH), F32)
        totals = (zero,) * 5
        lane = lax.broadcasted_iota(jnp.int32, (TB, 128), 1)
        for r in range(R):

            def tile(j, carry):
                after, gain_sum, bias_sum, *mix_sums = carry
                at = rows_at(r, NT - 1 - j)
                grads = (gk[at, :], gv[at, :], gg[at, :])
                d, n = diff[at, :].astype(F32), hat[at, :].astype(F32)
                now = back = None
                for share, grad in zip(shares, grads):
                    a, b = grad * share, grad * (1.0 - share)
                    now = a if now is None else now + a
                    back = b if back is None else back + b
                grad = now + shift_up(back, after)
                mine_own[at, :] = grad[:, :H]
                s0[at, :] = grad[:, H : H + SR]
                s1[at, :] = grad[:, H + SR :]
                scaled = grad * gain
                one = jnp.sum(scaled, axis=-1, keepdims=True)
                two = jnp.sum(scaled * n, axis=-1, keepdims=True)
                stats[at, :] = jnp.where(lane == 0, one, jnp.where(lane == 1, two, 0.0))
                return (
                    back[0:1, :],
                    gain_sum + jnp.sum(grad * n, axis=0, keepdims=True),
                    bias_sum + jnp.sum(grad, axis=0, keepdims=True),
                    *(
                        total + jnp.sum(one_grad * d, axis=0, keepdims=True)
                        for total, one_grad in zip(mix_sums, grads)
                    ),
                )

            front, *totals = lax.fori_loop(0, NT, tile, (zero, *totals))
            first_out[r : r + 1, :] = front
            totals[0] = totals[0] + front * edge[r : r + 1, :]
            totals[1] = totals[1] + front * flag
        for i in range(5):
            sums[i : i + 1, :] = totals[i]

    hidden_turn_out = square_turn(hold(hidden_state, late))
    hidden_cross = square_cross(*hidden_turn_out)
    grad_key, grad_value, one_own, *one_send, first_one, sums_one, sums_own = launch(
        time_backward,
        "s" + "v" * 19 + "h" * 5,
        (
            idx,
            grad_res,
            mixed_out,
            value,
            part_old,
            part_new,
            keep,
            fresh,
            nums,
            dens,
            fade,
            adjoint,
            late,
            fading,
            grad_gate,
            diff_one,
            hat_one,
            hat_edge_one,
            params,
            params_other,
            *time_pieces,
        ),
        [
            ((T, H), BF16),
            ((T, H), BF16),
            ((T, H), F32),
            ((T, SR), F32),
            ((T, SR), F32),
            ((T, 128), F32),
            ((R, WIDTH), F32),
            ((5, WIDTH), F32),
            ((2, H), F32),
        ],
        [pltpu.VMEM((WIDTH, 3 * H), BF16)]
        + [pltpu.VMEM((G, T, 128), F32)] * 2
        + [pltpu.VMEM((T, WIDTH), F32)] * 3
        + [pltpu.VMEM((G, 2 * R * CHUNKS, 128), F32), pltpu.SemaphoreType.DMA((5,))],
        after=(early_parts[1],),
    )
    one_other = [swap(part, "tp", 1) for part in one_send]
    first_one_own = along_ctx(first_one, -1, False)
    first_one_other = along_ctx(first_one, -1, True)

    sums_other = swap(jnp.concatenate([sums_one[:, H:], sums_two[:, H:]], axis=0), "tp", 1)
    late_parts = weight_grads(
        [[mixed_key], [mixed_value]],
        [grad_key, grad_value],
        [(0, 0, 0, H, 0, 0), (1, 1, 0, H, 1, 0)],
        after=(return_cross[1], return_cross[3], hidden_cross[1], hidden_cross[3],),
        riders=(sums_one, sums_two, sums_other, sums_own),
    )
    late_state = square_start(*late_parts)

    return_seen = []
    (return_w,) = scatter_line(
        *square_end(hold(return_cross, first_one_own, first_one_other)), widths=[FH], seen=return_seen
    )
    def input_backward(
        mine, sent, t0, t1, theirs, e_own, e_other, hat, root, po, pp, gm, out
    ):
        gain_full = both(po, pp, 0)
        tail = e_own[...] + swapped(e_other[...])
        row = lax.broadcasted_iota(jnp.int32, (TB, 1), 0)
        for r in range(R):
            weighted = tail[r : r + 1, :] * gain_full
            tail_one = jnp.sum(weighted, axis=-1, keepdims=True)
            tail_two = jnp.sum(
                weighted * hat[(r + 1) * L - TB : (r + 1) * L, :].astype(F32)[TB - 1 :],
                axis=-1,
                keepdims=True,
            )

            def tile(i, carry):
                at = rows_at(r, i)
                is_last = jnp.where((row == TB - 1) & (i == NT - 1), 1.0, 0.0).astype(F32)
                grad = mine[at, :] + columns((t0, t1), at) + is_last * tail[r : r + 1, :H]
                stats = sent[at, :] + theirs[at, :]
                mean_one = (stats[:, 0:1] + is_last * tail_one) * (1.0 / WIDTH)
                mean_two = (stats[:, 1:2] + is_last * tail_two) * (1.0 / WIDTH)
                scaled = grad * gain_full[:, :H]
                out[at, :] = gm[at, :] + root[at, :] * (
                    scaled - mean_one - hat[at, :H].astype(F32) * mean_two
                )
                return carry

            lax.fori_loop(0, NT, tile, 0)

    (input_grad,) = launch(
        input_backward,
        "v" * 12,
        (
            one_own,
            one_send[2],
            *one_other,
            first_one_own,
            first_one_other,
            hat_one,
            root_one,
            params,
            params_other,
            grad_mid_own,
        ),
        [((T, H), F32)],
        after=(late_parts[1],),
    )
    hidden_seen = []
    hidden_w, filter_w = scatter_line(
        *square_end(hidden_cross), widths=[FH, H], seen=hidden_seen
    )
    early_cross = square_cross(*square_turn(hold(early_state, hidden_seen[0], return_seen[-1])))
    late_cross = square_cross(*square_turn(late_state))
    early_seen = []
    output_w, gate_w = scatter_line(*square_end(hold(early_cross, late_cross[1], late_cross[3])), widths=[H, H], behind=hidden_seen[-1], seen=early_seen)
    key_w, value_w, *vectors = scatter_line(*square_end(late_cross), widths=[H, H])
    vectors = [vector.reshape(H) for vector in vectors]
    shape = block_entries.shape
    return (
        block_out.reshape(shape),
        input_grad.reshape(shape),
        vectors[0],
        vectors[1],
        vectors[2],
        vectors[3],
        vectors[4],
        vectors[9],
        vectors[10],
        gate_w,
        key_w,
        value_w,
        output_w.T,
        vectors[5],
        vectors[6],
        vectors[7],
        vectors[8],
        hidden_w,
        filter_w,
        return_w.T,
    )


def solution(mesh):
    token = P(None, "shard", "ctx", "tp")
    feature = P("tp")
    rows = P("shard", "tp")
    cols = P("tp", "shard")
    rows_out = P(("shard", "ctx"), "tp")
    cols_out = P("tp", ("shard", "ctx"))
    return jax.shard_map(
        per_device,
        mesh=mesh,
        in_specs=(
            (token, P(None, "shard"), token)
            + (feature,) * 7
            + (rows, rows, rows, cols)
            + (feature,) * 4
            + (rows, rows, cols)
        ),
        out_specs=(
            (token, token)
            + (feature,) * 7
            + (rows_out, rows_out, rows_out, cols_out)
            + (feature,) * 4
            + (rows_out, rows_out, cols_out)
        ),
        check_vma=False,
    )
```
